32 devices in a mesh: shard: 4 (over z), ctx: 4 (over y, x), tp: 2 (over core).
Axes of the slice: x: 2, y: 2, z: 4, core: 2. Of those that a mesh axis runs over, the one named last changes fastest.
Arguments:
- seq_in: bfloat16 [4, 4096, 1024], P('shard', 'ctx'), may hold values from -6 to 6
- w_zx: bfloat16 [2, 1024, 2, 2048], P(None, 'shard', None, 'tp'), may hold values from -0.1875 to 0.1875
- w_bc: bfloat16 [2, 1024, 256], P(None, 'shard'), may hold values from -0.1875 to 0.1875
- w_dt: bfloat16 [2, 1024, 32], P(None, 'shard', 'tp'), may hold values from -0.1875 to 0.1875
- w_out: bfloat16 [2, 2048, 1024], P(None, 'tp', 'shard'), may hold values from -0.125 to 0.125
- norm_gain: float32 [2, 1024], replicated, may hold values from 0.5 to 1.5
- conv_x: float32 [2, 5, 2048], P(None, None, 'tp'), may hold values from -3 to 3
- conv_bc: float32 [2, 5, 256], replicated, may hold values from -3 to 3
- head_params: float32 [2, 3, 32], P(None, None, 'tp'), may hold values from -7 to 3
- gate_gain: float32 [2, 2048], P(None, 'tp'), may hold values from 0.5 to 1.5
- segments: int32 [4, 4096], P('shard'), may hold values from 0 to 8, as said below
- pad_mask: int32 [4, 4096], P('shard'), may hold values from 0 to 1, as said below
- cotangent: bfloat16 [4, 4096, 1024], P('shard', 'ctx'), may hold values from -6 to 6
Outputs:
- output: float32 [4, 4096, 1024], P('shard', 'ctx')
- input_grad: float32 [4, 4096, 1024], P('shard', 'ctx')
- grad_zx: float32 [2, 1024, 2, 2048], P(None, ('shard', 'ctx'), None, 'tp')
- grad_bc: float32 [2, 1024, 256], P(None, ('shard', 'ctx'))
- grad_dt: float32 [2, 1024, 32], P(None, ('shard', 'ctx'), 'tp')
- grad_out: float32 [2, 2048, 1024], P(None, 'tp', ('shard', 'ctx'))
- grad_norm_gain: float32 [2, 1024], replicated
- grad_conv_x: float32 [2, 5, 2048], P(None, None, 'tp')
- grad_conv_bc: float32 [2, 5, 256], replicated
- grad_head_params: float32 [2, 3, 32], P(None, None, 'tp')
- grad_gate_gain: float32 [2, 2048], P(None, 'tp')
The draws below stay inside these ranges and needn't reach their ends.
Inputs may be any that keep to these rules, and one draw needn't show every extreme that they name: `segments`: within a sequence the numbers never fall; a sequence holds at most 8 documents, numbered below 8, and ends with one or more padding positions numbered 8. `pad_mask`: 0 exactly on the padding positions that end every sequence.
All inputs are finite; a program needn't handle non-finite values.
Results may differ from the reference program's by a relative error of at most 0.015.
Values may be sent and summed in bfloat16 or wider, within the bound.
No kernel may reach another device: no remote copies, remote signals or barrier semaphores. Data moves between devices by JAX's collectives and lax.ppermute only.
A program may use at most 768 MiB of HBM per device.

```python
import jax
import jax.numpy as jnp
from jax import lax

D = 1024
HEADS = 32
NST = 128
BLOCK = 256
LAYERS = 2
LEN = 4096
DOCS = 8
DI = 2048
SEQS = 4


def layout_draw(key):
    base = jax.random.fold_in(key, 7)
    key_one, key_two, key_three = jax.random.split(base, 3)
    first = jax.random.randint(key_one, (SEQS, DOCS - 1), 1, LEN)
    second = jax.random.randint(key_two, (SEQS, DOCS - 1), 1, LEN)
    cuts = first * second // LEN + 1
    padding = jax.random.randint(key_three, (SEQS, 1), 1, LEN // 4 + 1)
    positions = jnp.arange(LEN, dtype=jnp.int32)
    seg_ids = jnp.sum((cuts[:, :, None] <= positions[None, None, :]).astype(jnp.int32), axis=1)
    padded = positions[None, :] >= LEN - padding
    seg_ids = jnp.where(padded, DOCS, seg_ids).astype(jnp.int32)
    mask_ids = jnp.where(padded, 0, 1).astype(jnp.int32)
    return (seg_ids, mask_ids)


def draw_segments(key, part):
    return layout_draw(key)[0]


def draw_pad_mask(key, part):
    return layout_draw(key)[1]


def draw_head_params(key, part):
    key_one, key_two, key_three = jax.random.split(jax.random.fold_in(key, 11), 3)
    shape = (LAYERS, 1, HEADS)
    step_bias = jax.random.uniform(key_one, shape, jnp.float32, minval=-7.0, maxval=-2.3)
    rate_log = jax.random.uniform(key_two, shape, jnp.float32, minval=0.0, maxval=2.77)
    skip_coef = jax.random.uniform(key_three, shape, jnp.float32, minval=0.5, maxval=1.5)
    return jnp.concatenate([step_bias, rate_log, skip_coef], axis=1)


def block_levels(own_key, shape, shards, low, high):
    def one(dim, blocks):
        steps = jax.random.uniform(jax.random.fold_in(jax.random.fold_in(own_key, 6), dim), (blocks,), jnp.float32, low / len(shards), high / len(shards))
        return jnp.repeat(jnp.exp(steps), shape[dim] // blocks).reshape((-1,) + (1,) * (len(shape) - dim - 1))

    level = one(*shards[0])
    for cut in shards[1:]:
        level = level * one(*cut)
    return level


def noise(own_key, dims, deviation, bound, cuts=(), kind=jnp.bfloat16):
    factor_of = block_levels(own_key, dims, cuts, -0.22, 0.18) if cuts else 1.0
    values = jax.random.normal(own_key, dims, jnp.float32) * deviation * factor_of
    return jnp.minimum(jnp.maximum(values, -bound), bound).astype(kind)


def setup_inputs(seed: int = 0) -> dict:
    keys = jax.random.split(jax.random.key(seed), 14)
    return {
        "seq_in": noise(keys[0], (SEQS, LEN, D), 1.0, 6.0, ((0, 4), (1, 4))),
        "w_zx": noise(keys[1], (LAYERS, D, 2, DI), D ** -0.5, 0.1875, ((1, 4), (3, 2))),
        "w_bc": noise(keys[2], (LAYERS, D, 2 * NST), D ** -0.5, 0.1875, ((1, 4),)),
        "w_dt": noise(keys[3], (LAYERS, D, HEADS), D ** -0.5, 0.1875, ((1, 4), (2, 2))),
        "w_out": noise(keys[4], (LAYERS, DI, D), DI ** -0.5, 0.125, ((1, 2), (2, 4))),
        "norm_gain": jnp.clip(1.0 + 0.1 * jax.random.normal(keys[5], (LAYERS, D), jnp.float32), 0.5, 1.5),
        "conv_x": noise(keys[6], (LAYERS, 5, DI), 0.5, 3.0, ((2, 2),), jnp.float32),
        "conv_bc": noise(keys[7], (LAYERS, 5, 2 * NST), 0.5, 3.0, (), jnp.float32),
        "head_params": draw_head_params(jax.random.fold_in(keys[13], 71), 0),
        "gate_gain": jnp.clip(1.0 + 0.1 * jax.random.normal(keys[9], (LAYERS, DI), jnp.float32), 0.5, 1.5),
        "segments": draw_segments(jax.random.fold_in(keys[13], 71), 0),
        "pad_mask": draw_pad_mask(jax.random.fold_in(keys[13], 71), 0),
        "cotangent": noise(keys[12], (SEQS, LEN, D), 1.0, 6.0, ((0, 4), (1, 4))),
    }


EPSILON = 1e-05
PRECISE = lax.Precision.HIGHEST

@jax.custom_vjp
def low(v):
    return lax.optimization_barrier(v.astype(jnp.bfloat16)).astype(jnp.float32)

@jax.custom_vjp
def low_back(v):
    return v

def low_keep(v):
    return (low(v), None)

def low_pass(kept, grad):
    return (grad,)

def back_keep(v):
    return (v, None)

def back_low(kept, grad):
    return (low(grad),)
low.defvjp(low_keep, low_pass)
low_back.defvjp(back_keep, back_low)

def conv_apply(values, params, same_doc):
    length = same_doc.shape[1]
    summed = params[4]
    for shift_lag in range(4):
        summed = summed + params[shift_lag] * values[3 - shift_lag:3 - shift_lag + length] * same_doc[shift_lag][:, None]
    return jax.nn.silu(summed)

def block_step(running, pieces):
    state_now, seg_last = running
    x_part, b_part, c_part, dt_part, rate_part, seg_part = pieces
    length = seg_part.shape[0]
    cumulative = jnp.cumsum(rate_part, axis=0)
    gaps = cumulative[:, None, :] - cumulative[None, :, :]
    causal = jnp.arange(length)[:, None] >= jnp.arange(length)[None, :]
    kept_pairs = (causal & (seg_part[:, None] == seg_part[None, :]))[:, :, None]
    decays = jnp.where(kept_pairs, jnp.exp(jnp.where(kept_pairs, gaps, 0.0)), 0.0)
    intersection = jnp.dot(c_part, b_part.T, precision=PRECISE, preferred_element_type=jnp.float32)
    weighted = x_part * dt_part[:, :, None]
    result = jnp.einsum('tsh,shp->thp', decays * intersection[:, :, None], weighted, precision=PRECISE)
    carried = (seg_part == seg_last).astype(jnp.float32)[:, None] * jnp.exp(cumulative)
    result = result + carried[:, :, None] * jnp.einsum('tn,hpn->thp', c_part, state_now, precision=PRECISE)
    tail_decay = (seg_part == seg_part[length - 1]).astype(jnp.float32)[:, None] * jnp.exp(cumulative[length - 1][None, :] - cumulative)
    state_next = carried[length - 1][:, None, None] * state_now + jnp.einsum('sh,shp,sn->hpn', tail_decay, weighted, b_part, precision=PRECISE)
    return ((state_next, seg_part[length - 1]), result)

def layer_apply(params, hidden, seg_ids, mask_rows):
    w_in, w_bcl, w_dtl, w_outl, n_gain, convx, convbc, head_rows, g_gain = params
    model_width = hidden.shape[1]
    length = hidden.shape[0]
    inner_width = w_in.shape[2]
    head_count = head_rows.shape[1]
    head_width = inner_width // head_count
    state_width = w_bcl.shape[1] // 2
    norm_scale = lax.rsqrt(lax.optimization_barrier(jnp.mean(hidden * hidden, axis=-1, keepdims=True)) + EPSILON)
    lowered = low(hidden * norm_scale * n_gain)
    projected = jnp.dot(lowered, w_in.reshape(model_width, 2 * inner_width), precision=PRECISE, preferred_element_type=jnp.float32)
    gate_raw = low_back(projected[:, :inner_width])
    x_raw = low_back(low(projected[:, inner_width:]))
    bc_raw = low_back(low(jnp.dot(lowered, w_bcl, precision=PRECISE, preferred_element_type=jnp.float32)))
    dt_raw = low_back(jnp.dot(lowered, w_dtl, precision=PRECISE, preferred_element_type=jnp.float32))
    seg_ext = jnp.concatenate([jnp.full((3,), -1, jnp.int32), seg_ids])
    same_doc = jnp.stack([(seg_ext[3 - shift_lag:3 - shift_lag + length] == seg_ids).astype(jnp.float32) for shift_lag in range(4)])
    x_conv = low(conv_apply(jnp.concatenate([jnp.zeros((3, inner_width), jnp.float32), x_raw]), convx, same_doc))
    bc_conv = low(conv_apply(jnp.concatenate([jnp.zeros((3, 2 * state_width), jnp.float32), bc_raw]), convbc, same_doc))
    step_size = jax.nn.softplus(dt_raw + head_rows[0]) * mask_rows[:, None]
    rates = -jnp.exp(head_rows[1]) * step_size
    x_heads = x_conv.reshape(length, head_count, head_width)
    block_count = length // BLOCK

    def blocks(values):
        return values.reshape((block_count, BLOCK) + values.shape[1:])
    start_state = (jnp.zeros((head_count, head_width, state_width), jnp.float32), jnp.int32(-1))
    final_state, outputs = lax.scan(jax.checkpoint(block_step), start_state, (blocks(x_heads), blocks(bc_conv[:, :state_width]), blocks(bc_conv[:, state_width:]), blocks(step_size), blocks(rates), blocks(seg_ids)))
    mixed_heads = outputs.reshape(length, head_count, head_width) + head_rows[2][:, None] * x_heads
    gated_out = mixed_heads.reshape(length, inner_width) * jax.nn.silu(gate_raw)
    gate_scale = lax.rsqrt(lax.optimization_barrier(jnp.mean(gated_out * gated_out, axis=-1, keepdims=True)) + EPSILON)
    normed = low(gated_out * gate_scale * g_gain)
    branch = low_back(jnp.dot(normed, w_outl, precision=PRECISE, preferred_element_type=jnp.float32))
    return hidden + branch

def forward(weights, hidden, segments, mask_rows):
    for layer_idx in range(LAYERS):
        params = tuple((values[layer_idx] for values in weights))

        def one_sequence(item, params=params):
            return layer_apply(params, item[0], item[1], item[2])
        hidden = lax.map(jax.checkpoint(one_sequence), (hidden, segments, mask_rows))
    return hidden

def reference(seq_in, w_zx, w_bc, w_dt, w_out, norm_gain, conv_x, conv_bc, head_params, gate_gain, segments, pad_mask, cotangent):
    weights = tuple((values.astype(jnp.float32) for values in (w_zx, w_bc, w_dt, w_out, norm_gain, conv_x, conv_bc, head_params, gate_gain)))
    start_hidden = seq_in.astype(jnp.float32)
    mask_rows = pad_mask.astype(jnp.float32)

    def whole(wts, hidden):
        return forward(wts, hidden, segments, mask_rows)
    output, pullback = jax.vjp(whole, weights, start_hidden)
    weight_grads, input_grad = pullback(cotangent.astype(jnp.float32))
    return (output, input_grad, weight_grads[0], weight_grads[1], weight_grads[2], weight_grads[3], weight_grads[4], weight_grads[5], weight_grads[6], weight_grads[7], weight_grads[8])
```

```python
import functools

import jax
import jax.numpy as jnp
from jax import lax
from jax.experimental import pallas as pl
from jax.experimental.pallas import tpu as pltpu
from jax.sharding import PartitionSpec as P

EPSILON = 1e-05
EXACT = lax.Precision.HIGHEST
F32 = jnp.float32
BF16 = jnp.bfloat16
CHUNK = 128
LANES = 128
EDGE = 8
CLOSED = -1e30
VMEM = 48 << 20


def dot(a, b, dims=((1,), (0,)), precision=None):
    return lax.dot_general(a, b, (dims, ((), ())), precision=precision, preferred_element_type=F32)


def split(values):
    high = values.astype(BF16)
    return high, (values - high.astype(F32)).astype(BF16)


def expand(values, spread):
    high, rest = split(values)
    return dot(high, spread) + dot(rest, spread)


def head_sum(values, spread):
    high, rest = split(values)
    return dot(high, spread, ((1,), (1,))) + dot(rest, spread, ((1,), (1,)))


def conv_shifts(ext, same):
    return [ext[EDGE:]] + [pltpu.roll(ext, lag, 0)[EDGE:] * same[lag] for lag in (1, 2, 3)]


def conv_sum(shifts, taps):
    total = taps[4:5] + taps[0:1] * shifts[0]
    for lag in (1, 2, 3):
        total = total + taps[lag : lag + 1] * shifts[lag]
    return total


def same_columns(cols, width):
    return [None] + [jnp.broadcast_to(cols[:, lag - 1 : lag], (cols.shape[0], width)) for lag in (1, 2, 3)]


def pair_masked(values):
    lane = lax.broadcasted_iota(jnp.int32, values.shape, 1)
    zero = jnp.zeros_like(values)
    first = lane < LANES // 2
    return jnp.concatenate([jnp.where(first, values, zero), jnp.where(first, zero, values)], axis=0)


def pairs_bias(seg_col, seg_row, later_rows):
    size = seg_col.shape[0]
    row = lax.broadcasted_iota(jnp.int32, (size, size), 0)
    col = lax.broadcasted_iota(jnp.int32, (size, size), 1)
    ordered = (row >= col) if later_rows else (row <= col)
    return jnp.where(ordered & (seg_col == seg_row), 0.0, CLOSED)


def silu_parts(values):
    sig = jax.nn.sigmoid(values)
    return sig, values * sig


def call(body, grid, ins, outs, scratch=(), scalars=None, flops=0, name=None):
    count = 0 if scalars is None else 1

    def adapt(block, fn):
        if block is None:
            return pl.BlockSpec(memory_space=pl.ANY)
        return pl.BlockSpec(block, fn)

    in_specs = [adapt(block, fn) for _, block, fn in ins]
    out_specs = [adapt(block, fn) for _, _, block, fn in outs]
    shapes = [jax.ShapeDtypeStruct(shape, dtype) for shape, dtype, _, _ in outs]
    moved = sum(a.size * a.dtype.itemsize for a, _, _ in ins) + sum(
        s.size * s.dtype.itemsize for s in shapes
    )
    made = pl.pallas_call(
        body,
        out_shape=shapes,
        grid_spec=pltpu.PrefetchScalarGridSpec(
            num_scalar_prefetch=count,
            grid=grid,
            in_specs=in_specs,
            out_specs=out_specs,
            scratch_shapes=list(scratch),
        ),
        compiler_params=pltpu.CompilerParams(
            vmem_limit_bytes=VMEM, dimension_semantics=("arbitrary",) * len(grid)
        ),
        cost_estimate=pl.CostEstimate(flops=int(flops), bytes_accessed=int(moved), transcendentals=0),
        name=name,
    )
    arrays = [a for a, _, _ in ins]
    return made(*(([scalars] if count else []) + arrays))


def rows_at(i, *_):
    return (i, 0)


def fixed(*_):
    return (0, 0)


def enter_body(first, inner_total, *refs):
    if first:
        h_ref, gain, w_main, w_other, u_ref, x_ref, mine_ref, other_ref, dt_ref = refs
        hidden = h_ref[...].astype(F32)
    else:
        (h_ref, p_ref, q_ref, s_ref, t_ref, gain, w_main, w_other) = refs[:8]
        (h_out, u_ref, x_ref, mine_ref, other_ref, dt_ref) = refs[8:]
        scale = lax.rsqrt((s_ref[...] + t_ref[...])[:, :1] / inner_total + EPSILON)
        hidden = h_ref[...].astype(F32) + scale * (p_ref[...].astype(F32) + q_ref[...].astype(F32))
        h_out[...] = hidden
    norm = lax.rsqrt(jnp.mean(hidden * hidden, axis=1, keepdims=True) + EPSILON)
    lowered = (hidden * norm * gain[0:1]).astype(BF16)
    u_ref[...] = lowered
    width = x_ref.shape[1]
    state = mine_ref.shape[1]
    made = dot(lowered, w_main[...])
    x_ref[...] = made[:, :width].astype(BF16)
    mine_ref[...] = made[:, width : width + state].astype(BF16)
    dt_ref[...] = made[:, width + state :]
    other_ref[...] = dot(lowered, w_other[...]).astype(BF16)


def enter(hidden, parts, gain, w_main, w_other, width, inner_total):
    rows, model = hidden.shape
    state = w_other.shape[1]
    block = min(256, rows)
    wide = (block, model)
    ins = [(hidden, wide, rows_at)]
    outs = []
    if parts is not None:
        ins += [(parts[0], wide, rows_at), (parts[1], wide, rows_at)]
        ins += [(parts[2], (block, LANES), rows_at), (parts[3], (block, LANES), rows_at)]
        outs.append(((rows, model), F32, wide, rows_at))
    ins += [
        (gain, gain.shape, fixed),
        (w_main, w_main.shape, fixed),
        (w_other, w_other.shape, fixed),
    ]
    outs += [
        ((rows, model), BF16, wide, rows_at),
        ((rows, width), BF16, (block, width), rows_at),
        ((rows, state), BF16, (block, state), rows_at),
        ((rows, state), BF16, (block, state), rows_at),
        ((rows, LANES), F32, (block, LANES), rows_at),
    ]
    flops = 2 * rows * model * (w_main.shape[1] + state)
    made = call(
        functools.partial(enter_body, parts is None, inner_total), (rows // block,), ins, outs, flops=flops, name="enter"
    )
    return made if parts is not None else [hidden] + list(made)


def states_body(
    flag, x_ref, mine_ref, other_ref, dt_ref, edge_ref, cols_ref, taps_ref, taps_bc_ref, head_ref,
    spread_ref, lower_ref, xc_ref, bc_ref, step_ref, cum_ref, enter_ref, phi_ref, last_ref,
    tail_x, tail_bc, state, phi,
):
    chunk = pl.program_id(0)
    width = x_ref.shape[1]
    ns = mine_ref.shape[1]

    @pl.when(chunk == 0)
    def _():
        tail_x[...] = edge_ref[:, :width].astype(F32)
        tail_bc[...] = edge_ref[:, width:].astype(F32)
        state[...] = jnp.zeros_like(state)
        phi[...] = jnp.ones_like(phi)

    cols = cols_ref[...]
    same = same_columns(cols, LANES)
    dt = jax.nn.softplus(dt_ref[...] + head_ref[0:1]) * cols[:, 3:4]
    rates = head_ref[1:2] * dt
    cum = dot(lower_ref[...], rates, precision=EXACT)
    step_ref[...] = dt
    cum_ref[...] = cum
    size = cum.shape[0]
    tail_dt = cols[:, 5:6] * jnp.exp(cum[size - 1 : size] - cum) * dt
    tail_wide = expand(tail_dt, spread_ref[...])
    fold = cols[size - 1 : size, 4:5] * jnp.exp(cum[size - EDGE : size])[EDGE - 1 : EDGE]
    fold_rows = jnp.broadcast_to(fold, phi.shape)
    fold_wide = expand(fold_rows, spread_ref[...])[0:1]

    halves = []
    for i, source in enumerate((mine_ref, other_ref)):
        part = slice(i * ns, (i + 1) * ns)
        now = source[...].astype(F32)
        shifts = conv_shifts(jnp.concatenate([tail_bc[:, part], now], axis=0), same)
        tail_bc[:, part] = now[size - EDGE :]
        halves.append(silu_parts(conv_sum(shifts, taps_bc_ref[:, part]))[1].astype(BF16))
    swap = flag[0] != 0
    b_part = jnp.where(swap, halves[1].astype(F32), halves[0].astype(F32)).astype(BF16)
    c_part = jnp.where(swap, halves[0].astype(F32), halves[1].astype(F32)).astype(BF16)
    bc_ref[:, :ns] = b_part
    bc_ref[:, ns:] = c_part
    b_turned = b_part.astype(F32).T.astype(BF16)

    enter_ref[0] = state[...].astype(BF16)
    phi_ref[0] = phi[...]
    for i in range(width // LANES):
        part = slice(i * LANES, (i + 1) * LANES)
        now = x_ref[:, part].astype(F32)
        shifts = conv_shifts(jnp.concatenate([tail_x[:, part], now], axis=0), same)
        tail_x[:, part] = now[size - EDGE :]
        x_conv = silu_parts(conv_sum(shifts, taps_ref[:, part]))[1].astype(BF16)
        xc_ref[:, part] = x_conv
        held = (x_conv.astype(F32) * tail_wide[:, part]).astype(BF16)
        state[:, part] = fold_wide[:, part] * state[:, part] + dot(b_turned, held)
    phi[...] = phi[...] * fold_rows

    @pl.when(chunk == pl.num_programs(0) - 1)
    def _():
        last_ref[:ns] = state[...].astype(BF16)
        last_ref[ns:] = expand(phi[...], spread_ref[...]).astype(BF16)


def states(flag, x_raw, mine, other, dt_raw, edge, cols, taps, taps_bc, head, spread, lower):
    rows, width = x_raw.shape
    ns = mine.shape[1]
    count = rows // CHUNK
    ins = [
        (x_raw, (CHUNK, width), rows_at),
        (mine, (CHUNK, ns), rows_at),
        (other, (CHUNK, ns), rows_at),
        (dt_raw, (CHUNK, LANES), rows_at),
        (edge, edge.shape, fixed),
        (cols, (CHUNK, cols.shape[1]), rows_at),
        (taps, taps.shape, fixed),
        (taps_bc, taps_bc.shape, fixed),
        (head, head.shape, fixed),
        (spread, spread.shape, fixed),
        (lower, lower.shape, fixed),
    ]
    outs = [
        ((rows, width), BF16, (CHUNK, width), rows_at),
        ((rows, 2 * ns), BF16, (CHUNK, 2 * ns), rows_at),
        ((rows, LANES), F32, (CHUNK, LANES), rows_at),
        ((rows, LANES), F32, (CHUNK, LANES), rows_at),
        ((count, ns, width), BF16, (1, ns, width), lambda i, *_: (i, 0, 0)),
        ((count, EDGE, LANES), F32, (1, EDGE, LANES), lambda i, *_: (i, 0, 0)),
        ((ns + EDGE, width), BF16, (ns + EDGE, width), fixed),
    ]
    scratch = [
        pltpu.VMEM((EDGE, width), F32),
        pltpu.VMEM((EDGE, 2 * ns), F32),
        pltpu.VMEM((ns, width), F32),
        pltpu.VMEM((EDGE, LANES), F32),
    ]
    return call(states_body, (count,), ins, outs, scratch, flag, flops=2 * rows * width * ns * 4, name="states")


def within_body(xc_ref, bc_ref, step_ref, cum_ref, cols_ref, segs_ref, spread_ref, y_ref):
    ns = bc_ref.shape[1] // 2
    width = xc_ref.shape[1]
    cum = cum_ref[...]
    cum_rows = cum.T
    bias = pairs_bias(cols_ref[:, 7:8], segs_ref[0:1], True)
    both = dot(bc_ref[:, ns:], bc_ref[:, :ns], ((1,), (1,)))
    step_wide = expand(step_ref[...], spread_ref[...])
    for pair in range(width // LANES):
        part = slice(pair * LANES, (pair + 1) * LANES)
        weighted = (xc_ref[:, part].astype(F32) * step_wide[:, part]).astype(BF16)
        maps = []
        for head in (2 * pair, 2 * pair + 1):
            gap = (cum[:, head : head + 1] - cum_rows[head : head + 1]) + bias
            maps.append((jnp.exp(gap) * both).astype(BF16))
        y_ref[:, part] = dot(jnp.concatenate(maps, axis=1), pair_masked(weighted))


def within(xc, bc, step, cum, cols, segs, spread):
    rows, width = xc.shape
    ins = [
        (xc, (CHUNK, width), rows_at),
        (bc, (CHUNK, bc.shape[1]), rows_at),
        (step, (CHUNK, LANES), rows_at),
        (cum, (CHUNK, LANES), rows_at),
        (cols, (CHUNK, cols.shape[1]), rows_at),
        (segs, (EDGE, CHUNK), lambda i, *_: (0, i)),
        (spread, spread.shape, fixed),
    ]
    outs = [((rows, width), F32, (CHUNK, width), rows_at)]
    return call(within_body, (rows // CHUNK,), ins, outs, flops=2 * rows * CHUNK * width * 4, name="within")[0]


def leave_body(
    y_ref, xc_ref, bc_ref, cum_ref, cols_ref, enter_ref, phi_ref, in_ref, gate_ref, rows_ref, spread_ref, w_ref,
    ssm_ref, p_ref, sq_ref, normed,
):
    ns = in_ref.shape[0]
    width = xc_ref.shape[1]
    spread = spread_ref[...]
    for sub in range(y_ref.shape[0] // CHUNK):
        here = slice(sub * CHUNK, (sub + 1) * CHUNK)
        phi_wide = expand(phi_ref[sub], spread)[0:1]
        begun = (enter_ref[sub].astype(F32) + phi_wide * in_ref[...]).astype(BF16)
        carried = cols_ref[here, 4:5] * jnp.exp(cum_ref[here])
        carried_wide = expand(carried, spread)
        far = dot(bc_ref[here, ns:], begun)
        ssm_ref[here] = y_ref[here] + carried_wide * far
    total = jnp.zeros((y_ref.shape[0], LANES), F32)
    for i in range(width // LANES):
        part = slice(i * LANES, (i + 1) * LANES)
        mixed = ssm_ref[:, part] + rows_ref[1:2, part] * xc_ref[:, part].astype(F32)
        gated = mixed * silu_parts(gate_ref[:, part])[1]
        total = total + gated * gated
        normed[:, part] = (gated * rows_ref[0:1, part]).astype(BF16)
    sq_ref[...] = jnp.broadcast_to(jnp.sum(total, axis=1, keepdims=True), total.shape)
    p_ref[...] = dot(normed[...], w_ref[...]).astype(BF16)


def leave(y_in, xc, bc, cum, cols, entered, phi, state_in, gate, rowpack, spread, w_out):
    rows, width = xc.shape
    model = w_out.shape[1]
    ns = state_in.shape[0]
    block = min(256, rows)
    subs = block // CHUNK
    ins = [
        (y_in, (block, width), rows_at),
        (xc, (block, width), rows_at),
        (bc, (block, bc.shape[1]), rows_at),
        (cum, (block, LANES), rows_at),
        (cols, (block, cols.shape[1]), rows_at),
        (entered, (subs, ns, width), lambda i, *_: (i, 0, 0)),
        (phi, (subs, EDGE, LANES), lambda i, *_: (i, 0, 0)),
        (state_in, state_in.shape, fixed),
        (gate, (block, width), rows_at),
        (rowpack, rowpack.shape, fixed),
        (spread, spread.shape, fixed),
        (w_out, w_out.shape, fixed),
    ]
    outs = [
        ((rows, width), F32, (block, width), rows_at),
        ((rows, model), BF16, (block, model), rows_at),
        ((rows, LANES), F32, (block, LANES), rows_at),
    ]
    scratch = [pltpu.VMEM((block, width), BF16)]
    return call(leave_body, (rows // block,), ins, outs, scratch, flops=2 * rows * width * model * 1.3, name="leave")


def back_gate_body(
    inner_total, up_ref, p_ref, q_ref, s_ref, t_ref, ssm_ref, xc_ref, gate_ref, bc_ref, cum_ref, cols_ref, phi_ref,
    factor_ref, rows_ref, spread_ref, w_ref,
    do_ref, dy_ref, dgate_ref, n_ref, gain_ref, out_ref, state,
):
    step = pl.program_id(0)
    ns = state.shape[0]
    width = xc_ref.shape[1]
    spread = spread_ref[...]

    @pl.when(step == 0)
    def _():
        gain_ref[...] = jnp.zeros_like(gain_ref)
        state[...] = jnp.zeros_like(state)

    scale = lax.rsqrt((s_ref[...] + t_ref[...])[:, :1] / inner_total + EPSILON)
    up = up_ref[...].astype(BF16)
    do_ref[...] = up
    summed = p_ref[...].astype(F32) + q_ref[...].astype(F32)
    spread_sum = jnp.sum(up.astype(F32) * summed, axis=1, keepdims=True)
    pull = scale * scale * scale * spread_sum / inner_total
    scale_wide = jnp.broadcast_to(scale, (scale.shape[0], LANES))
    pull_wide = jnp.broadcast_to(pull, scale_wide.shape)
    back = dot(up, w_ref[...], ((1,), (1,)))
    for i in range(width // LANES):
        part = slice(i * LANES, (i + 1) * LANES)
        gain = rows_ref[0:1, part]
        gate = gate_ref[:, part]
        sig, soft = silu_parts(gate)
        mixed = ssm_ref[:, part] + rows_ref[1:2, part] * xc_ref[:, part].astype(F32)
        gated = mixed * soft
        scaled = gated * scale_wide
        grad = back[:, part]
        gain_ref[0:1, part] += jnp.sum(grad * scaled, axis=0, keepdims=True)
        grad_gated = grad * gain * scale_wide - gated * pull_wide
        dy_ref[:, part] = (grad_gated * soft).astype(BF16)
        dgate_ref[:, part] = (grad_gated * mixed * (sig * (1.0 + gate * (1.0 - sig)))).astype(BF16)
        n_ref[:, part] = (scaled * gain).astype(BF16)
    for sub in range(up_ref.shape[0] // CHUNK):
        here = slice(sub * CHUNK, (sub + 1) * CHUNK)
        phi_wide = expand(phi_ref[sub], spread)[0:1]
        carried_wide = expand(cols_ref[here, 4:5] * jnp.exp(cum_ref[here]), spread)
        c_turned = bc_ref[here, ns:].astype(F32).T.astype(BF16)
        carried_dy = (dy_ref[here].astype(F32) * carried_wide).astype(BF16)
        state[...] += phi_wide * dot(c_turned, carried_dy)

    @pl.when(step == pl.num_programs(0) - 1)
    def _():
        out_ref[:ns] = state[...].astype(BF16)
        out_ref[ns:] = factor_ref[...]


def back_gate(up, parts, ssm, xc, gate, bc, cum, cols, phi, ended, rowpack, spread, w_out, inner_total):
    rows, width = xc.shape
    model = w_out.shape[1]
    ns = bc.shape[1] // 2
    block = min(256, rows)
    subs = block // CHUNK
    wide = (block, model)
    ins = [
        (up, wide, rows_at),
        (parts[0], wide, rows_at),
        (parts[1], wide, rows_at),
        (parts[2], (block, LANES), rows_at),
        (parts[3], (block, LANES), rows_at),
        (ssm, (block, width), rows_at),
        (xc, (block, width), rows_at),
        (gate, (block, width), rows_at),
        (bc, (block, 2 * ns), rows_at),
        (cum, (block, LANES), rows_at),
        (cols, (block, cols.shape[1]), rows_at),
        (phi, (subs, EDGE, LANES), lambda i, *_: (i, 0, 0)),
        (ended, (EDGE, width), lambda i, *_: (ns // EDGE, 0)),
        (rowpack, rowpack.shape, fixed),
        (spread, spread.shape, fixed),
        (w_out, w_out.shape, fixed),
    ]
    outs = [
        ((rows, model), BF16, wide, rows_at),
        ((rows, width), BF16, (block, width), rows_at),
        ((rows, width), BF16, (block, width), rows_at),
        ((rows, width), BF16, (block, width), rows_at),
        ((EDGE, width), F32, (EDGE, width), fixed),
        ((ns + EDGE, width), BF16, (ns + EDGE, width), fixed),
    ]
    scratch = [pltpu.VMEM((ns, width), F32)]
    return call(
        functools.partial(back_gate_body, inner_total), (rows // block,), ins, outs, scratch,
        flops=2 * rows * width * model * 1.3, name="back_gate",
    )


def back_within_body(
    xc_ref, bc_ref, step_ref, cum_ref, cols_ref, segs_ref, spread_ref, dy_ref, dx_ref, left_ref, dbc_ref
):
    ns = bc_ref.shape[1] // 2
    width = xc_ref.shape[1]
    size = xc_ref.shape[0]
    spread = spread_ref[...]
    cum = cum_ref[...]
    cum_rows = cum.T
    bias = pairs_bias(cols_ref[:, 7:8], segs_ref[0:1], False)
    b_part = bc_ref[:, :ns]
    c_part = bc_ref[:, ns:]
    both = dot(b_part, c_part, ((1,), (1,)))
    step_wide = expand(step_ref[...], spread)
    grad_both = jnp.zeros((size, size), F32)
    left = jnp.zeros((size, LANES), F32)
    for pair in range(width // LANES):
        part = slice(pair * LANES, (pair + 1) * LANES)
        weighted = (xc_ref[:, part].astype(F32) * step_wide[:, part]).astype(BF16)
        dy_pair = pair_masked(dy_ref[:, part])
        grad_maps = dot(weighted, dy_pair, ((1,), (1,)))
        maps = []
        for k in (0, 1):
            head = 2 * pair + k
            decay = jnp.exp((cum_rows[head : head + 1] - cum[:, head : head + 1]) + bias)
            maps.append((decay * both).astype(BF16))
            grad_both = grad_both + decay * grad_maps[:, k * size : (k + 1) * size]
        grad_x = dot(jnp.concatenate(maps, axis=1), dy_pair)
        dx_ref[:, part] = grad_x.astype(BF16)
        left = left + head_sum(weighted.astype(F32) * grad_x, spread[:, part])
    left_ref[...] = left
    grad_low = grad_both.astype(BF16)
    dbc_ref[:, :ns] = dot(grad_low, c_part)
    dbc_ref[:, ns:] = dot(grad_both.T.astype(BF16), b_part)


def back_within(xc, bc, step, cum, cols, segs, spread, dy):
    rows, width = xc.shape
    ins = [
        (xc, (CHUNK, width), rows_at),
        (bc, (CHUNK, bc.shape[1]), rows_at),
        (step, (CHUNK, LANES), rows_at),
        (cum, (CHUNK, LANES), rows_at),
        (cols, (CHUNK, cols.shape[1]), rows_at),
        (segs, (EDGE, CHUNK), lambda i, *_: (0, i)),
        (spread, spread.shape, fixed),
        (dy, (CHUNK, width), rows_at),
    ]
    outs = [
        ((rows, width), BF16, (CHUNK, width), rows_at),
        ((rows, LANES), F32, (CHUNK, LANES), rows_at),
        ((rows, bc.shape[1]), F32, (CHUNK, bc.shape[1]), rows_at),
    ]
    return call(back_within_body, (rows // CHUNK,), ins, outs, flops=2 * rows * CHUNK * width * 8, name="back_within")


def conv_back(ext, same, taps, grad_conv, next_rows):
    size = ext.shape[0] - EDGE
    shifts = conv_shifts(ext, same)
    pre = conv_sum(shifts, taps)
    sig = jax.nn.sigmoid(pre)
    grad_pre = grad_conv * (sig * (1.0 + pre * (1.0 - sig)))
    sums = [jnp.sum(grad_pre * shifts[lag], axis=0, keepdims=True) for lag in range(4)]
    sums.append(jnp.sum(grad_pre, axis=0, keepdims=True))
    zero = jnp.zeros((EDGE, ext.shape[1]), F32)
    length = size + 2 * EDGE
    raw = taps[0:1] * jnp.concatenate([zero, grad_pre], axis=0)
    firsts = []
    for lag in (1, 2, 3):
        term = grad_pre * same[lag] * taps[lag : lag + 1]
        firsts.append(term[:EDGE])
        padded = jnp.concatenate([zero, term, next_rows[lag - 1]], axis=0)
        raw = raw + pltpu.roll(padded, length - lag, 0)[: size + EDGE]
    return raw, firsts, sums


def back_inter_body(
    x_ref, before_ref, edge_ref, xc_ref, bc_ref, step_ref, cum_ref, cols_ref, dt_ref, dy_ref, ssm_ref, dxi_ref,
    left_ref, dbci_ref, enter_ref, phi_ref, in_ref, later_ref, taps_ref, head_ref, rows_ref, spread_ref, sums_ref,
    dx_ref, last_ref, prior_ref, dbc_ref, ddt_ref, conv_ref, heads_ref, skip_ref,
    grad_state, next_rows,
):
    step = pl.program_id(0)
    count = pl.num_programs(0)
    chunk = count - 1 - step
    ns = in_ref.shape[0]
    size, width = xc_ref.shape
    spread = spread_ref[...]

    @pl.when(step == 0)
    def _():
        grad_state[...] = later_ref[...]
        next_rows[...] = jnp.zeros_like(next_rows)
        conv_ref[...] = jnp.zeros_like(conv_ref)
        heads_ref[...] = jnp.zeros_like(heads_ref)
        skip_ref[...] = jnp.zeros_like(skip_ref)

    cols = cols_ref[...]
    same = same_columns(cols, LANES)
    cum = cum_ref[...]
    dt = step_ref[...]
    decay_in = cols[:, 4:5] * jnp.exp(cum)
    decay_out = cols[:, 5:6] * jnp.exp(cum[size - 1 : size] - cum)
    fold_rows = jnp.broadcast_to(decay_in[size - EDGE : size][EDGE - 1 : EDGE], (EDGE, LANES))
    b_part = bc_ref[:, :ns]
    c_part = bc_ref[:, ns:]
    c_turned = c_part.astype(F32).T.astype(BF16)
    dbc_b = dbci_ref[:, :ns]
    dbc_c = dbci_ref[:, ns:]
    right = jnp.zeros((size, LANES), F32)
    outward = jnp.zeros((size, LANES), F32)
    direct = jnp.zeros((size, LANES), F32)
    through = jnp.zeros((EDGE, LANES), F32)
    in_split = split(decay_in)
    out_split = split(decay_out)
    dt_split = split(dt)
    fold_split = split(fold_rows)
    phi_split = split(phi_ref[0])
    first_chunk = chunk == 0
    for i in range(width // LANES):
        part = slice(i * LANES, (i + 1) * LANES)
        across = spread[:, part]

        def over(pieces, across=across):
            return dot(pieces[0], across) + dot(pieces[1], across)

        in_wide, out_wide, dt_wide = over(in_split), over(out_split), over(dt_split)
        fold_wide, phi_wide = over(fold_split)[0:1], over(phi_split)[0:1]
        begun = enter_ref[0, :, part].astype(F32) + phi_wide * in_ref[:, part]
        grad_end = grad_state[:, part]
        x_conv = xc_ref[:, part].astype(F32)
        dy = dy_ref[:, part].astype(F32)
        weighted = x_conv * dt_wide
        carried_dy = (dy * in_wide).astype(BF16)
        held = (weighted * out_wide).astype(BF16)
        end_low = grad_end.astype(BF16)
        dbc_c = dbc_c + dot(carried_dy, begun.astype(BF16), ((1,), (1,)))
        dbc_b = dbc_b + dot(held, end_low, ((1,), (1,)))
        grad_far = out_wide * dot(b_part, end_low)
        grad_weighted = dxi_ref[:, part].astype(F32) + grad_far
        right = right + head_sum(dy * ssm_ref[:, part], across)
        outward = outward + head_sum(weighted * grad_far, across)
        direct = direct + head_sum(x_conv * grad_weighted, across)
        pass_sum = jnp.sum(begun * grad_end, axis=0, keepdims=True) * fold_wide
        through = through + head_sum(jnp.broadcast_to(pass_sum, (EDGE, LANES)), across)
        skip_ref[0:1, part] += jnp.sum(dy * x_conv, axis=0, keepdims=True)
        grad_state[:, part] = fold_wide * grad_end + dot(c_turned, carried_dy)
        grad_conv = dt_wide * grad_weighted + rows_ref[1:2, part] * dy

        ahead = jnp.where(first_chunk, edge_ref[:, part].astype(F32), before_ref[:, part].astype(F32))
        ext = jnp.concatenate([ahead, x_ref[:, part].astype(F32)], axis=0)
        raw, firsts, sums = conv_back(
            ext, same, taps_ref[:, part], grad_conv, [next_rows[k, :, part] for k in range(3)]
        )
        for k in range(3):
            next_rows[k, :, part] = firsts[k]
        for k in range(5):
            conv_ref[k : k + 1, part] += sums[k]
        dx_ref[:, part] = raw[EDGE:].astype(BF16)
        prior_ref[:, part] = raw[:EDGE]

        @pl.when(step == 0)
        def _(raw=raw, part=part):
            last_ref[:, part] = raw[size:]

    dbc_ref[:, :ns] = dbc_b.astype(BF16)
    dbc_ref[:, ns:] = dbc_c.astype(BF16)
    stacked = jnp.concatenate([right - left_ref[...], outward], axis=0)
    grad_rate = dot(sums_ref[...], stacked, precision=EXACT) + through[0:1]
    grad_dt = direct + head_ref[1:2] * grad_rate
    grad_raw = grad_dt * cols[:, 3:4] * jax.nn.sigmoid(dt_ref[...] + head_ref[0:1])
    ddt_ref[...] = grad_raw.astype(BF16)
    heads_ref[0:1] += jnp.sum(grad_raw, axis=0, keepdims=True)
    heads_ref[1:2] += jnp.sum(grad_rate * head_ref[1:2] * dt, axis=0, keepdims=True)


def back_inter(
    x_raw, edge_x, xc, bc, step, cum, cols, dt_raw, dy, ssm, dx_in, left, dbc_in, entered, phi, state_in, later,
    taps, head, rowpack, spread, sums,
):
    rows, width = xc.shape
    ns = bc.shape[1] // 2
    count = rows // CHUNK

    def back(i, *_):
        return (count - 1 - i, 0)

    def back3(i, *_):
        return (count - 1 - i, 0, 0)

    def before(i, *_):
        return (jnp.maximum((count - 1 - i) * (CHUNK // EDGE) - 1, 0), 0)

    def at(width_now):
        return (CHUNK, width_now)

    ins = [
        (x_raw, at(width), back),
        (x_raw, (EDGE, width), before),
        (edge_x, edge_x.shape, fixed),
        (xc, at(width), back),
        (bc, at(2 * ns), back),
        (step, at(LANES), back),
        (cum, at(LANES), back),
        (cols, at(cols.shape[1]), back),
        (dt_raw, at(LANES), back),
        (dy, at(width), back),
        (ssm, at(width), back),
        (dx_in, at(width), back),
        (left, at(LANES), back),
        (dbc_in, at(2 * ns), back),
        (entered, (1, ns, width), back3),
        (phi, (1, EDGE, LANES), back3),
        (state_in, state_in.shape, fixed),
        (later, later.shape, fixed),
        (taps, taps.shape, fixed),
        (head, head.shape, fixed),
        (rowpack, rowpack.shape, fixed),
        (spread, spread.shape, fixed),
        (sums, sums.shape, fixed),
    ]
    outs = [
        ((rows, width), BF16, at(width), back),
        ((EDGE, width), F32, (EDGE, width), fixed),
        ((EDGE, width), F32, (EDGE, width), fixed),
        ((rows, 2 * ns), BF16, at(2 * ns), back),
        ((rows, LANES), BF16, at(LANES), back),
        ((EDGE, width), F32, (EDGE, width), fixed),
        ((EDGE, LANES), F32, (EDGE, LANES), fixed),
        ((EDGE, width), F32, (EDGE, width), fixed),
    ]
    scratch = [pltpu.VMEM((ns, width), F32), pltpu.VMEM((3, EDGE, width), F32)]
    return call(back_inter_body, (count,), ins, outs, scratch, flops=2 * rows * width * ns * 16, name="back_inter")


def back_bc_body(raw_ref, edge_ref, cols_ref, taps_ref, mine_ref, theirs_ref, out_ref, last_ref, prior_ref, sums_ref):
    size, width = raw_ref.shape
    same = same_columns(cols_ref[...], width)
    ext = jnp.concatenate([edge_ref[...].astype(F32), raw_ref[...].astype(F32)], axis=0)
    grad = mine_ref[...].astype(F32) + theirs_ref[...].astype(F32)
    zero = jnp.zeros((EDGE, width), F32)
    raw, _, sums = conv_back(ext, same, taps_ref[...], grad, [zero] * 3)
    out_ref[...] = raw[EDGE:].astype(BF16)
    last_ref[...] = raw[size:]
    prior_ref[...] = raw[:EDGE]
    sums_ref[...] = jnp.concatenate(sums + [zero[:3]], axis=0)


def back_bc(raw, edge, cols, taps, mine, theirs):
    rows, width = raw.shape
    ins = [(a, a.shape, fixed) for a in (raw, edge, cols, taps, mine, theirs)]
    outs = [((rows, width), BF16, (rows, width), fixed)]
    outs += [((EDGE, width), F32, (EDGE, width), fixed)] * 3
    return call(back_bc_body, (1,), ins, outs, name="back_bc")


def back_norm_body(up_ref, a_ref, b_ref, h_ref, gain_ref, out_ref, sum_ref):
    @pl.when(pl.program_id(0) == 0)
    def _():
        sum_ref[...] = jnp.zeros_like(sum_ref)

    hidden = h_ref[...].astype(F32)
    grad = a_ref[...].astype(F32) + b_ref[...].astype(F32)
    model = hidden.shape[1]
    norm = lax.rsqrt(jnp.mean(hidden * hidden, axis=1, keepdims=True) + EPSILON)
    normed = hidden * norm
    sum_ref[0:1] += jnp.sum(grad * normed, axis=0, keepdims=True)
    gained = grad * gain_ref[0:1]
    inner = jnp.sum(gained * normed, axis=1, keepdims=True) / model
    out_ref[...] = up_ref[...].astype(F32) + norm * (gained - normed * inner)


def back_norm(up, a, b, hidden, gain):
    rows, model = hidden.shape
    block = min(256, rows)
    wide = (block, model)
    ins = [(v, wide, rows_at) for v in (up, a, b, hidden)] + [(gain, gain.shape, fixed)]
    outs = [((rows, model), F32, wide, rows_at), ((EDGE, model), F32, (EDGE, model), fixed)]
    return call(back_norm_body, (rows // block,), ins, outs, name="back_norm")


def weight_grad_body(places, count, shards, where, a_ref, b_ref, *refs):
    outs, (turned, result) = refs[:places], refs[places:]
    model = a_ref.shape[1]
    rows = model // (places * shards)

    @pl.when(pl.program_id(0) == 0)
    def _():
        for i in range(0, model, 256):
            turned[i : i + 256] = a_ref[:, i : i + 256].T

    result[...] = dot(turned[...], b_ref[...])
    for k in range(places):
        for z in range(shards):
            start = pl.multiple_of((z * places + where[k]) * rows, rows)
            outs[k][z * rows : (z + 1) * rows] = result[pl.ds(start, rows)].astype(BF16)


def weight_grad(where, places, shards, a, b):
    rows, model = a.shape
    width = b.shape[1]
    tile = min(256, width)
    ins = [(a, a.shape, fixed), (b, (rows, tile), lambda i, *_: (0, i))]
    part = model // places
    outs = [((part, width), BF16, (part, tile), lambda i, *_: (0, i))] * places
    scratch = [pltpu.VMEM((model, rows), BF16), pltpu.VMEM((model, tile), F32)]
    return call(
        functools.partial(weight_grad_body, places, None, shards), (width // tile,), ins, outs, scratch, where,
        flops=2 * rows * model * width, name="weight_grad",
    )


def relative(value, axis, by):
    size = lax.axis_size(axis)
    return lax.ppermute(value, axis, [(i, i ^ by) for i in range(size)])


def shifted(value, axis, by):
    size = lax.axis_size(axis)
    return lax.ppermute(value, axis, [(i, i + by) for i in range(size) if 0 <= i + by < size])


def tree_sum(values):
    while len(values) > 1:
        values = [a + b for a, b in zip(values[0::2], values[1::2])]
    return values[0]


def place_body(shards, places, rows, by_rows, where, *refs):
    sources, out, sems = refs[:places], refs[places], refs[places + 1]
    width = sources[0].shape[1]
    copies = []
    for k in range(places):
        for z in range(shards):
            if by_rows:
                start = (where[z] * places + where[shards + k]) * rows
                target = out.at[pl.ds(pl.multiple_of(start, rows), rows)]
            else:
                target = out.at[
                    pl.ds(pl.multiple_of(where[shards + k] * rows, rows), rows),
                    pl.ds(pl.multiple_of(where[z] * width, width), width),
                ]
            copies.append(
                pltpu.make_async_copy(sources[k].at[pl.ds(z * rows, rows)], target, sems.at[k * shards + z])
            )
    for one in copies:
        one.start()
    for one in copies:
        one.wait()


def gather_pieces(piece):
    shards, places = lax.axis_size("shard"), lax.axis_size("ctx")
    along = jnp.concatenate([piece] + [relative(piece, "shard", k) for k in range(1, shards)], axis=0)
    return [along] + [relative(along, "ctx", k) for k in range(1, places)]


def gather_weight(value, by_rows):
    shards, places = lax.axis_size("shard"), lax.axis_size("ctx")
    rows = value.shape[0] // places
    if rows % 16:
        return lax.all_gather(value, "shard", axis=0 if by_rows else 1, tiled=True)
    z, c = lax.axis_index("shard"), lax.axis_index("ctx")
    piece = lax.dynamic_slice_in_dim(value, c * rows, rows, 0)
    pieces = gather_pieces(piece)
    where = jnp.concatenate([z ^ jnp.arange(shards), c ^ jnp.arange(places)]).astype(jnp.int32)
    if by_rows:
        shape = (value.shape[0] * shards, value.shape[1])
    else:
        shape = (value.shape[0], value.shape[1] * shards)
    ins = [(p, None, None) for p in pieces]
    outs = [(shape, value.dtype, None, None)]
    scratch = [pltpu.SemaphoreType.DMA((shards * places,))]
    return call(
        functools.partial(place_body, shards, places, rows, by_rows), (1,), ins, outs, scratch, where, name="place"
    )[0]


def own_rows(pieces):
    shards, places = lax.axis_size("shard"), lax.axis_size("ctx")
    z = lax.axis_index("shard")
    rows = pieces[0].shape[0] // shards
    near = [pieces[0]] + [relative(p, "ctx", k) for k, p in enumerate(pieces) if k]
    sums = []
    for k in range(shards):
        start = (z ^ k) * rows
        sums.append(tree_sum([lax.dynamic_slice_in_dim(p, start, rows, 0).astype(F32) for p in near]))
    far = [sums[0]] + [relative(sums[k].astype(BF16), "shard", k).astype(F32) for k in range(1, shards)]
    return tree_sum(far)


def all_sum(value):
    for axis in ("ctx", "shard"):
        value = tree_sum([value] + [relative(value, axis, k) for k in range(1, lax.axis_size(axis))])
    return value


def state_before(ended, sign):
    ns = ended.shape[0] - EDGE
    got = [shifted(ended, "ctx", sign * d).astype(F32) for d in range(1, lax.axis_size("ctx"))]
    total = got[-1][:ns]
    for one in reversed(got[:-1]):
        total = one[:ns] + one[ns : ns + 1] * total
    return total


def swap(value):
    return lax.ppermute(value, "tp", [(0, 1), (1, 0)])


def pad_rows(value):
    return jnp.pad(value, ((0, EDGE - value.shape[0]), (0, 0)))


def per_device(
    seq_in, w_zx, w_bc, w_dt, w_out, norm_gain, conv_x, conv_bc, head_params, gate_gain, segments, pad_mask, cotangent
):
    rows, model = seq_in.shape[1:]
    layers = w_zx.shape[0]
    width = w_zx.shape[3]
    heads = head_params.shape[2]
    ns = w_bc.shape[2] // 2
    shards, places = lax.axis_size("shard"), lax.axis_size("ctx")
    inner_total = width * lax.axis_size("tp")
    z, c, t = lax.axis_index("shard"), lax.axis_index("ctx"), lax.axis_index("tp")
    flag = t.astype(jnp.int32).reshape(1)
    chunks = rows // CHUNK

    ids = jnp.concatenate([jnp.full((3,), -1, jnp.int32), segments[0]])
    ext = lax.dynamic_slice_in_dim(ids, c * rows, rows + 3, 0)
    seg = ext[3:]
    mask = lax.dynamic_slice_in_dim(pad_mask[0], c * rows, rows, 0)
    firsts = ext[2 : 2 + rows].reshape(chunks, CHUNK)[:, :1]
    lasts = seg.reshape(chunks, CHUNK)[:, CHUNK - 1 :]
    by_chunk = seg.reshape(chunks, CHUNK)
    columns = [(ext[3 - lag : 3 - lag + rows] == seg) for lag in (1, 2, 3)]
    columns += [mask, (by_chunk == firsts).reshape(rows), (by_chunk == lasts).reshape(rows), mask, seg]
    cols = jnp.stack([v.astype(F32) for v in columns], axis=1)
    segs = jnp.broadcast_to(seg.astype(F32)[None], (EDGE, rows))

    head_of = jnp.arange(width)[None] // (width // heads)
    spread = (jnp.arange(LANES)[:, None] == head_of).astype(BF16)
    at = jnp.arange(CHUNK)
    lower = (at[:, None] >= at[None]).astype(F32)
    sums = jnp.concatenate([(at[:, None] <= at[None]).astype(F32), (at[:, None] > at[None]).astype(F32)], axis=1)

    def half(value, which):
        return lax.dynamic_slice_in_dim(value, which * ns, ns, value.ndim - 1)

    weights = []
    for layer in range(layers):
        lanes_dt = jnp.pad(w_dt[layer], ((0, 0), (0, LANES - heads)))
        main = jnp.concatenate([w_zx[layer, :, 1], half(w_bc[layer], t), lanes_dt], axis=1)
        w_main = gather_weight(main, True)
        w_other = swap(w_main[:, width : width + ns])
        w_gate = gather_weight(w_zx[layer, :, 0], True)
        w_down = gather_weight(w_out[layer], False)
        weights.append((w_main, w_other, w_gate, w_down))

    hidden = seq_in[0]
    parts = None
    kept = []
    for layer in range(layers):
        w_main, w_other, w_gate, w_down = weights[layer]
        gain_in = pad_rows(norm_gain[layer][None])
        taps = pad_rows(conv_x[layer])
        taps_mine = pad_rows(half(conv_bc[layer], t))
        taps_bc = jnp.concatenate([taps_mine, pad_rows(half(conv_bc[layer], 1 - t))], axis=1)
        decay = -jnp.exp(head_params[layer, 1])
        head = jnp.pad(
            jnp.stack([head_params[layer, 0], decay]), ((0, EDGE - 2), (0, LANES - heads))
        )
        skip = jnp.repeat(head_params[layer, 2], width // heads)
        rowpack = pad_rows(jnp.stack([gate_gain[layer], skip]))

        hidden, low, x_raw, mine, other, dt_raw = enter(hidden, parts, gain_in, w_main, w_other, width, inner_total)
        tails = jnp.concatenate([v[rows - EDGE :] for v in (x_raw, mine, other)], axis=1)
        edge = shifted(tails, "ctx", 1)
        gate = jnp.dot(low, w_gate, preferred_element_type=F32)
        xc, bc, step, cum, entered, phi, ended = states(
            flag, x_raw, mine, other, dt_raw, edge, cols, taps, taps_bc, head, spread, lower
        )
        y_in = within(xc, bc, step, cum, cols, segs, spread)
        state_in = state_before(ended, 1)
        ssm, p_own, sq_own = leave(y_in, xc, bc, cum, cols, entered, phi, state_in, gate, rowpack, spread, w_down)
        parts = (p_own, swap(p_own), sq_own, swap(sq_own))
        kept.append(
            dict(
                hidden=hidden, low=low, x_raw=x_raw, mine=mine, dt_raw=dt_raw, edge=edge, gate=gate, xc=xc, bc=bc,
                step=step, cum=cum, entered=entered, phi=phi, ended=ended, state_in=state_in, ssm=ssm, parts=parts,
                gain_in=gain_in, taps=taps, taps_mine=taps_mine, head=head, rowpack=rowpack,
            )
        )
    scale = lax.rsqrt((parts[2] + parts[3])[:, :1] / inner_total + EPSILON)
    output = hidden + scale * (parts[0].astype(F32) + parts[1].astype(F32))

    direct = (model // (shards * places)) % 16 == 0
    where = (c ^ jnp.arange(places)).astype(jnp.int32)

    def weight_sum(a, b):
        if direct:
            return own_rows(weight_grad(where, places, shards, a, b))
        full = lax.dot_general(a, b, (((0,), (0,)), ((), ())), preferred_element_type=F32)
        return lax.psum_scatter(full, ("shard", "ctx"), scatter_dimension=0, tiled=True)

    up = cotangent[0]
    grads = []
    for layer in reversed(range(layers)):
        w_main, w_other, w_gate, w_down = weights[layer]
        k = kept[layer]
        do, dy, dgate, normed, gain_rows, begun = back_gate(
            up, k["parts"], k["ssm"], k["xc"], k["gate"], k["bc"], k["cum"], cols, k["phi"], k["ended"],
            k["rowpack"], spread, w_down, inner_total,
        )
        later = state_before(begun, -1)
        dx_in, left, dbc_in = back_within(k["xc"], k["bc"], k["step"], k["cum"], cols, segs, spread, dy)
        g_out = weight_sum(do, normed)
        g_gate = weight_sum(k["low"], dgate)
        edge = k["edge"]
        dx, last, prior, dbc, ddt, conv_rows, head_rows, skip_rows = back_inter(
            k["x_raw"], edge[:, :width], k["xc"], k["bc"], k["step"], k["cum"], cols, k["dt_raw"], dy, k["ssm"],
            dx_in, left, dbc_in, k["entered"], k["phi"], k["state_in"], later, k["taps"], k["head"], k["rowpack"],
            spread, sums,
        )
        dbc_theirs = swap(half(dbc, 1 - t))
        db, last_bc, prior_bc, conv_bc_rows = back_bc(
            k["mine"], edge[:, width : width + ns], cols, k["taps_mine"], half(dbc, t), dbc_theirs
        )
        back_rows = shifted(jnp.concatenate([prior, prior_bc], axis=1), "ctx", -1)
        dx = lax.dynamic_update_slice_in_dim(dx, (last + back_rows[:, :width]).astype(BF16), rows - EDGE, 0)
        db = lax.dynamic_update_slice_in_dim(db, (last_bc + back_rows[:, width:]).astype(BF16), rows - EDGE, 0)
        small = jnp.concatenate([db, ddt], axis=1)
        dlow = (
            lax.dot_general(dgate, w_gate, (((1,), (1,)), ((), ())), preferred_element_type=F32)
            + lax.dot_general(dx, w_main[:, :width], (((1,), (1,)), ((), ())), preferred_element_type=F32)
            + lax.dot_general(small, w_main[:, width:], (((1,), (1,)), ((), ())), preferred_element_type=F32)
        ).astype(BF16)
        up, norm_rows = back_norm(up, dlow, swap(dlow), k["hidden"], k["gain_in"])
        g_x = weight_sum(k["low"], dx)
        g_small = weight_sum(k["low"], small)
        packed = jnp.concatenate(
            [norm_rows[0], conv_rows[:5].reshape(-1), gain_rows[0], skip_rows[0], conv_bc_rows[:5].reshape(-1),
             head_rows[:2].reshape(-1)]
        )
        grads.insert(0, (g_gate, g_x, g_small, g_out, packed))

    packed = all_sum(jnp.concatenate([g[4] for g in grads])).reshape(layers, -1)
    cuts = [model, 5 * width, width, width, 5 * ns, 2 * LANES]
    ends = [sum(cuts[: i + 1]) for i in range(len(cuts))]
    n_sum, cx_sum, gg_sum, sk_sum, cb_sum, hd_sum = jnp.split(packed, ends[:-1], axis=1)
    cb_mine = cb_sum.reshape(layers, 5, ns)
    small_mine = jnp.stack([g[2][:, :ns] for g in grads])
    cb_other, small_other = swap(cb_mine), swap(small_mine)

    def ordered(own, other):
        first = jnp.where(t == 0, own, other)
        return jnp.concatenate([first, jnp.where(t == 0, other, own)], axis=-1)

    hd = hd_sum.reshape(layers, 2, LANES)[:, :, :heads]
    skip_sum = jnp.sum(sk_sum.reshape(layers, heads, width // heads), axis=-1)
    return (
        output[None],
        up[None],
        jnp.stack([jnp.stack([g[0], g[1]], axis=1) for g in grads]),
        ordered(small_mine, small_other),
        jnp.stack([g[2][:, ns : ns + heads] for g in grads]),
        jnp.stack([g[3].T for g in grads]),
        n_sum,
        cx_sum.reshape(layers, 5, width),
        ordered(cb_mine, cb_other),
        jnp.concatenate([hd, skip_sum[:, None]], axis=1),
        gg_sum,
    )


def solution(mesh):
    in_specs = (
        P("shard", "ctx", None),
        P(None, "shard", None, "tp"),
        P(None, "shard", None),
        P(None, "shard", "tp"),
        P(None, "tp", "shard"),
        P(),
        P(None, None, "tp"),
        P(),
        P(None, None, "tp"),
        P(None, "tp"),
        P("shard", None),
        P("shard", None),
        P("shard", "ctx", None),
    )
    out_specs = (
        P("shard", "ctx", None),
        P("shard", "ctx", None),
        P(None, ("shard", "ctx"), None, "tp"),
        P(None, ("shard", "ctx"), None),
        P(None, ("shard", "ctx"), "tp"),
        P(None, "tp", ("shard", "ctx")),
        P(),
        P(None, None, "tp"),
        P(),
        P(None, None, "tp"),
        P(None, "tp"),
    )
    return jax.shard_map(per_device, mesh=mesh, in_specs=in_specs, out_specs=out_specs, check_vma=False)
```

```python
import functools

import jax
import jax.numpy as jnp
from jax import lax
from jax.experimental import pallas as pl
from jax.experimental.pallas import tpu as pltpu
from jax.sharding import PartitionSpec as P

EPSILON = 1e-05
EXACT = lax.Precision.HIGHEST
F32 = jnp.float32
BF16 = jnp.bfloat16
CHUNK = 128
LANES = 128
EDGE = 8
CLOSED = -1e30
VMEM = 54 << 20


def dot(a, b, dims=((1,), (0,)), precision=None):
    return lax.dot_general(a, b, (dims, ((), ())), precision=precision, preferred_element_type=F32)


def split(values):
    high = values.astype(BF16)
    return high, (values - high.astype(F32)).astype(BF16)


def expand(values, spread):
    return dot(jnp.concatenate(split(values), axis=1), spread)


def folded(payloads):
    ns = payloads[0].shape[0] - EDGE
    total = payloads[-1][:ns].astype(F32)
    for one in reversed(payloads[:-1]):
        total = one[:ns].astype(F32) + one[ns : ns + 1].astype(F32) * total
    return total


def conv_shifts(ext, same):
    return [ext[EDGE:]] + [pltpu.roll(ext, lag, 0)[EDGE:] * same[lag] for lag in (1, 2, 3)]


def conv_sum(shifts, taps):
    total = taps[4:5] + taps[0:1] * shifts[0]
    for lag in (1, 2, 3):
        total = total + taps[lag : lag + 1] * shifts[lag]
    return total


def same_columns(cols, width):
    return [None] + [jnp.broadcast_to(cols[:, lag - 1 : lag], (cols.shape[0], width)) for lag in (1, 2, 3)]


def pair_masked(values):
    lane = lax.broadcasted_iota(jnp.int32, values.shape, 1)
    zero = jnp.zeros_like(values)
    first = lane < LANES // 2
    return jnp.concatenate([jnp.where(first, values, zero), jnp.where(first, zero, values)], axis=0)


def pairs_bias(seg_col, seg_row, later_rows):
    size = seg_col.shape[0]
    row = lax.broadcasted_iota(jnp.int32, (size, size), 0)
    col = lax.broadcasted_iota(jnp.int32, (size, size), 1)
    ordered = (row >= col) if later_rows else (row <= col)
    return jnp.where(ordered & (seg_col == seg_row), 0.0, CLOSED)


def silu_parts(values):
    sig = jax.nn.sigmoid(values)
    return sig, values * sig


def call(body, grid, ins, outs, scratch=(), scalars=None, flops=0, name=None):
    count = 0 if scalars is None else 1

    def adapt(block, fn):
        if block is None:
            return pl.BlockSpec(memory_space=pl.ANY)
        return pl.BlockSpec(block, fn)

    in_specs = [adapt(block, fn) for _, block, fn in ins]
    out_specs = [adapt(block, fn) for _, _, block, fn in outs]
    shapes = [jax.ShapeDtypeStruct(shape, dtype) for shape, dtype, _, _ in outs]
    moved = sum(a.size * a.dtype.itemsize for a, _, _ in ins) + sum(
        s.size * s.dtype.itemsize for s in shapes
    )
    made = pl.pallas_call(
        body,
        out_shape=shapes,
        grid_spec=pltpu.PrefetchScalarGridSpec(
            num_scalar_prefetch=count,
            grid=grid,
            in_specs=in_specs,
            out_specs=out_specs,
            scratch_shapes=list(scratch),
        ),
        compiler_params=pltpu.CompilerParams(
            vmem_limit_bytes=VMEM, dimension_semantics=("arbitrary",) * len(grid)
        ),
        cost_estimate=pl.CostEstimate(flops=1, bytes_accessed=1, transcendentals=0),
        name=name,
    )
    arrays = [a for a, _, _ in ins]
    return made(*(([scalars] if count else []) + arrays))


def rows_at(i, *_):
    return (i, 0)


def columns_at(i, *_):
    return (0, i)


def fixed(*_):
    return (0, 0)


def piece_copies(pieces, sems):
    copies = []
    for source, target, start in pieces:
        rows = source.shape[0]
        at = target.at[pl.ds(pl.multiple_of(start, rows), rows)]
        copies.append(pltpu.make_async_copy(source, at, sems.at[len(copies)]))
    for one in copies:
        one.start()
    for one in copies:
        one.wait()


def enter_body(first, inner_total, cuts, where, *refs):
    shards, places, rows = cuts
    near, refs = refs[:places], refs[places:]
    far, refs = (refs[:shards], refs[shards:]) if first else ((), refs)
    if first:
        h_ref, gain, u_ref, turned_ref, x_ref, bc_ref, dt_ref, w_x, w_other, sems = refs
        hidden = h_ref[...].astype(F32)
    else:
        h_ref, p_ref, q_ref, gain, h_out, u_ref, turned_ref, x_ref, bc_ref, dt_ref, w_x, w_other, sems = refs
        model = h_ref.shape[1]
        summed = p_ref[:, :model].astype(F32) + q_ref[:, :model].astype(F32)
        hidden = h_ref[...].astype(F32) + gated_scale(p_ref, q_ref, model, inner_total) * summed
        h_out[...] = hidden
    both = bc_ref.shape[1]
    width = x_ref.shape[1]

    @pl.when(pl.program_id(0) == 0)
    def _():
        pieces = [(v, w_other, where[z] * v.shape[0]) for z, v in enumerate(far)]
        for z in range(shards):
            for k in range(places):
                start = (where[z] * places + where[shards + k]) * rows
                source = near[k].at[pl.ds(z * rows, rows)]
                pieces.append((source.at[:, :width], w_x, start))
                if not far:
                    pieces.append((source.at[:, width:], w_other, start))
        piece_copies(pieces, sems)

    norm = lax.rsqrt(jnp.mean(hidden * hidden, axis=1, keepdims=True) + EPSILON)
    lowered = (hidden * norm * gain[0:1]).astype(BF16)
    u_ref[...] = lowered
    turned_ref[...] = lowered.T
    x_ref[...] = dot(lowered, w_x[...]).astype(BF16)
    made = dot(lowered, w_other[...])
    bc_ref[...] = made[:, :both].astype(BF16)
    dt_ref[...] = made[:, both:]


def gated_scale(p_ref, q_ref, model, inner_total):
    squares = p_ref[:, model:].astype(F32) + q_ref[:, model:].astype(F32)
    return lax.rsqrt((squares[:, 0:1] + squares[:, 1:2]) / inner_total + EPSILON)


def block_of(part):
    array, width, index = part
    return (array, (array.shape[0], width), lambda *_: (0, index))


def enter(where, shards, near, far, hidden, parts, gain, width, both, inner_total):
    rows, model = hidden.shape
    first = parts is None
    block = min(256, rows)
    wide = (block, model)
    ins = [(v, None, None) for v in near + far] + [(hidden, wide, rows_at)]
    outs = []
    if not first:
        ins += [(part, (block, model + LANES), rows_at) for part in parts]
        outs.append(((rows, model), F32, wide, rows_at))
    ins += [(gain, gain.shape, fixed)]
    outs += [
        ((rows, model), BF16, wide, rows_at),
        ((model, rows), BF16, (model, block), columns_at),
        ((rows, width), BF16, (block, width), rows_at),
        ((rows, both), BF16, (block, both), rows_at),
        ((rows, LANES), F32, (block, LANES), rows_at),
    ]
    outs += [((model, v), BF16, (model, v), fixed) for v in (width, both + LANES)]
    scratch = [pltpu.SemaphoreType.DMA((shards * (2 * len(near)),))]
    cuts = (shards, len(near), near[0].shape[0] // shards)
    made = call(
        functools.partial(enter_body, first, inner_total, cuts), (rows // block,), ins, outs, scratch, where, name="enter"
    )
    return [hidden] + list(made) if first else list(made)


def states_body(
    x_ref, raw_bc_ref, dt_ref, before_ref, gain_ref, w_x, w_other, cols_ref, taps_ref, taps_bc_ref, head_ref,
    spread_ref, lower_ref, edge_ref, xc_ref, bc_ref, step_ref, cum_ref, enter_ref, phi_ref, last_ref,
    tail_x, tail_bc, state, phi,
):
    chunk = pl.program_id(0)
    width = x_ref.shape[1]
    ns = raw_bc_ref.shape[1] // 2

    @pl.when(chunk == 0)
    def _():
        before = before_ref[...].astype(F32)
        norm = lax.rsqrt(jnp.mean(before * before, axis=1, keepdims=True) + EPSILON)
        lowered = (before * norm * gain_ref[0:1]).astype(BF16)
        edge = dot(lowered, w_x[...]).astype(BF16)
        edge_bc = dot(lowered, w_other[:, : 2 * ns]).astype(BF16)
        edge_ref[:, :width] = edge
        edge_ref[:, width:] = edge_bc
        tail_x[...] = edge.astype(F32)
        tail_bc[...] = edge_bc.astype(F32)
        state[...] = jnp.zeros_like(state)
        phi[...] = jnp.ones_like(phi)

    cols = cols_ref[...]
    same = same_columns(cols, LANES)
    dt = jax.nn.softplus(dt_ref[...] + head_ref[0:1]) * cols[:, 3:4]
    rates = head_ref[1:2] * dt
    cum = dot(lower_ref[...], rates, precision=EXACT)
    step_ref[...] = dt
    cum_ref[...] = cum
    size = cum.shape[0]
    tail_dt = cols[:, 5:6] * jnp.exp(cum[size - 1 : size] - cum) * dt
    tail_wide = expand(tail_dt, spread_ref[...])
    fold = cols[size - 1 : size, 4:5] * jnp.exp(cum[size - EDGE : size])[EDGE - 1 : EDGE]
    fold_rows = jnp.broadcast_to(fold, phi.shape)
    fold_wide = expand(fold_rows, spread_ref[...])[0:1]

    halves = []
    for i in range(2):
        part = slice(i * ns, (i + 1) * ns)
        now = raw_bc_ref[:, part].astype(F32)
        shifts = conv_shifts(jnp.concatenate([tail_bc[:, part], now], axis=0), same)
        tail_bc[:, part] = now[size - EDGE :]
        halves.append(silu_parts(conv_sum(shifts, taps_bc_ref[:, part]))[1].astype(BF16))
        bc_ref[:, part] = halves[i]
    b_part = halves[0]
    b_turned = b_part.astype(F32).T.astype(BF16)

    enter_ref[0] = state[...].astype(BF16)
    phi_ref[0] = phi[...]
    for i in range(width // LANES):
        part = slice(i * LANES, (i + 1) * LANES)
        now = x_ref[:, part].astype(F32)
        shifts = conv_shifts(jnp.concatenate([tail_x[:, part], now], axis=0), same)
        tail_x[:, part] = now[size - EDGE :]
        x_conv = silu_parts(conv_sum(shifts, taps_ref[:, part]))[1].astype(BF16)
        xc_ref[:, part] = x_conv
        held = (x_conv.astype(F32) * tail_wide[:, part]).astype(BF16)
        state[:, part] = fold_wide[:, part] * state[:, part] + dot(b_turned, held)
    phi[...] = phi[...] * fold_rows

    @pl.when(chunk == pl.num_programs(0) - 1)
    def _():
        last_ref[:ns] = state[...].astype(BF16)
        last_ref[ns:] = expand(phi[...], spread_ref[...]).astype(BF16)


def states(x_raw, raw_bc, dt_raw, before, gain, weights, cols, taps, taps_bc, head, spread, lower):
    rows, width = x_raw.shape
    ns = raw_bc.shape[1] // 2
    count = rows // CHUNK
    ins = [
        (x_raw, (CHUNK, width), rows_at),
        (raw_bc, (CHUNK, 2 * ns), rows_at),
        (dt_raw, (CHUNK, LANES), rows_at),
        (before, before.shape, fixed),
        (gain, gain.shape, fixed),
        block_of(weights["x"]),
        block_of(weights["other"]),
        (cols, (CHUNK, cols.shape[1]), rows_at),
        (taps, taps.shape, fixed),
        (taps_bc, taps_bc.shape, fixed),
        (head, head.shape, fixed),
        (spread, spread.shape, fixed),
        (lower, lower.shape, fixed),
    ]
    outs = [
        ((EDGE, width + 2 * ns), BF16, (EDGE, width + 2 * ns), fixed),
        ((rows, width), BF16, (CHUNK, width), rows_at),
        ((rows, 2 * ns), BF16, (CHUNK, 2 * ns), rows_at),
        ((rows, LANES), F32, (CHUNK, LANES), rows_at),
        ((rows, LANES), F32, (CHUNK, LANES), rows_at),
        ((count, ns, width), BF16, (1, ns, width), lambda i, *_: (i, 0, 0)),
        ((count, EDGE, LANES), F32, (1, EDGE, LANES), lambda i, *_: (i, 0, 0)),
        ((ns + EDGE, width), BF16, (ns + EDGE, width), fixed),
    ]
    scratch = [
        pltpu.VMEM((EDGE, width), F32),
        pltpu.VMEM((EDGE, 2 * ns), F32),
        pltpu.VMEM((ns, width), F32),
        pltpu.VMEM((EDGE, LANES), F32),
    ]
    return call(states_body, (count,), ins, outs, scratch, flops=2 * rows * width * ns * 4, name="states")


def within_body(xc_ref, bc_ref, step_ref, cum_ref, cols_ref, segs_ref, spread_ref, y_ref):
    ns = bc_ref.shape[1] // 2
    width = xc_ref.shape[1]
    cum = cum_ref[...]
    cum_rows = cum.T
    bias = pairs_bias(cols_ref[:, 7:8], segs_ref[0:1], True)
    both = dot(bc_ref[:, ns:], bc_ref[:, :ns], ((1,), (1,)))
    step_wide = expand(step_ref[...], spread_ref[...])
    for pair in range(width // LANES):
        part = slice(pair * LANES, (pair + 1) * LANES)
        weighted = (xc_ref[:, part].astype(F32) * step_wide[:, part]).astype(BF16)
        maps = []
        for head in (2 * pair, 2 * pair + 1):
            gap = (cum[:, head : head + 1] - cum_rows[head : head + 1]) + bias
            maps.append((jnp.exp(gap) * both).astype(BF16))
        y_ref[:, part] = dot(jnp.concatenate(maps, axis=1), pair_masked(weighted))


def within(xc, bc, step, cum, cols, segs, spread):
    rows, width = xc.shape
    ins = [
        (xc, (CHUNK, width), rows_at),
        (bc, (CHUNK, bc.shape[1]), rows_at),
        (step, (CHUNK, LANES), rows_at),
        (cum, (CHUNK, LANES), rows_at),
        (cols, (CHUNK, cols.shape[1]), rows_at),
        (segs, (EDGE, CHUNK), lambda i, *_: (0, i)),
        (spread, spread.shape, fixed),
    ]
    outs = [((rows, width), F32, (CHUNK, width), rows_at)]
    return call(within_body, (rows // CHUNK,), ins, outs, flops=2 * rows * CHUNK * width * 4, name="within")[0]


def leave_body(count, *refs):
    payloads, refs = refs[:count], refs[count:]
    (w_gate, w_out, y_ref, low_ref, xc_ref, bc_ref, cum_ref, cols_ref, enter_ref, phi_ref, rows_ref, spread_ref) = refs[:12]
    ssm_ref, gate_ref, p_ref, in_ref, normed = refs[12:]
    ns = in_ref.shape[0]
    width = xc_ref.shape[1]
    spread = spread_ref[...]

    @pl.when(pl.program_id(0) == 0)
    def _():
        in_ref[...] = folded([p[...] for p in payloads])

    gate_ref[...] = dot(low_ref[...], w_gate[...])
    for sub in range(y_ref.shape[0] // CHUNK):
        here = slice(sub * CHUNK, (sub + 1) * CHUNK)
        phi_wide = expand(phi_ref[sub], spread)[0:1]
        begun = (enter_ref[sub].astype(F32) + phi_wide * in_ref[...]).astype(BF16)
        carried = cols_ref[here, 4:5] * jnp.exp(cum_ref[here])
        carried_wide = expand(carried, spread)
        far = dot(bc_ref[here, ns:], begun)
        ssm_ref[here] = y_ref[here] + carried_wide * far
    total = jnp.zeros((y_ref.shape[0], LANES), F32)
    for i in range(width // LANES):
        part = slice(i * LANES, (i + 1) * LANES)
        mixed = ssm_ref[:, part] + rows_ref[1:2, part] * xc_ref[:, part].astype(F32)
        gated = mixed * silu_parts(gate_ref[:, part])[1]
        total = total + gated * gated
        normed[:, part] = (gated * rows_ref[0:1, part]).astype(BF16)
    high, rest = split(jnp.broadcast_to(jnp.sum(total, axis=1, keepdims=True), total.shape))
    lane = lax.broadcasted_iota(jnp.int32, total.shape, 1)
    model = w_out.shape[0]
    p_ref[:, :model] = dot(normed[...], w_out[...], ((1,), (1,))).astype(BF16)
    p_ref[:, model:] = jnp.where(lane == 0, high.astype(F32), rest.astype(F32)).astype(BF16)


def leave(payloads, y_in, low, xc, bc, cum, cols, entered, phi, rowpack, spread, weights):
    rows, width = xc.shape
    model = low.shape[1]
    ns = bc.shape[1] // 2
    block = min(256, rows)
    subs = block // CHUNK
    ins = [(p, p.shape, fixed) for p in payloads]
    ins += [
        block_of(weights["gate"]),
        block_of(weights["out"]),
        (y_in, (block, width), rows_at),
        (low, (block, model), rows_at),
        (xc, (block, width), rows_at),
        (bc, (block, bc.shape[1]), rows_at),
        (cum, (block, LANES), rows_at),
        (cols, (block, cols.shape[1]), rows_at),
        (entered, (subs, ns, width), lambda i, *_: (i, 0, 0)),
        (phi, (subs, EDGE, LANES), lambda i, *_: (i, 0, 0)),
        (rowpack, rowpack.shape, fixed),
        (spread, spread.shape, fixed),
    ]
    outs = [
        ((rows, width), F32, (block, width), rows_at),
        ((rows, width), F32, (block, width), rows_at),
        ((rows, model + LANES), BF16, (block, model + LANES), rows_at),
        ((ns, width), F32, (ns, width), fixed),
    ]
    scratch = [pltpu.VMEM((block, width), BF16)]
    return call(functools.partial(leave_body, len(payloads)), (rows // block,), ins, outs, scratch, name="leave")


def back_gate_body(
    inner_total, ends, *refs
):
    if ends:
        hidden_ref, refs = refs[0], refs[1:]
        output_ref, refs = refs[14], refs[:14] + refs[15:]
    (
        up_ref, p_ref, q_ref, ssm_ref, xc_ref, gate_ref, bc_ref, cum_ref, cols_ref, phi_ref,
        factor_ref, rows_ref, spread_ref, w_ref,
        do_ref, dy_ref, dgate_ref, n_ref, gain_ref, out_ref, state,
    ) = refs
    step = pl.program_id(0)
    ns = state.shape[0]
    width = xc_ref.shape[1]
    spread = spread_ref[...]

    @pl.when(step == 0)
    def _():
        gain_ref[...] = jnp.zeros_like(gain_ref)
        state[...] = jnp.zeros_like(state)

    model = up_ref.shape[1]
    scale = gated_scale(p_ref, q_ref, model, inner_total)
    up = up_ref[...].astype(BF16)
    do_ref[...] = up.T
    summed = p_ref[:, :model].astype(F32) + q_ref[:, :model].astype(F32)
    if ends:
        output_ref[...] = hidden_ref[...].astype(F32) + scale * summed
    spread_sum = jnp.sum(up.astype(F32) * summed, axis=1, keepdims=True)
    pull = scale * scale * scale * spread_sum / inner_total
    scale_wide = jnp.broadcast_to(scale, (scale.shape[0], LANES))
    pull_wide = jnp.broadcast_to(pull, scale_wide.shape)
    back = dot(up, w_ref[...])
    for i in range(width // LANES):
        part = slice(i * LANES, (i + 1) * LANES)
        gain = rows_ref[0:1, part]
        gate = gate_ref[:, part]
        sig, soft = silu_parts(gate)
        mixed = ssm_ref[:, part] + rows_ref[1:2, part] * xc_ref[:, part].astype(F32)
        gated = mixed * soft
        scaled = gated * scale_wide
        grad = back[:, part]
        gain_ref[0:1, part] += jnp.sum(grad * scaled, axis=0, keepdims=True)
        grad_gated = grad * gain * scale_wide - gated * pull_wide
        dy_ref[:, part] = (grad_gated * soft).astype(BF16)
        dgate_ref[:, part] = (grad_gated * mixed * (sig * (1.0 + gate * (1.0 - sig)))).astype(BF16)
        n_ref[:, part] = (scaled * gain).astype(BF16)
    for sub in range(up_ref.shape[0] // CHUNK):
        here = slice(sub * CHUNK, (sub + 1) * CHUNK)
        phi_wide = expand(phi_ref[sub], spread)[0:1]
        carried_wide = expand(cols_ref[here, 4:5] * jnp.exp(cum_ref[here]), spread)
        c_turned = bc_ref[here, ns:].astype(F32).T.astype(BF16)
        carried_dy = (dy_ref[here].astype(F32) * carried_wide).astype(BF16)
        state[...] += phi_wide * dot(c_turned, carried_dy)

    @pl.when(step == pl.num_programs(0) - 1)
    def _():
        out_ref[:ns] = state[...].astype(BF16)
        out_ref[ns:] = factor_ref[...]


def back_gate(up, parts, ssm, xc, gate, bc, cum, cols, phi, ended, rowpack, spread, weights, inner_total, hidden=None):
    rows, width = xc.shape
    model = up.shape[1]
    ns = bc.shape[1] // 2
    block = min(256, rows)
    subs = block // CHUNK
    wide = (block, model)
    ins = [
        (up, wide, rows_at),
        (parts[0], (block, model + LANES), rows_at),
        (parts[1], (block, model + LANES), rows_at),
        (ssm, (block, width), rows_at),
        (xc, (block, width), rows_at),
        (gate, (block, width), rows_at),
        (bc, (block, 2 * ns), rows_at),
        (cum, (block, LANES), rows_at),
        (cols, (block, cols.shape[1]), rows_at),
        (phi, (subs, EDGE, LANES), lambda i, *_: (i, 0, 0)),
        (ended, (EDGE, width), lambda i, *_: (ns // EDGE, 0)),
        (rowpack, rowpack.shape, fixed),
        (spread, spread.shape, fixed),
        block_of(weights["out"]),
    ]
    outs = [
        ((model, rows), BF16, (model, block), columns_at),
        ((rows, width), BF16, (block, width), rows_at),
        ((rows, width), BF16, (block, width), rows_at),
        ((rows, width), BF16, (block, width), rows_at),
        ((EDGE, width), F32, (EDGE, width), fixed),
        ((ns + EDGE, width), BF16, (ns + EDGE, width), fixed),
    ]
    if hidden is not None:
        ins = [(hidden, wide, rows_at)] + ins
        outs = [((rows, model), F32, wide, rows_at)] + outs
    scratch = [pltpu.VMEM((ns, width), F32)]
    return call(
        functools.partial(back_gate_body, inner_total, hidden is not None), (rows // block,), ins, outs, scratch,
        flops=2 * rows * width * model * 1.3, name="back_gate",
    )


def back_within_body(
    xc_ref, bc_ref, step_ref, cum_ref, cols_ref, segs_ref, spread_ref, gather_ref, dy_ref, ssm_ref,
    dx_ref, left_ref, dbc_ref, products,
):
    ns = bc_ref.shape[1] // 2
    size, width = xc_ref.shape
    cum = cum_ref[...]
    cum_rows = cum.T
    bias = pairs_bias(cols_ref[:, 7:8], segs_ref[0:1], False)
    b_part = bc_ref[:, :ns]
    c_part = bc_ref[:, ns:]
    both = dot(b_part, c_part, ((1,), (1,)))
    step_wide = expand(step_ref[...], spread_ref[...])
    grad_both = jnp.zeros((size, size), F32)
    for pair in range(width // LANES):
        part = slice(pair * LANES, (pair + 1) * LANES)
        weighted = (xc_ref[:, part].astype(F32) * step_wide[:, part]).astype(BF16)
        dy = dy_ref[:, part]
        dy_pair = pair_masked(dy)
        grad_maps = dot(weighted, dy_pair, ((1,), (1,)))
        maps = []
        for k in (0, 1):
            head = 2 * pair + k
            decay = jnp.exp((cum_rows[head : head + 1] - cum[:, head : head + 1]) + bias)
            maps.append((decay * both).astype(BF16))
            grad_both = grad_both + decay * grad_maps[:, k * size : (k + 1) * size]
        grad_x = dot(jnp.concatenate(maps, axis=1), dy_pair)
        dx_ref[:, part] = grad_x.astype(BF16)
        high, rest = split(dy.astype(F32) * ssm_ref[:, part] - weighted.astype(F32) * grad_x)
        products[:size, part] = high
        products[size:, part] = rest
    left = dot(products[...], gather_ref[...])
    left_ref[...] = left[:size] + left[size:]
    dbc_ref[:, :ns] = dot(grad_both.astype(BF16), c_part)
    dbc_ref[:, ns:] = dot(grad_both.T.astype(BF16), b_part)


def back_within(xc, bc, step, cum, cols, segs, spread, gather, dy, ssm):
    rows, width = xc.shape
    ins = [
        (xc, (CHUNK, width), rows_at),
        (bc, (CHUNK, bc.shape[1]), rows_at),
        (step, (CHUNK, LANES), rows_at),
        (cum, (CHUNK, LANES), rows_at),
        (cols, (CHUNK, cols.shape[1]), rows_at),
        (segs, (EDGE, CHUNK), lambda i, *_: (0, i)),
        (spread, spread.shape, fixed),
        (gather, gather.shape, fixed),
        (dy, (CHUNK, width), rows_at),
        (ssm, (CHUNK, width), rows_at),
    ]
    outs = [
        ((rows, width), BF16, (CHUNK, width), rows_at),
        ((rows, LANES), F32, (CHUNK, LANES), rows_at),
        ((rows, bc.shape[1]), F32, (CHUNK, bc.shape[1]), rows_at),
    ]
    scratch = [pltpu.VMEM((2 * CHUNK, width), BF16)]
    return call(back_within_body, (rows // CHUNK,), ins, outs, scratch, name="back_within")


def conv_back(ext, same, taps, grad_conv, next_rows):
    size = ext.shape[0] - EDGE
    shifts = conv_shifts(ext, same)
    pre = conv_sum(shifts, taps)
    sig = jax.nn.sigmoid(pre)
    grad_pre = grad_conv * (sig * (1.0 + pre * (1.0 - sig)))
    sums = [jnp.sum(grad_pre * shifts[lag], axis=0, keepdims=True) for lag in range(4)]
    sums.append(jnp.sum(grad_pre, axis=0, keepdims=True))
    zero = jnp.zeros((EDGE, ext.shape[1]), F32)
    length = size + 2 * EDGE
    raw = taps[0:1] * jnp.concatenate([zero, grad_pre], axis=0)
    firsts = []
    for lag in (1, 2, 3):
        term = grad_pre * same[lag] * taps[lag : lag + 1]
        firsts.append(term[:EDGE])
        padded = jnp.concatenate([zero, term, next_rows[lag - 1]], axis=0)
        raw = raw + pltpu.roll(padded, length - lag, 0)[: size + EDGE]
    return raw, firsts, sums


def back_inter_body(count_in, flag, *refs):
    payloads, refs = refs[:count_in], refs[count_in:]
    (
        x_ref, before_ref, edge_ref, xc_ref, bc_ref, step_ref, cum_ref, cols_ref, dt_ref, dy_ref, dxi_ref,
        left_ref, dbci_ref, enter_ref, phi_ref, in_ref, taps_ref, head_ref, rows_ref, spread_ref, gather_ref, sums_ref,
        dx_ref, last_ref, prior_ref, mine_ref, theirs_ref, ddt_ref, conv_ref, heads_ref, skip_ref,
        grad_state, next_rows, wide, far, carried, held, begun, ending, products,
    ) = refs
    step = pl.program_id(0)
    chunk = pl.num_programs(0) - 1 - step
    ns = in_ref.shape[0]
    size, width = xc_ref.shape

    @pl.when(step == 0)
    def _():
        grad_state[...] = folded([p[...] for p in payloads])
        next_rows[...] = jnp.zeros_like(next_rows)
        conv_ref[...] = jnp.zeros_like(conv_ref)
        heads_ref[...] = jnp.zeros_like(heads_ref)
        skip_ref[...] = jnp.zeros_like(skip_ref)

    cols = cols_ref[...]
    same = same_columns(cols, LANES)
    cum = cum_ref[...]
    dt = step_ref[...]
    decay_in = cols[:, 4:5] * jnp.exp(cum)
    decay_out = cols[:, 5:6] * jnp.exp(cum[size - 1 : size] - cum)
    fold_rows = jnp.broadcast_to(decay_in[size - EDGE : size][EDGE - 1 : EDGE], (EDGE, LANES))
    b_part = bc_ref[:, :ns]
    c_part = bc_ref[:, ns:]
    c_turned = c_part.astype(F32).T.astype(BF16)
    stacked = jnp.concatenate([decay_in, decay_out, dt, fold_rows, phi_ref[0]], axis=0)
    wide[...] = expand(stacked, spread_ref[...])
    fold_at = 3 * size
    for i in range(width // LANES):
        part = slice(i * LANES, (i + 1) * LANES)
        dy = dy_ref[:, part].astype(F32)
        weighted = xc_ref[:, part].astype(F32) * wide[2 * size : 3 * size, part]
        fold_wide = wide[fold_at : fold_at + 1, part]
        grad_end = grad_state[:, part]
        start = enter_ref[0, :, part].astype(F32) + wide[fold_at + EDGE : fold_at + EDGE + 1, part] * in_ref[:, part]
        carried[:, part] = (dy * wide[:size, part]).astype(BF16)
        held[:, part] = (weighted * wide[size : 2 * size, part]).astype(BF16)
        begun[:, part] = start.astype(BF16)
        ending[:, part] = grad_end.astype(BF16)
        pass_sum = jnp.sum(start * grad_end, axis=0, keepdims=True) * fold_wide
        products[2 * size :, part] = jnp.broadcast_to(pass_sum, (2 * EDGE, LANES)).astype(BF16)
        grad_state[:, part] = fold_wide * grad_end
    far[...] = dot(b_part, ending[...])
    dbc_c = dbci_ref[:, ns:] + dot(carried[...], begun[...], ((1,), (1,)))
    dbc_b = dbci_ref[:, :ns] + dot(held[...], ending[...], ((1,), (1,)))
    grad_state[...] += dot(c_turned, carried[...])
    own_b = flag[0] == 0
    mine_ref[...] = jnp.where(own_b, dbc_b, dbc_c).astype(BF16)
    theirs_ref[...] = jnp.where(own_b, dbc_c, dbc_b).astype(BF16)

    first_chunk = chunk == 0
    for i in range(width // LANES):
        part = slice(i * LANES, (i + 1) * LANES)
        dy = dy_ref[:, part].astype(F32)
        x_conv = xc_ref[:, part].astype(F32)
        dt_wide = wide[2 * size : 3 * size, part]
        grad_far = wide[size : 2 * size, part] * far[:, part]
        grad_weighted = dxi_ref[:, part].astype(F32) + grad_far
        products[:size, part] = (x_conv * dt_wide * grad_far).astype(BF16)
        products[size : 2 * size, part] = (x_conv * grad_weighted).astype(BF16)
        skip_ref[0:1, part] += jnp.sum(dy * x_conv, axis=0, keepdims=True)
        grad_conv = dt_wide * grad_weighted + rows_ref[1:2, part] * dy
        ahead = jnp.where(first_chunk, edge_ref[:, part].astype(F32), before_ref[:, part].astype(F32))
        ext = jnp.concatenate([ahead, x_ref[:, part].astype(F32)], axis=0)
        raw, firsts, tap_sums = conv_back(
            ext, same, taps_ref[:, part], grad_conv, [next_rows[k, :, part] for k in range(3)]
        )
        for k in range(3):
            next_rows[k, :, part] = firsts[k]
        for k in range(5):
            conv_ref[k : k + 1, part] += tap_sums[k]
        dx_ref[:, part] = raw[EDGE:].astype(BF16)
        prior_ref[:, part] = raw[:EDGE]

        @pl.when(step == 0)
        def _(raw=raw, part=part):
            last_ref[:, part] = raw[size:]

    per_head = dot(products[...], gather_ref[...])
    outward, direct, through = per_head[:size], per_head[size : 2 * size], per_head[2 * size : 2 * size + 1]
    grad_rate = dot(sums_ref[...], jnp.concatenate([left_ref[...], outward], axis=0), precision=EXACT) + through
    grad_dt = direct + head_ref[1:2] * grad_rate
    grad_raw = grad_dt * cols[:, 3:4] * jax.nn.sigmoid(dt_ref[...] + head_ref[0:1])
    ddt_ref[...] = grad_raw.astype(BF16)
    heads_ref[0:1] += jnp.sum(grad_raw, axis=0, keepdims=True)
    heads_ref[1:2] += jnp.sum(grad_rate * head_ref[1:2] * dt, axis=0, keepdims=True)


def back_inter(
    flag, payloads, x_raw, edge, xc, bc, step, cum, cols, dt_raw, dy, dx_in, left, dbc_in, entered, phi, state_in,
    taps, head, rowpack, spread, gather, sums,
):
    rows, width = xc.shape
    ns = bc.shape[1] // 2
    count = rows // CHUNK

    def back(i, *_):
        return (count - 1 - i, 0)

    def back3(i, *_):
        return (count - 1 - i, 0, 0)

    def before(i, *_):
        return (jnp.maximum((count - 1 - i) * (CHUNK // EDGE) - 1, 0), 0)

    def at(width_now):
        return (CHUNK, width_now)

    ins = [(p, p.shape, fixed) for p in payloads] + [
        (x_raw, at(width), back),
        (x_raw, (EDGE, width), before),
        (edge, (EDGE, width), fixed),
        (xc, at(width), back),
        (bc, at(2 * ns), back),
        (step, at(LANES), back),
        (cum, at(LANES), back),
        (cols, at(cols.shape[1]), back),
        (dt_raw, at(LANES), back),
        (dy, at(width), back),
        (dx_in, at(width), back),
        (left, at(LANES), back),
        (dbc_in, at(2 * ns), back),
        (entered, (1, ns, width), back3),
        (phi, (1, EDGE, LANES), back3),
        (state_in, state_in.shape, fixed),
        (taps, taps.shape, fixed),
        (head, head.shape, fixed),
        (rowpack, rowpack.shape, fixed),
        (spread, spread.shape, fixed),
        (gather, gather.shape, fixed),
        (sums, sums.shape, fixed),
    ]
    outs = [
        ((rows, width), BF16, at(width), back),
        ((EDGE, width), F32, (EDGE, width), fixed),
        ((EDGE, width), F32, (EDGE, width), fixed),
        ((rows, ns), BF16, at(ns), back),
        ((rows, ns), BF16, at(ns), back),
        ((rows, LANES), BF16, at(LANES), back),
        ((EDGE, width), F32, (EDGE, width), fixed),
        ((EDGE, LANES), F32, (EDGE, LANES), fixed),
        ((EDGE, width), F32, (EDGE, width), fixed),
    ]
    scratch = [
        pltpu.VMEM((ns, width), F32),
        pltpu.VMEM((3, EDGE, width), F32),
        pltpu.VMEM((3 * CHUNK + 2 * EDGE, width), F32),
        pltpu.VMEM((CHUNK, width), F32),
        pltpu.VMEM((CHUNK, width), BF16),
        pltpu.VMEM((CHUNK, width), BF16),
        pltpu.VMEM((ns, width), BF16),
        pltpu.VMEM((ns, width), BF16),
        pltpu.VMEM((2 * CHUNK + 2 * EDGE, width), BF16),
    ]
    return call(
        functools.partial(back_inter_body, len(payloads)), (count,), ins, outs, scratch, flag, name="back_inter"
    )


def back_bc_body(
    flag, raw_ref, edge_ref, cols_ref, taps_ref, mine_ref, theirs_ref, out_ref, last_ref, prior_ref, sums_ref
):
    size, width = raw_ref.shape
    same = same_columns(cols_ref[...], width)
    ext = jnp.concatenate([edge_ref[...].astype(F32), raw_ref[...].astype(F32)], axis=0)
    grad = mine_ref[...].astype(F32) + theirs_ref[...].astype(F32)
    zero = jnp.zeros((EDGE, width), F32)
    raw, _, sums = conv_back(ext, same, taps_ref[...], grad, [zero] * 3)
    out_ref[...] = raw[EDGE:].astype(BF16)
    last_ref[...] = raw[size:]
    prior_ref[...] = raw[:EDGE]
    sums_ref[...] = jnp.concatenate(sums + [zero[:3]], axis=0)


def back_bc(flag, raw, edge, cols, taps, mine, theirs):
    rows, ns = mine.shape
    before = edge.shape[1] // ns - 2
    ins = [
        (raw, (rows, ns), lambda i, t: (0, t[0])),
        (edge, (EDGE, ns), lambda i, t: (0, before + t[0])),
        (cols, cols.shape, fixed),
        (taps, (EDGE, ns), lambda i, t: (0, t[0])),
        (mine, mine.shape, fixed),
        (theirs, theirs.shape, fixed),
    ]
    outs = [((rows, ns), BF16, (rows, ns), fixed)]
    outs += [((EDGE, ns), F32, (EDGE, ns), fixed)] * 3
    return call(back_bc_body, (1,), ins, outs, (), flag, name="back_bc")


def back_low_body(flag, gate_ref, x_ref, bc_ref, dt_ref, wg_ref, wx_ref, wb_ref, wt_ref, out_ref):
    over = ((1,), (1,))
    total = dot(gate_ref[...], wg_ref[...], over) + dot(x_ref[...], wx_ref[...], over)
    total = total + dot(bc_ref[...], wb_ref[...], over) + dot(dt_ref[...], wt_ref[...], over)
    out_ref[...] = total.astype(BF16)


def back_low(flag, dgate, dx, dbc, ddt, weights):
    rows, width = dx.shape
    ns = dbc.shape[1]
    array, first = weights["lanes"]
    model = array.shape[0]
    block = min(256, rows)
    ins = [(v, (block, v.shape[1]), rows_at) for v in (dgate, dx, dbc, ddt)]
    ins += [
        block_of(weights["gate"]),
        block_of(weights["x"]),
        (array, (model, ns), lambda i, t: (0, first + t[0])),
        block_of((array, LANES, first + 2)),
    ]
    outs = [((rows, model), BF16, (block, model), rows_at)]
    return call(
        back_low_body, (rows // block,), ins, outs, (), flag, flops=2 * rows * model * (2 * width + 256), name="back_low"
    )[0]


def back_norm_body(up_ref, a_ref, b_ref, h_ref, gain_ref, out_ref, sum_ref):
    @pl.when(pl.program_id(0) == 0)
    def _():
        sum_ref[...] = jnp.zeros_like(sum_ref)

    hidden = h_ref[...].astype(F32)
    grad = a_ref[...].astype(F32) + b_ref[...].astype(F32)
    model = hidden.shape[1]
    norm = lax.rsqrt(jnp.mean(hidden * hidden, axis=1, keepdims=True) + EPSILON)
    normed = hidden * norm
    sum_ref[0:1] += jnp.sum(grad * normed, axis=0, keepdims=True)
    gained = grad * gain_ref[0:1]
    inner = jnp.sum(gained * normed, axis=1, keepdims=True) / model
    out_ref[...] = up_ref[...].astype(F32) + norm * (gained - normed * inner)


def back_norm(up, a, b, hidden, gain):
    rows, model = hidden.shape
    block = min(256, rows)
    wide = (block, model)
    ins = [(v, wide, rows_at) for v in (up, a, b, hidden)] + [(gain, gain.shape, fixed)]
    outs = [((rows, model), F32, wide, rows_at), ((EDGE, model), F32, (EDGE, model), fixed)]
    return call(back_norm_body, (rows // block,), ins, outs, name="back_norm")


def weight_grad_body(places, shards, cuts, owners, where, *refs):
    lefts, refs = refs[: max(owners) + 1], refs[max(owners) + 1 :]
    factors, outs, result = refs[: len(cuts)], refs[len(cuts) : len(cuts) + places], refs[len(cuts) + places]
    model = lefts[0].shape[0]
    rows = model // (places * shards)
    step = pl.program_id(0)
    for factor, owner, (start, end) in zip(factors, owners, cuts):

        @pl.when((step >= start) & (step < end))
        def _(factor=factor, owner=owner):
            made = dot(lefts[owner][...], factor[...])
            if places == 1:
                outs[0][...] = made.astype(BF16)
            else:
                result[...] = made

    if places == 1:
        return
    for k in range(places):
        for z in range(shards):
            start = pl.multiple_of((z * places + where[k]) * rows, rows)
            outs[k][z * rows : (z + 1) * rows] = result[pl.ds(start, rows)].astype(BF16)


def weight_grad(where, places, shards, products):
    model, rows = products[0][0].shape
    tile = 512 if places == 1 and all(b.shape[1] % 512 == 0 for _, factors in products for b in factors) else 256
    cuts, owners, ins, at = [], [], [], 0
    for i, (a, factors) in enumerate(products):
        ins.append((a, a.shape, fixed))
        for b in factors:
            cuts.append((at, at + b.shape[1] // tile))
            owners.append(i)
            at = cuts[-1][1]
    for b, (start, end) in zip([b for _, factors in products for b in factors], cuts):
        ins.append((b, (rows, tile), lambda i, *_, s=start, e=end: (0, jnp.clip(i - s, 0, e - s - 1))))
    width = at * tile
    part = model // places
    outs = [((part, width), BF16, (part, tile), columns_at)] * places
    scratch = [pltpu.VMEM((model, tile), F32)]
    return call(
        functools.partial(weight_grad_body, places, shards, cuts, owners), (at,), ins, outs, scratch, where,
        name="weight_grad",
    )


def relative(value, axis, by):
    size = lax.axis_size(axis)
    return lax.ppermute(value, axis, [(i, i ^ by) for i in range(size)])


def shifted(value, axis, by):
    size = lax.axis_size(axis)
    return lax.ppermute(value, axis, [(i, i + by) for i in range(size) if 0 <= i + by < size])


def tree_sum(values):
    while len(values) > 1:
        values = [a + b for a, b in zip(values[0::2], values[1::2])]
    return values[0]


def cut_body(joined, where, zx_ref, wbc_ref, wdt_ref, down_ref, *refs):
    width = zx_ref.shape[3]
    both, heads = wbc_ref.shape[2], wdt_ref.shape[2]
    rest, main, turned = refs[0], refs[1], refs[-1]
    other, at = (main, width) if joined else (refs[2], 0)
    rows = main.shape[0]
    main[:, :width] = zx_ref[0, :, 1]
    other[:, at : at + both] = wbc_ref[0]
    other[:, at + both :] = jnp.zeros((other.shape[0], LANES), BF16)
    other[:, at + both : at + both + heads] = wdt_ref[0]
    turned[...] = down_ref[0].astype(F32).T
    rest[:, :width] = zx_ref[0, :, 0]
    rest[:, width:] = turned[pl.ds(pl.multiple_of(where[0] * rows, rows), rows)].astype(BF16)


def cut_rows(layer, joined, place, rows, w_zx, w_bc, w_dt, w_out):
    local, _, width = w_zx.shape[1:]
    extra = w_bc.shape[2] + LANES
    taken = rows if joined else local
    ins = [(w_zx, (1, rows, 2, width), lambda i, c: (layer, c[0], 0, 0))]
    ins += [(v, (1, taken, v.shape[2]), lambda i, c: (layer, c[0] if joined else 0, 0)) for v in (w_bc, w_dt)]
    ins += [(w_out, (1,) + w_out.shape[1:], lambda i, c: (layer, 0, 0))]
    shapes = [(rows, 2 * width)] + ([(rows, width + extra)] if joined else [(rows, width), (local, extra)])
    outs = [(shape, BF16, shape, fixed) for shape in shapes]
    scratch = [pltpu.VMEM((local, width), F32)]
    return call(functools.partial(cut_body, joined), (1,), ins, outs, scratch, place, name="cut")


def gather_rows(piece):
    return lax.all_gather(piece, ("shard", "ctx"), axis=0, tiled=True)


def gather_shard(piece):
    return jnp.concatenate([piece] + [relative(piece, "shard", k) for k in range(1, lax.axis_size("shard"))], axis=0)


def gather_ctx(along):
    return [along] + [relative(along, "ctx", k) for k in range(1, lax.axis_size("ctx"))]


def gather_far(piece):
    return [piece] + [relative(piece, "shard", k) for k in range(1, lax.axis_size("shard"))]


def near_rows(pieces):
    return [pieces[0]] + [relative(p, "ctx", k) for k, p in enumerate(pieces) if k]


def split_sum_body(counts, where, *refs):
    arrays, outs = refs[: sum(counts)], refs[sum(counts) :]
    rows = outs[0].shape[0]
    for k, out in enumerate(outs):
        at = pl.ds(pl.multiple_of(where[k] * rows, rows), rows)
        done, column = 0, 0
        for count in counts:
            total = tree_sum([v[at].astype(F32) for v in arrays[done : done + count]])
            out[:, column : column + total.shape[1]] = total.astype(out.dtype)
            done, column = done + count, column + total.shape[1]


def split_sum(order, parts, groups):
    ins = [(v, v.shape, fixed) for group in groups for v in group]
    shape = (groups[0][0].shape[0] // parts, sum(group[0].shape[1] for group in groups))
    outs = [(shape, BF16 if k else F32, shape, fixed) for k in range(parts)]
    counts = [len(group) for group in groups]
    return call(functools.partial(split_sum_body, counts), (1,), ins, outs, (), order, name="split_sum")


def scattered(pieces, axis):
    return [pieces[0]] + [relative(pieces[k], axis, k) for k in range(1, len(pieces))]


def finish_body(counts, *refs):
    zx_ref, out_ref, small_ref = refs[-3:]
    layers, width = zx_ref.shape[0], zx_ref.shape[3]
    late = tree_sum([v[...].astype(F32) for v in refs[sum(counts) : -3]])
    span = late.shape[1] // layers
    for layer, count in enumerate(counts):
        early = tree_sum([v[...].astype(F32) for v in refs[:count]])
        refs = refs[count:]
        zx_ref[layer, :, 0] = early[:, :width]
        zx_ref[layer, :, 1] = late[:, layer * span : layer * span + width]
        out_ref[layer] = early[:, width:].T
        small_ref[layer] = late[:, layer * span + width : (layer + 1) * span]


def finish(early, late, width):
    layers = len(early)
    rows, span = late[0].shape
    ins = [(v, v.shape, fixed) for parts in list(early) + [late] for v in parts]
    shapes = [(layers, rows, 2, width), (layers, width, rows), (layers, rows, span // layers - width)]
    outs = [(v, F32, v, lambda *_, n=len(v): (0,) * n) for v in shapes]
    return call(functools.partial(finish_body, [len(parts) for parts in early]), (1,), ins, outs, name="finish")


def axis_sum(value, axis):
    return tree_sum([value] + [relative(value, axis, k) for k in range(1, lax.axis_size(axis))])


def around(value, by=1):
    size = lax.axis_size("shard")
    return lax.ppermute(value, "shard", [(i, (i + by) % size) for i in range(size)])


def neighbours(ended, sign):
    return [shifted(ended, "ctx", sign * d) for d in range(1, lax.axis_size("ctx"))]


def swap(value):
    return lax.ppermute(value, "tp", [(0, 1), (1, 0)])


def pad_rows(value):
    return jnp.pad(value, ((0, EDGE - value.shape[0]), (0, 0)))


def per_device(
    seq_in, w_zx, w_bc, w_dt, w_out, norm_gain, conv_x, conv_bc, head_params, gate_gain, segments, pad_mask, cotangent
):
    rows, model = seq_in.shape[1:]
    layers = w_zx.shape[0]
    width = w_zx.shape[3]
    heads = head_params.shape[2]
    ns = w_bc.shape[2] // 2
    shards, places = lax.axis_size("shard"), lax.axis_size("ctx")
    inner_total = width * lax.axis_size("tp")
    z, c, t = lax.axis_index("shard"), lax.axis_index("ctx"), lax.axis_index("tp")
    flag = t.astype(jnp.int32).reshape(1)
    chunks = rows // CHUNK

    ids = jnp.concatenate([jnp.full((3,), -1, jnp.int32), segments[0]])
    ext = lax.dynamic_slice_in_dim(ids, c * rows, rows + 3, 0)
    seg = ext[3:]
    mask = lax.dynamic_slice_in_dim(pad_mask[0], c * rows, rows, 0)
    firsts = ext[2 : 2 + rows].reshape(chunks, CHUNK)[:, :1]
    lasts = seg.reshape(chunks, CHUNK)[:, CHUNK - 1 :]
    by_chunk = seg.reshape(chunks, CHUNK)
    columns = [(ext[3 - lag : 3 - lag + rows] == seg) for lag in (1, 2, 3)]
    columns += [mask, (by_chunk == firsts).reshape(rows), (by_chunk == lasts).reshape(rows), mask, seg]
    cols = jnp.stack([v.astype(F32) for v in columns], axis=1)
    segs = jnp.broadcast_to(seg.astype(F32)[None], (EDGE, rows))

    head_of = jnp.arange(width)[None] // (width // heads)
    spread = (jnp.arange(2 * LANES)[:, None] % LANES == head_of).astype(BF16)
    gather = (head_of.T == jnp.arange(LANES)[None]).astype(BF16)
    at = jnp.arange(CHUNK)
    lower = (at[:, None] >= at[None]).astype(F32)
    sums = jnp.concatenate([(at[:, None] <= at[None]).astype(F32), (at[:, None] > at[None]).astype(F32)], axis=1)

    own_count = model // (shards * places)
    tie = lax.optimization_barrier
    place = c.astype(jnp.int32).reshape(1)
    crossed = jnp.concatenate([z ^ jnp.arange(shards), c ^ jnp.arange(places)]).astype(jnp.int32)

    rest_piece, x_piece, other_piece = cut_rows(0, False, place, own_count, w_zx, w_bc, w_dt, w_out)
    before = shifted(seq_in[0, rows - EDGE :], "ctx", 1)
    near, far = gather_ctx(gather_shard(x_piece)), gather_far(other_piece)
    extra = 2 * ns + LANES
    rest = gather_rows(rest_piece)
    weights = [dict(gate=(rest, width, 0), out=(rest, width, 1))]
    mains = [None]
    for layer in range(1, layers):
        rest_piece, main_piece = cut_rows(layer, True, place, own_count, w_zx, w_bc, w_dt, w_out)
        rest = gather_rows(rest_piece)
        weights.append(dict(gate=(rest, width, 0), out=(rest, width, 1)))
        mains.append(main_piece)

    hidden = seq_in[0]
    parts = None
    kept = []
    for layer in range(layers):
        gain_in = pad_rows(norm_gain[layer][None])
        taps = pad_rows(conv_x[layer])
        taps_bc = pad_rows(conv_bc[layer])
        decay = -jnp.exp(head_params[layer, 1])
        head = jnp.pad(
            jnp.stack([head_params[layer, 0], decay]), ((0, EDGE - 2), (0, LANES - heads))
        )
        skip = jnp.repeat(head_params[layer, 2], width // heads)
        rowpack = pad_rows(jnp.stack([gate_gain[layer], skip]))

        if layer > 0:
            p_tail, q_tail = parts[0][rows - EDGE :].astype(F32), parts[1][rows - EDGE :].astype(F32)
            squares = p_tail[:, model : model + 2] + q_tail[:, model : model + 2]
            scale = lax.rsqrt(jnp.sum(squares, axis=1, keepdims=True) / inner_total + EPSILON)
            tail = hidden[rows - EDGE :].astype(F32) + scale * (p_tail[:, :model] + q_tail[:, :model])
            before = shifted(tail, "ctx", 1)
        hidden, low, turned, x_raw, raw_bc, dt_raw, w_x, w_other = enter(
            crossed, shards, near, far, hidden, parts, gain_in, width, 2 * ns, inner_total
        )
        weights[layer].update(x=(w_x, width, 0), other=(w_other, extra, 0), lanes=(w_other, 0))
        more = layer + 1 < layers
        if more:
            main, dt_raw = tie((mains[layer + 1], dt_raw))
            coming = gather_shard(main)
        edge, xc, bc, step, cum, entered, phi, ended = states(
            x_raw, raw_bc, dt_raw, before, gain_in, weights[layer], cols, taps, taps_bc, head, spread, lower
        )
        y_in = within(xc, bc, step, cum, cols, segs, spread)
        given = neighbours(ended, 1)
        if more:
            given, coming, y_in = tie((given, coming, y_in))
            near, far = gather_ctx(coming), []
        ssm, gate, p_own, state_in = leave(
            given, y_in, low, xc, bc, cum, cols, entered, phi, rowpack, spread, weights[layer]
        )
        if more:
            p_own, near = tie((p_own, near))
        parts = (p_own, swap(p_own))
        kept.append(
            dict(
                hidden=hidden, turned=turned, x_raw=x_raw, raw_bc=raw_bc, dt_raw=dt_raw, edge=edge, gate=gate, xc=xc, bc=bc,
                step=step, cum=cum, entered=entered, phi=phi, ended=ended, state_in=state_in, ssm=ssm, parts=parts,
                gain_in=gain_in, taps=taps, taps_bc=taps_bc, head=head, rowpack=rowpack,
            )
        )
    direct = own_count % 16 == 0
    ctx_order = (c ^ jnp.arange(places)).astype(jnp.int32)
    ring_order = ((z - 1 - jnp.arange(shards)) % shards).astype(jnp.int32)
    shard_order = (z ^ jnp.arange(shards)).astype(jnp.int32)

    def owned(full):
        return lax.psum_scatter(full, ("shard", "ctx"), scatter_dimension=0, tiled=True)

    def add(a, b):
        return (a.astype(F32) + b.astype(F32)).astype(BF16)

    up = cotangent[0]
    smalls, early_sums, late_above = [], [], []
    for layer in reversed(range(layers)):
        k = kept[layer]
        last_layer = layer == layers - 1
        made = back_gate(
            up, k["parts"], k["ssm"], k["xc"], k["gate"], k["bc"], k["cum"], cols, k["phi"], k["ended"],
            k["rowpack"], spread, weights[layer], inner_total, k["hidden"] if last_layer else None,
        )
        if last_layer:
            output, made = made[0], made[1:]
        do, dy, dgate, normed, gain_rows, begun = made
        early_pair = [(k["turned"], [dgate]), (do, [normed])]
        later = neighbours(begun, -1)
        quick = direct and layer == 0
        if quick:
            early = weight_grad(ring_order, shards, 1, early_pair)
            dy, early = tie((dy, early))
            moving = around(early[0])
        else:
            early = weight_grad(ctx_order, 1, 1, early_pair)[0]
            dy, early = tie((dy, early))
        dx_in, left, dbc_in = back_within(
            k["xc"], k["bc"], k["step"], k["cum"], cols, segs, spread, gather, dy, k["ssm"]
        )
        if not quick:
            dx_in, later, early = tie((dx_in, later, early))
            g_early = owned(early)
        if quick and not last_layer:
            dx_in, early_sums[0] = tie((dx_in, early_sums[0]))
            later, rest_above = tie((later, rest_above))
            rest_above = near_rows(rest_above)
        edge = k["edge"]
        dx, last, prior, dbc_mine, dbc_theirs, ddt, conv_rows, head_rows, skip_rows = back_inter(
            flag, later, k["x_raw"], edge, k["xc"], k["bc"], k["step"], k["cum"], cols, k["dt_raw"], dy,
            dx_in, left, dbc_in, k["entered"], k["phi"], k["state_in"], k["taps"], k["head"], k["rowpack"],
            spread, gather, sums,
        )
        if quick:
            dx, moving = tie((dx, moving))
            moving = around(add(moving, early[1]))
            if not last_layer:
                dbc_theirs, late_above[0] = tie((dbc_theirs, rest_above))
        db, last_bc, prior_bc, conv_bc_rows = back_bc(
            flag, k["raw_bc"], edge, cols, k["taps_bc"], dbc_mine, swap(dbc_theirs)
        )
        back_rows = shifted(jnp.concatenate([prior, prior_bc], axis=1), "ctx", -1)
        dx = lax.dynamic_update_slice_in_dim(dx, (last + back_rows[:, :width]).astype(BF16), rows - EDGE, 0)
        db = lax.dynamic_update_slice_in_dim(db, (last_bc + back_rows[:, width:]).astype(BF16), rows - EDGE, 0)
        late_pair = [(k["turned"], [dx, jnp.concatenate([db, ddt], axis=1)])]
        if direct:
            rest = weight_grad(ctx_order, places, shards, late_pair)
            dgate, rest = tie((dgate, rest))
            if quick:
                rest = near_rows(rest)
        else:
            g_rest = owned(weight_grad(ctx_order, 1, 1, late_pair)[0])
        dlow = back_low(flag, dgate, dx, db, ddt, weights[layer])
        if quick:
            dlow, moving = tie((dlow, moving))
            for one in early[2:-1]:
                moving = around(add(moving, one))
            dlow, rest = tie((dlow, rest))
        up, norm_rows = back_norm(up, dlow, swap(dlow), k["hidden"], k["gain_in"])
        packed = jnp.concatenate(
            [norm_rows[0], conv_rows[:5].reshape(-1), gain_rows[0], skip_rows[0], conv_bc_rows[:5].reshape(-1),
             head_rows[:2].reshape(-1)]
        )
        smalls.insert(0, packed)
        if not direct:
            early_sums.insert(0, [g_early])
            late_above.insert(0, g_rest)
        elif not quick:
            rest_above = rest
            early_sums.insert(0, [g_early])
            late_above.insert(0, None)
        else:
            late_sum = scattered(split_sum(shard_order, shards, [rest] + late_above), "shard")
            partial = axis_sum(jnp.concatenate(smalls), "ctx")
            partial, moving, late_sum = tie((partial, moving, late_sum))
            early_sums.insert(0, scattered(split_sum(ctx_order, places, [[moving, early[-1]]]), "ctx"))
    if not direct:
        late_sum = [jnp.concatenate(late_above, axis=1)]
        partial = axis_sum(jnp.concatenate(smalls), "ctx")
    packed = axis_sum(partial, "shard").reshape(layers, -1)
    cuts = [model, 5 * width, width, width, 5 * ns, 2 * LANES]
    ends = [sum(cuts[: i + 1]) for i in range(len(cuts))]
    n_sum, cx_sum, gg_sum, sk_sum, cb_sum, hd_sum = jnp.split(packed, ends[:-1], axis=1)
    cb_mine = cb_sum.reshape(layers, 5, ns)
    grad_zx, grad_out, grad_small = finish(early_sums, late_sum, width)
    small_mine = grad_small[:, :, :ns]
    cb_other, small_other = swap(cb_mine), swap(small_mine)

    def ordered(own, other):
        first = jnp.where(t == 0, own, other)
        return jnp.concatenate([first, jnp.where(t == 0, other, own)], axis=-1)

    hd = hd_sum.reshape(layers, 2, LANES)[:, :, :heads]
    skip_sum = jnp.sum(sk_sum.reshape(layers, heads, width // heads), axis=-1)
    return (
        output[None],
        up[None],
        grad_zx,
        ordered(small_mine, small_other),
        grad_small[:, :, ns : ns + heads],
        grad_out,
        n_sum,
        cx_sum.reshape(layers, 5, width),
        ordered(cb_mine, cb_other),
        jnp.concatenate([hd, skip_sum[:, None]], axis=1),
        gg_sum,
    )


def solution(mesh):
    in_specs = (
        P("shard", "ctx", None),
        P(None, "shard", None, "tp"),
        P(None, "shard", None),
        P(None, "shard", "tp"),
        P(None, "tp", "shard"),
        P(),
        P(None, None, "tp"),
        P(),
        P(None, None, "tp"),
        P(None, "tp"),
        P("shard", None),
        P("shard", None),
        P("shard", "ctx", None),
    )
    out_specs = (
        P("shard", "ctx", None),
        P("shard", "ctx", None),
        P(None, ("shard", "ctx"), None, "tp"),
        P(None, ("shard", "ctx"), None),
        P(None, ("shard", "ctx"), "tp"),
        P(None, "tp", ("shard", "ctx")),
        P(),
        P(None, None, "tp"),
        P(),
        P(None, None, "tp"),
        P(None, "tp"),
    )
    return jax.shard_map(per_device, mesh=mesh, in_specs=in_specs, out_specs=out_specs, check_vma=False)
```

```python
import functools

import jax
import jax.numpy as jnp
from jax import lax
from jax.experimental import pallas as pl
from jax.experimental.pallas import tpu as pltpu
from jax.sharding import PartitionSpec as P

EPSILON = 1e-05
EXACT = lax.Precision.HIGHEST
F32 = jnp.float32
BF16 = jnp.bfloat16
CHUNK = 128
LANES = 128
EDGE = 8
CLOSED = -1e30
VMEM = 54 << 20


def dot(a, b, dims=((1,), (0,)), precision=None):
    return lax.dot_general(a, b, (dims, ((), ())), precision=precision, preferred_element_type=F32)


def split(values):
    high = values.astype(BF16)
    return high, (values - high.astype(F32)).astype(BF16)


def expand(values, spread):
    return dot(jnp.concatenate(split(values), axis=1), spread)


def folded(payloads):
    ns = payloads[0].shape[0] - EDGE
    total = payloads[-1][:ns].astype(F32)
    for one in reversed(payloads[:-1]):
        total = one[:ns].astype(F32) + one[ns : ns + 1].astype(F32) * total
    return total


def conv_shifts(ext, same):
    return [ext[EDGE:]] + [pltpu.roll(ext, lag, 0)[EDGE:] * same[lag] for lag in (1, 2, 3)]


def conv_sum(shifts, taps):
    total = taps[4:5] + taps[0:1] * shifts[0]
    for lag in (1, 2, 3):
        total = total + taps[lag : lag + 1] * shifts[lag]
    return total


def same_columns(cols, width):
    return [None] + [jnp.broadcast_to(cols[:, lag - 1 : lag], (cols.shape[0], width)) for lag in (1, 2, 3)]


def pair_masked(values):
    lane = lax.broadcasted_iota(jnp.int32, values.shape, 1)
    zero = jnp.zeros_like(values)
    first = lane < LANES // 2
    return jnp.concatenate([jnp.where(first, values, zero), jnp.where(first, zero, values)], axis=0)


def pairs_bias(seg_col, seg_row, later_rows):
    size = seg_col.shape[0]
    row = lax.broadcasted_iota(jnp.int32, (size, size), 0)
    col = lax.broadcasted_iota(jnp.int32, (size, size), 1)
    ordered = (row >= col) if later_rows else (row <= col)
    return jnp.where(ordered & (seg_col == seg_row), 0.0, CLOSED)


def chunks_of(ref):
    return [slice(at, at + CHUNK) for at in range(0, ref.shape[0], CHUNK)]


def silu_parts(values):
    sig = jax.nn.sigmoid(values)
    return sig, values * sig


def call(body, grid, ins, outs, scratch=(), scalars=None, flops=0, name=None):
    count = 0 if scalars is None else 1

    def adapt(block, fn):
        if block is None:
            return pl.BlockSpec(memory_space=pl.ANY)
        return pl.BlockSpec(block, fn)

    in_specs = [adapt(block, fn) for _, block, fn in ins]
    out_specs = [adapt(block, fn) for _, _, block, fn in outs]
    shapes = [jax.ShapeDtypeStruct(shape, dtype) for shape, dtype, _, _ in outs]
    moved = sum(a.size * a.dtype.itemsize for a, _, _ in ins) + sum(
        s.size * s.dtype.itemsize for s in shapes
    )
    made = pl.pallas_call(
        body,
        out_shape=shapes,
        grid_spec=pltpu.PrefetchScalarGridSpec(
            num_scalar_prefetch=count,
            grid=grid,
            in_specs=in_specs,
            out_specs=out_specs,
            scratch_shapes=list(scratch),
        ),
        compiler_params=pltpu.CompilerParams(
            vmem_limit_bytes=VMEM, dimension_semantics=("arbitrary",) * len(grid)
        ),
        cost_estimate=pl.CostEstimate(flops=1, bytes_accessed=1, transcendentals=0),
        name=name,
    )
    arrays = [a for a, _, _ in ins]
    return made(*(([scalars] if count else []) + arrays))


def rows_at(i, *_):
    return (i, 0)


def columns_at(i, *_):
    return (0, i)


def fixed(*_):
    return (0, 0)


def piece_copies(pieces, sems):
    copies = []
    for source, target, start in pieces:
        rows = source.shape[0]
        at = target.at[pl.ds(pl.multiple_of(start, rows), rows)]
        copies.append(pltpu.make_async_copy(source, at, sems.at[len(copies)]))
    for one in copies:
        one.start()
    for one in copies:
        one.wait()


def enter_body(first, inner_total, cuts, where, *refs):
    shards, places, rows = cuts
    near, refs = refs[:places], refs[places:]
    far, refs = (refs[:shards], refs[shards:]) if first else ((), refs)
    if first:
        h_ref, gain, u_ref, turned_ref, x_ref, bc_ref, dt_ref, w_x, w_other, sems = refs
        hidden = h_ref[...].astype(F32)
    else:
        h_ref, p_ref, q_ref, gain, h_out, u_ref, turned_ref, x_ref, bc_ref, dt_ref, w_x, w_other, sems = refs
        model = h_ref.shape[1]
        summed = p_ref[:, :model].astype(F32) + q_ref[:, :model].astype(F32)
        hidden = h_ref[...].astype(F32) + gated_scale(p_ref, q_ref, model, inner_total) * summed
        h_out[...] = hidden
    both = bc_ref.shape[1]
    width = x_ref.shape[1]

    @pl.when(pl.program_id(0) == 0)
    def _():
        pieces = [(v, w_other, where[z] * v.shape[0]) for z, v in enumerate(far)]
        for z in range(shards):
            for k in range(places):
                start = (where[z] * places + where[shards + k]) * rows
                source = near[k].at[pl.ds(z * rows, rows)]
                pieces.append((source.at[:, :width], w_x, start))
                if not far:
                    pieces.append((source.at[:, width:], w_other, start))
        piece_copies(pieces, sems)

    norm = lax.rsqrt(jnp.mean(hidden * hidden, axis=1, keepdims=True) + EPSILON)
    lowered = (hidden * norm * gain[0:1]).astype(BF16)
    u_ref[...] = lowered
    turned_ref[...] = lowered.T
    x_ref[...] = dot(lowered, w_x[...]).astype(BF16)
    made = dot(lowered, w_other[...])
    bc_ref[...] = made[:, :both].astype(BF16)
    dt_ref[...] = made[:, both:]


def gated_scale(p_ref, q_ref, model, inner_total):
    squares = p_ref[:, model:].astype(F32) + q_ref[:, model:].astype(F32)
    return lax.rsqrt((squares[:, 0:1] + squares[:, 1:2]) / inner_total + EPSILON)


def block_of(part):
    array, width, index = part
    return (array, (array.shape[0], width), lambda *_: (0, index))


def enter(where, shards, near, far, hidden, parts, gain, width, both, inner_total):
    rows, model = hidden.shape
    first = parts is None
    block = min(256, rows)
    wide = (block, model)
    ins = [(v, None, None) for v in near + far] + [(hidden, wide, rows_at)]
    outs = []
    if not first:
        ins += [(part, (block, model + LANES), rows_at) for part in parts]
        outs.append(((rows, model), F32, wide, rows_at))
    ins += [(gain, gain.shape, fixed)]
    outs += [
        ((rows, model), BF16, wide, rows_at),
        ((model, rows), BF16, (model, block), columns_at),
        ((rows, width), BF16, (block, width), rows_at),
        ((rows, both), BF16, (block, both), rows_at),
        ((rows, LANES), F32, (block, LANES), rows_at),
    ]
    outs += [((model, v), BF16, (model, v), fixed) for v in (width, both + LANES)]
    scratch = [pltpu.SemaphoreType.DMA((shards * (2 * len(near)),))]
    cuts = (shards, len(near), near[0].shape[0] // shards)
    made = call(
        functools.partial(enter_body, first, inner_total, cuts), (rows // block,), ins, outs, scratch, where, name="enter"
    )
    return [hidden] + list(made) if first else list(made)


def states_body(
    x_ref, raw_bc_ref, dt_ref, before_ref, gain_ref, w_x, w_other, cols_ref, taps_ref, taps_bc_ref, head_ref,
    spread_ref, lower_ref, edge_ref, before_turned, xc_ref, bc_ref, step_ref, cum_ref, enter_ref, phi_ref, last_ref,
    tail_x, tail_bc, state, phi,
):
    chunk = pl.program_id(0)
    width = x_ref.shape[1]
    ns = raw_bc_ref.shape[1] // 2

    @pl.when(chunk == 0)
    def _():
        before = before_ref[...].astype(F32)
        norm = lax.rsqrt(jnp.mean(before * before, axis=1, keepdims=True) + EPSILON)
        lowered = (before * norm * gain_ref[0:1]).astype(BF16)
        padding = jnp.zeros((LANES - EDGE, lowered.shape[1]), F32)
        before_turned[...] = jnp.concatenate([lowered.astype(F32), padding], axis=0).T.astype(BF16)
        edge = dot(lowered, w_x[...]).astype(BF16)
        edge_bc = dot(lowered, w_other[:, : 2 * ns]).astype(BF16)
        edge_ref[:, :width] = edge
        edge_ref[:, width:] = edge_bc
        tail_x[...] = edge.astype(F32)
        tail_bc[...] = edge_bc.astype(F32)
        state[...] = jnp.zeros_like(state)
        phi[...] = jnp.ones_like(phi)

    for sub, here in enumerate(chunks_of(x_ref)):
        cols = cols_ref[here]
        same = same_columns(cols, LANES)
        dt = jax.nn.softplus(dt_ref[here] + head_ref[0:1]) * cols[:, 3:4]
        rates = head_ref[1:2] * dt
        cum = dot(lower_ref[...], rates, precision=EXACT)
        step_ref[here] = dt
        cum_ref[here] = cum
        size = cum.shape[0]
        tail_dt = cols[:, 5:6] * jnp.exp(cum[size - 1 : size] - cum) * dt
        fold = cols[size - 1 : size, 4:5] * jnp.exp(cum[size - EDGE : size])[EDGE - 1 : EDGE]
        fold_rows = jnp.broadcast_to(fold, phi.shape)
        wide = expand(jnp.concatenate([tail_dt, fold_rows], axis=0), spread_ref[...])

        halves = []
        for i in range(2):
            part = slice(i * ns, (i + 1) * ns)
            now = raw_bc_ref[here, part].astype(F32)
            shifts = conv_shifts(jnp.concatenate([tail_bc[:, part], now], axis=0), same)
            tail_bc[:, part] = now[size - EDGE :]
            halves.append(silu_parts(conv_sum(shifts, taps_bc_ref[:, part]))[1].astype(BF16))
            bc_ref[here, part] = halves[i]
        b_turned = halves[0].astype(F32).T.astype(BF16)

        enter_ref[sub] = state[...].astype(BF16)
        phi_ref[sub] = phi[...]
        for i in range(width // LANES):
            part = slice(i * LANES, (i + 1) * LANES)
            now = x_ref[here, part].astype(F32)
            shifts = conv_shifts(jnp.concatenate([tail_x[:, part], now], axis=0), same)
            tail_x[:, part] = now[size - EDGE :]
            x_conv = silu_parts(conv_sum(shifts, taps_ref[:, part]))[1].astype(BF16)
            xc_ref[here, part] = x_conv
            held = (x_conv.astype(F32) * wide[:size, part]).astype(BF16)
            state[:, part] = wide[size : size + 1, part] * state[:, part] + dot(b_turned, held)
        phi[...] = phi[...] * fold_rows

    @pl.when(chunk == pl.num_programs(0) - 1)
    def _():
        last_ref[:ns] = state[...].astype(BF16)
        last_ref[ns:] = expand(phi[...], spread_ref[...]).astype(BF16)


def states(x_raw, raw_bc, dt_raw, before, gain, weights, cols, taps, taps_bc, head, spread, lower):
    rows, width = x_raw.shape
    ns = raw_bc.shape[1] // 2
    count = rows // CHUNK
    block = min(256, rows)
    subs = block // CHUNK
    ins = [
        (x_raw, (block, width), rows_at),
        (raw_bc, (block, 2 * ns), rows_at),
        (dt_raw, (block, LANES), rows_at),
        (before, before.shape, fixed),
        (gain, gain.shape, fixed),
        block_of(weights["x"]),
        block_of(weights["other"]),
        (cols, (block, cols.shape[1]), rows_at),
        (taps, taps.shape, fixed),
        (taps_bc, taps_bc.shape, fixed),
        (head, head.shape, fixed),
        (spread, spread.shape, fixed),
        (lower, lower.shape, fixed),
    ]
    outs = [
        ((EDGE, width + 2 * ns), BF16, (EDGE, width + 2 * ns), fixed),
        ((before.shape[1], LANES), BF16, (before.shape[1], LANES), fixed),
        ((rows, width), BF16, (block, width), rows_at),
        ((rows, 2 * ns), BF16, (block, 2 * ns), rows_at),
        ((rows, LANES), F32, (block, LANES), rows_at),
        ((rows, LANES), F32, (block, LANES), rows_at),
        ((count, ns, width), BF16, (subs, ns, width), lambda i, *_: (i, 0, 0)),
        ((count, EDGE, LANES), F32, (subs, EDGE, LANES), lambda i, *_: (i, 0, 0)),
        ((ns + EDGE, width), BF16, (ns + EDGE, width), fixed),
    ]
    scratch = [
        pltpu.VMEM((EDGE, width), F32),
        pltpu.VMEM((EDGE, 2 * ns), F32),
        pltpu.VMEM((ns, width), F32),
        pltpu.VMEM((EDGE, LANES), F32),
    ]
    return call(states_body, (rows // block,), ins, outs, scratch, flops=2 * rows * width * ns * 4, name="states")


def within_body(xc_ref, bc_ref, step_ref, cum_ref, cols_ref, segs_ref, spread_ref, y_ref):
    ns = bc_ref.shape[1] // 2
    width = xc_ref.shape[1]
    for here in chunks_of(y_ref):
        cum = cum_ref[here]
        cum_rows = cum.T
        bias = pairs_bias(cols_ref[here, 7:8], segs_ref[0:1, here], True)
        both = dot(bc_ref[here, ns:], bc_ref[here, :ns], ((1,), (1,)))
        step_wide = expand(step_ref[here], spread_ref[...])
        for pair in range(width // LANES):
            part = slice(pair * LANES, (pair + 1) * LANES)
            weighted = (xc_ref[here, part].astype(F32) * step_wide[:, part]).astype(BF16)
            maps = []
            for head in (2 * pair, 2 * pair + 1):
                gap = (cum[:, head : head + 1] - cum_rows[head : head + 1]) + bias
                maps.append((jnp.exp(gap) * both).astype(BF16))
            y_ref[here, part] = dot(jnp.concatenate(maps, axis=1), pair_masked(weighted))


def within(xc, bc, step, cum, cols, segs, spread):
    rows, width = xc.shape
    block = min(512, rows)
    ins = [
        (xc, (block, width), rows_at),
        (bc, (block, bc.shape[1]), rows_at),
        (step, (block, LANES), rows_at),
        (cum, (block, LANES), rows_at),
        (cols, (block, cols.shape[1]), rows_at),
        (segs, (EDGE, block), columns_at),
        (spread, spread.shape, fixed),
    ]
    outs = [((rows, width), F32, (block, width), rows_at)]
    return call(within_body, (rows // block,), ins, outs, name="within")[0]


def leave_body(count, *refs):
    payloads, refs = refs[:count], refs[count:]
    (w_gate, w_out, y_ref, low_ref, xc_ref, bc_ref, cum_ref, cols_ref, enter_ref, phi_ref, rows_ref, spread_ref) = refs[:12]
    ssm_ref, gate_ref, p_ref, in_ref, normed = refs[12:]
    ns = in_ref.shape[0]
    width = xc_ref.shape[1]
    spread = spread_ref[...]

    @pl.when(pl.program_id(0) == 0)
    def _():
        in_ref[...] = folded([p[...] for p in payloads])

    gate_ref[...] = dot(low_ref[...], w_gate[...])
    for sub in range(y_ref.shape[0] // CHUNK):
        here = slice(sub * CHUNK, (sub + 1) * CHUNK)
        phi_wide = expand(phi_ref[sub], spread)[0:1]
        begun = (enter_ref[sub].astype(F32) + phi_wide * in_ref[...]).astype(BF16)
        carried = cols_ref[here, 4:5] * jnp.exp(cum_ref[here])
        carried_wide = expand(carried, spread)
        far = dot(bc_ref[here, ns:], begun)
        ssm_ref[here] = y_ref[here] + carried_wide * far
    total = jnp.zeros((y_ref.shape[0], LANES), F32)
    for i in range(width // LANES):
        part = slice(i * LANES, (i + 1) * LANES)
        mixed = ssm_ref[:, part] + rows_ref[1:2, part] * xc_ref[:, part].astype(F32)
        gated = mixed * silu_parts(gate_ref[:, part])[1]
        total = total + gated * gated
        normed[:, part] = (gated * rows_ref[0:1, part]).astype(BF16)
    high, rest = split(jnp.broadcast_to(jnp.sum(total, axis=1, keepdims=True), total.shape))
    lane = lax.broadcasted_iota(jnp.int32, total.shape, 1)
    model = w_out.shape[0]
    p_ref[:, :model] = dot(normed[...], w_out[...], ((1,), (1,))).astype(BF16)
    p_ref[:, model:] = jnp.where(lane == 0, high.astype(F32), rest.astype(F32)).astype(BF16)


def leave(payloads, y_in, low, xc, bc, cum, cols, entered, phi, rowpack, spread, weights):
    rows, width = xc.shape
    model = low.shape[1]
    ns = bc.shape[1] // 2
    block = min(256, rows)
    subs = block // CHUNK
    ins = [(p, p.shape, fixed) for p in payloads]
    ins += [
        block_of(weights["gate"]),
        block_of(weights["out"]),
        (y_in, (block, width), rows_at),
        (low, (block, model), rows_at),
        (xc, (block, width), rows_at),
        (bc, (block, bc.shape[1]), rows_at),
        (cum, (block, LANES), rows_at),
        (cols, (block, cols.shape[1]), rows_at),
        (entered, (subs, ns, width), lambda i, *_: (i, 0, 0)),
        (phi, (subs, EDGE, LANES), lambda i, *_: (i, 0, 0)),
        (rowpack, rowpack.shape, fixed),
        (spread, spread.shape, fixed),
    ]
    outs = [
        ((rows, width), F32, (block, width), rows_at),
        ((rows, width), F32, (block, width), rows_at),
        ((rows, model + LANES), BF16, (block, model + LANES), rows_at),
        ((ns, width), F32, (ns, width), fixed),
    ]
    scratch = [pltpu.VMEM((block, width), BF16)]
    return call(functools.partial(leave_body, len(payloads)), (rows // block,), ins, outs, scratch, name="leave")


def back_gate_body(
    inner_total, ends, *refs
):
    if ends:
        hidden_ref, refs = refs[0], refs[1:]
        output_ref, refs = refs[14], refs[:14] + refs[15:]
    (
        up_ref, p_ref, q_ref, ssm_ref, xc_ref, gate_ref, bc_ref, cum_ref, cols_ref, phi_ref,
        factor_ref, rows_ref, spread_ref, w_ref,
        do_ref, dy_ref, dgate_ref, n_ref, gain_ref, out_ref, state,
    ) = refs
    step = pl.program_id(0)
    ns = state.shape[0]
    width = xc_ref.shape[1]
    spread = spread_ref[...]

    @pl.when(step == 0)
    def _():
        gain_ref[...] = jnp.zeros_like(gain_ref)
        state[...] = jnp.zeros_like(state)

    model = up_ref.shape[1]
    scale = gated_scale(p_ref, q_ref, model, inner_total)
    up = up_ref[...].astype(BF16)
    do_ref[...] = up.T
    summed = p_ref[:, :model].astype(F32) + q_ref[:, :model].astype(F32)
    if ends:
        output_ref[...] = hidden_ref[...].astype(F32) + scale * summed
    spread_sum = jnp.sum(up.astype(F32) * summed, axis=1, keepdims=True)
    pull = scale * scale * scale * spread_sum / inner_total
    scale_wide = jnp.broadcast_to(scale, (scale.shape[0], LANES))
    pull_wide = jnp.broadcast_to(pull, scale_wide.shape)
    back = dot(up, w_ref[...])
    for i in range(width // LANES):
        part = slice(i * LANES, (i + 1) * LANES)
        gain = rows_ref[0:1, part]
        gate = gate_ref[:, part]
        sig, soft = silu_parts(gate)
        mixed = ssm_ref[:, part] + rows_ref[1:2, part] * xc_ref[:, part].astype(F32)
        gated = mixed * soft
        scaled = gated * scale_wide
        grad = back[:, part]
        gain_ref[6:7, part] += jnp.sum(grad * scaled, axis=0, keepdims=True)
        grad_gated = grad * gain * scale_wide - gated * pull_wide
        dy_ref[:, part] = (grad_gated * soft).astype(BF16)
        dgate_ref[:, part] = (grad_gated * mixed * (sig * (1.0 + gate * (1.0 - sig)))).astype(BF16)
        n_ref[:, part] = (scaled * gain).astype(BF16)
    for sub in range(up_ref.shape[0] // CHUNK):
        here = slice(sub * CHUNK, (sub + 1) * CHUNK)
        phi_wide = expand(phi_ref[sub], spread)[0:1]
        carried_wide = expand(cols_ref[here, 4:5] * jnp.exp(cum_ref[here]), spread)
        c_turned = bc_ref[here, ns:].astype(F32).T.astype(BF16)
        carried_dy = (dy_ref[here].astype(F32) * carried_wide).astype(BF16)
        state[...] += phi_wide * dot(c_turned, carried_dy)

    @pl.when(step == pl.num_programs(0) - 1)
    def _():
        out_ref[:ns] = state[...].astype(BF16)
        out_ref[ns:] = factor_ref[...]


def back_gate(up, parts, ssm, xc, gate, bc, cum, cols, phi, ended, rowpack, spread, weights, inner_total, hidden=None):
    rows, width = xc.shape
    model = up.shape[1]
    ns = bc.shape[1] // 2
    block = min(256, rows)
    subs = block // CHUNK
    wide = (block, model)
    ins = [
        (up, wide, rows_at),
        (parts[0], (block, model + LANES), rows_at),
        (parts[1], (block, model + LANES), rows_at),
        (ssm, (block, width), rows_at),
        (xc, (block, width), rows_at),
        (gate, (block, width), rows_at),
        (bc, (block, 2 * ns), rows_at),
        (cum, (block, LANES), rows_at),
        (cols, (block, cols.shape[1]), rows_at),
        (phi, (subs, EDGE, LANES), lambda i, *_: (i, 0, 0)),
        (ended, (EDGE, width), lambda i, *_: (ns // EDGE, 0)),
        (rowpack, rowpack.shape, fixed),
        (spread, spread.shape, fixed),
        block_of(weights["out"]),
    ]
    outs = [
        ((model, rows), BF16, (model, block), columns_at),
        ((rows, width), BF16, (block, width), rows_at),
        ((rows, width), BF16, (block, width), rows_at),
        ((rows, width), BF16, (block, width), rows_at),
        ((EDGE, width), F32, (EDGE, width), fixed),
        ((ns + EDGE, width), BF16, (ns + EDGE, width), fixed),
    ]
    if hidden is not None:
        ins = [(hidden, wide, rows_at)] + ins
        outs = [((rows, model), F32, wide, rows_at)] + outs
    scratch = [pltpu.VMEM((ns, width), F32)]
    return call(
        functools.partial(back_gate_body, inner_total, hidden is not None), (rows // block,), ins, outs, scratch,
        flops=2 * rows * width * model * 1.3, name="back_gate",
    )


def back_within_body(
    xc_ref, bc_ref, step_ref, cum_ref, cols_ref, segs_ref, spread_ref, gather_ref, dy_ref, ssm_ref,
    dx_ref, left_ref, dbc_ref, products,
):
    ns = bc_ref.shape[1] // 2
    size, width = CHUNK, xc_ref.shape[1]
    for here in chunks_of(xc_ref):
        cum = cum_ref[here]
        cum_rows = cum.T
        bias = pairs_bias(cols_ref[here, 7:8], segs_ref[0:1, here], False)
        b_part = bc_ref[here, :ns]
        c_part = bc_ref[here, ns:]
        both = dot(b_part, c_part, ((1,), (1,)))
        step_wide = expand(step_ref[here], spread_ref[...])
        grad_both = jnp.zeros((size, size), F32)
        for pair in range(width // LANES):
            part = slice(pair * LANES, (pair + 1) * LANES)
            weighted = (xc_ref[here, part].astype(F32) * step_wide[:, part]).astype(BF16)
            dy = dy_ref[here, part]
            dy_pair = pair_masked(dy)
            grad_maps = dot(weighted, dy_pair, ((1,), (1,)))
            maps = []
            for k in (0, 1):
                head = 2 * pair + k
                decay = jnp.exp((cum_rows[head : head + 1] - cum[:, head : head + 1]) + bias)
                maps.append((decay * both).astype(BF16))
                grad_both = grad_both + decay * grad_maps[:, k * size : (k + 1) * size]
            grad_x = dot(jnp.concatenate(maps, axis=1), dy_pair)
            dx_ref[here, part] = grad_x.astype(BF16)
            high, rest = split(dy.astype(F32) * ssm_ref[here, part] - weighted.astype(F32) * grad_x)
            products[:size, part] = high
            products[size:, part] = rest
        left = dot(products[...], gather_ref[...])
        left_ref[here] = left[:size] + left[size:]
        dbc_ref[here, :ns] = dot(grad_both.astype(BF16), c_part)
        dbc_ref[here, ns:] = dot(grad_both.T.astype(BF16), b_part)


def back_within(xc, bc, step, cum, cols, segs, spread, gather, dy, ssm):
    rows, width = xc.shape
    block = min(256, rows)
    ins = [
        (xc, (block, width), rows_at),
        (bc, (block, bc.shape[1]), rows_at),
        (step, (block, LANES), rows_at),
        (cum, (block, LANES), rows_at),
        (cols, (block, cols.shape[1]), rows_at),
        (segs, (EDGE, block), columns_at),
        (spread, spread.shape, fixed),
        (gather, gather.shape, fixed),
        (dy, (block, width), rows_at),
        (ssm, (block, width), rows_at),
    ]
    outs = [
        ((rows, width), BF16, (block, width), rows_at),
        ((rows, LANES), F32, (block, LANES), rows_at),
        ((rows, bc.shape[1]), F32, (block, bc.shape[1]), rows_at),
    ]
    scratch = [pltpu.VMEM((2 * CHUNK, width), BF16)]
    return call(back_within_body, (rows // block,), ins, outs, scratch, name="back_within")


def conv_back(ext, same, taps, grad_conv, next_rows):
    size = ext.shape[0] - EDGE
    shifts = conv_shifts(ext, same)
    pre = conv_sum(shifts, taps)
    sig = jax.nn.sigmoid(pre)
    grad_pre = grad_conv * (sig * (1.0 + pre * (1.0 - sig)))
    sums = [jnp.sum(grad_pre * shifts[lag], axis=0, keepdims=True) for lag in range(4)]
    sums.append(jnp.sum(grad_pre, axis=0, keepdims=True))
    zero = jnp.zeros((EDGE, ext.shape[1]), F32)
    length = size + 2 * EDGE
    raw = taps[0:1] * jnp.concatenate([zero, grad_pre], axis=0)
    firsts = []
    for lag in (1, 2, 3):
        term = grad_pre * same[lag] * taps[lag : lag + 1]
        firsts.append(term[:EDGE])
        padded = jnp.concatenate([zero, term, next_rows[lag - 1]], axis=0)
        raw = raw + pltpu.roll(padded, length - lag, 0)[: size + EDGE]
    return raw, firsts, sums


def back_inter_body(count_in, flag, *refs):
    payloads, refs = refs[:count_in], refs[count_in:]
    (
        x_ref, before_ref, edge_ref, xc_ref, bc_ref, step_ref, cum_ref, cols_ref, dt_ref, dy_ref, dxi_ref,
        left_ref, dbci_ref, enter_ref, phi_ref, in_ref, taps_ref, head_ref, rows_ref, spread_ref, gather_ref, sums_ref,
        dx_ref, last_ref, prior_ref, mine_ref, theirs_ref, ddt_ref, conv_ref, heads_ref,
        grad_state, next_rows, wide, far, carried, held, begun, ending, products,
    ) = refs
    step = pl.program_id(0)
    first_block = step == pl.num_programs(0) - 1
    ns = in_ref.shape[0]
    size, width = CHUNK, xc_ref.shape[1]

    @pl.when(step == 0)
    def _():
        grad_state[...] = folded([p[...] for p in payloads])
        next_rows[...] = jnp.zeros_like(next_rows)
        conv_ref[...] = jnp.zeros_like(conv_ref)
        heads_ref[...] = jnp.zeros_like(heads_ref)

    subs = len(chunks_of(xc_ref))
    for sub, here in reversed(list(enumerate(chunks_of(xc_ref)))):
        cols = cols_ref[here]
        same = same_columns(cols, LANES)
        cum = cum_ref[here]
        dt = step_ref[here]
        decay_in = cols[:, 4:5] * jnp.exp(cum)
        decay_out = cols[:, 5:6] * jnp.exp(cum[size - 1 : size] - cum)
        fold_rows = jnp.broadcast_to(decay_in[size - EDGE : size][EDGE - 1 : EDGE], (EDGE, LANES))
        b_part = bc_ref[here, :ns]
        c_part = bc_ref[here, ns:]
        c_turned = c_part.astype(F32).T.astype(BF16)
        stacked = jnp.concatenate([decay_in, decay_out, dt, fold_rows, phi_ref[sub]], axis=0)
        wide[...] = expand(stacked, spread_ref[...])
        fold_at = 3 * size
        for i in range(width // LANES):
            part = slice(i * LANES, (i + 1) * LANES)
            dy = dy_ref[here, part].astype(F32)
            weighted = xc_ref[here, part].astype(F32) * wide[2 * size : 3 * size, part]
            fold_wide = wide[fold_at : fold_at + 1, part]
            grad_end = grad_state[:, part]
            start = enter_ref[sub, :, part].astype(F32) + wide[fold_at + EDGE : fold_at + EDGE + 1, part] * in_ref[:, part]
            carried[:, part] = (dy * wide[:size, part]).astype(BF16)
            held[:, part] = (weighted * wide[size : 2 * size, part]).astype(BF16)
            begun[:, part] = start.astype(BF16)
            ending[:, part] = grad_end.astype(BF16)
            pass_sum = jnp.sum(start * grad_end, axis=0, keepdims=True) * fold_wide
            products[2 * size :, part] = jnp.broadcast_to(pass_sum, (2 * EDGE, LANES)).astype(BF16)
            grad_state[:, part] = fold_wide * grad_end
        far[...] = dot(b_part, ending[...])
        dbc_c = dbci_ref[here, ns:] + dot(carried[...], begun[...], ((1,), (1,)))
        dbc_b = dbci_ref[here, :ns] + dot(held[...], ending[...], ((1,), (1,)))
        grad_state[...] += dot(c_turned, carried[...])
        own_b = flag[0] == 0
        mine_ref[here] = jnp.where(own_b, dbc_b, dbc_c).astype(BF16)
        theirs_ref[here] = jnp.where(own_b, dbc_c, dbc_b).astype(BF16)

        for i in range(width // LANES):
            part = slice(i * LANES, (i + 1) * LANES)
            dy = dy_ref[here, part].astype(F32)
            x_conv = xc_ref[here, part].astype(F32)
            dt_wide = wide[2 * size : 3 * size, part]
            grad_far = wide[size : 2 * size, part] * far[:, part]
            grad_weighted = dxi_ref[here, part].astype(F32) + grad_far
            products[:size, part] = (x_conv * dt_wide * grad_far).astype(BF16)
            products[size : 2 * size, part] = (x_conv * grad_weighted).astype(BF16)
            conv_ref[5:6, part] += jnp.sum(dy * x_conv, axis=0, keepdims=True)
            grad_conv = dt_wide * grad_weighted + rows_ref[1:2, part] * dy
            if sub:
                ahead = x_ref[here.start - EDGE : here.start, part].astype(F32)
            else:
                ahead = jnp.where(first_block, edge_ref[:, part].astype(F32), before_ref[:, part].astype(F32))
            ext = jnp.concatenate([ahead, x_ref[here, part].astype(F32)], axis=0)
            raw, firsts, tap_sums = conv_back(
                ext, same, taps_ref[:, part], grad_conv, [next_rows[k, :, part] for k in range(3)]
            )
            for k in range(3):
                next_rows[k, :, part] = firsts[k]
            for k in range(5):
                conv_ref[k : k + 1, part] += tap_sums[k]
            dx_ref[here, part] = raw[EDGE:].astype(BF16)
            prior_ref[:, part] = raw[:EDGE]

            if sub == subs - 1:

                @pl.when(step == 0)
                def _(raw=raw, part=part):
                    last_ref[:, part] = raw[size:]

        per_head = dot(products[...], gather_ref[...])
        outward, direct, through = per_head[:size], per_head[size : 2 * size], per_head[2 * size : 2 * size + 1]
        grad_rate = dot(sums_ref[...], jnp.concatenate([left_ref[here], outward], axis=0), precision=EXACT) + through
        grad_dt = direct + head_ref[1:2] * grad_rate
        grad_raw = grad_dt * cols[:, 3:4] * jax.nn.sigmoid(dt_ref[here] + head_ref[0:1])
        ddt_ref[here] = grad_raw.astype(BF16)
        heads_ref[0:1] += jnp.sum(grad_raw, axis=0, keepdims=True)
        heads_ref[1:2] += jnp.sum(grad_rate * head_ref[1:2] * dt, axis=0, keepdims=True)


def back_inter(
    flag, payloads, x_raw, edge, xc, bc, step, cum, cols, dt_raw, dy, dx_in, left, dbc_in, entered, phi, state_in,
    taps, head, rowpack, spread, gather, sums,
):
    rows, width = xc.shape
    ns = bc.shape[1] // 2
    block = min(256, rows)
    subs = block // CHUNK
    count = rows // block

    def back(i, *_):
        return (count - 1 - i, 0)

    def back3(i, *_):
        return (count - 1 - i, 0, 0)

    def before(i, *_):
        return (jnp.maximum((count - 1 - i) * (block // EDGE) - 1, 0), 0)

    def at(width_now):
        return (block, width_now)

    ins = [(p, p.shape, fixed) for p in payloads] + [
        (x_raw, at(width), back),
        (x_raw, (EDGE, width), before),
        (edge, (EDGE, width), fixed),
        (xc, at(width), back),
        (bc, at(2 * ns), back),
        (step, at(LANES), back),
        (cum, at(LANES), back),
        (cols, at(cols.shape[1]), back),
        (dt_raw, at(LANES), back),
        (dy, at(width), back),
        (dx_in, at(width), back),
        (left, at(LANES), back),
        (dbc_in, at(2 * ns), back),
        (entered, (subs, ns, width), back3),
        (phi, (subs, EDGE, LANES), back3),
        (state_in, state_in.shape, fixed),
        (taps, taps.shape, fixed),
        (head, head.shape, fixed),
        (rowpack, rowpack.shape, fixed),
        (spread, spread.shape, fixed),
        (gather, gather.shape, fixed),
        (sums, sums.shape, fixed),
    ]
    outs = [
        ((rows, width), BF16, at(width), back),
        ((EDGE, width), F32, (EDGE, width), fixed),
        ((EDGE, width), F32, (EDGE, width), fixed),
        ((rows, ns), BF16, at(ns), back),
        ((rows, ns), BF16, at(ns), back),
        ((rows, LANES), BF16, at(LANES), back),
        ((EDGE, width), F32, (EDGE, width), fixed),
        ((EDGE, LANES), F32, (EDGE, LANES), fixed),
    ]
    scratch = [
        pltpu.VMEM((ns, width), F32),
        pltpu.VMEM((3, EDGE, width), F32),
        pltpu.VMEM((3 * CHUNK + 2 * EDGE, width), F32),
        pltpu.VMEM((CHUNK, width), F32),
        pltpu.VMEM((CHUNK, width), BF16),
        pltpu.VMEM((CHUNK, width), BF16),
        pltpu.VMEM((ns, width), BF16),
        pltpu.VMEM((ns, width), BF16),
        pltpu.VMEM((2 * CHUNK + 2 * EDGE, width), BF16),
    ]
    return call(
        functools.partial(back_inter_body, len(payloads)), (count,), ins, outs, scratch, flag, name="back_inter"
    )


def back_bc_body(
    flag, raw_ref, edge_ref, cols_ref, taps_ref, mine_ref, theirs_ref, out_ref, last_ref, prior_ref, sums_ref
):
    size, width = raw_ref.shape
    same = same_columns(cols_ref[...], width)
    ext = jnp.concatenate([edge_ref[...].astype(F32), raw_ref[...].astype(F32)], axis=0)
    grad = mine_ref[...].astype(F32) + theirs_ref[...].astype(F32)
    zero = jnp.zeros((EDGE, width), F32)
    raw, _, sums = conv_back(ext, same, taps_ref[...], grad, [zero] * 3)
    out_ref[...] = raw[EDGE:].astype(BF16)
    last_ref[...] = raw[size:]
    prior_ref[...] = raw[:EDGE]
    sums_ref[...] = jnp.concatenate(sums + [zero[:3]], axis=0)


def back_bc(flag, raw, edge, cols, taps, mine, theirs):
    rows, ns = mine.shape
    before = edge.shape[1] // ns - 2
    ins = [
        (raw, (rows, ns), lambda i, t: (0, t[0])),
        (edge, (EDGE, ns), lambda i, t: (0, before + t[0])),
        (cols, cols.shape, fixed),
        (taps, (EDGE, ns), lambda i, t: (0, t[0])),
        (mine, mine.shape, fixed),
        (theirs, theirs.shape, fixed),
    ]
    outs = [((rows, ns), BF16, (rows, ns), fixed)]
    outs += [((EDGE, ns), F32, (EDGE, ns), fixed)] * 3
    return call(back_bc_body, (1,), ins, outs, (), flag, name="back_bc")


def back_low_body(
    flag, gate_ref, x_ref, bc_ref, dt_ref, last_x, last_bc, back_ref, wg_ref, wx_ref, wb_ref, wt_ref, out_ref
):
    def product(gate, x, bc, dt):
        over = ((1,), (1,))
        total = dot(gate, wg_ref[...], over) + dot(x, wx_ref[...], over)
        return (total + dot(bc, wb_ref[...], over) + dot(dt, wt_ref[...], over)).astype(BF16)

    out_ref[...] = product(gate_ref[...], x_ref[...], bc_ref[...], dt_ref[...])

    @pl.when(pl.program_id(0) == pl.num_programs(0) - 1)
    def _():
        size, width = x_ref.shape
        end = slice(size - 2 * EDGE, size)

        def righted(ref, last, back):
            kept = ref[end].astype(F32)[:EDGE]
            return jnp.concatenate([kept, last[...] + back], axis=0).astype(BF16)

        x = righted(x_ref, last_x, back_ref[:, :width])
        bc = righted(bc_ref, last_bc, back_ref[:, width:])
        out_ref[end] = product(gate_ref[end], x, bc, dt_ref[end])


def back_low(flag, dgate, dx, dbc, ddt, last_x, last_bc, back_rows, weights):
    rows, width = dx.shape
    ns = dbc.shape[1]
    array, first = weights["lanes"]
    model = array.shape[0]
    block = min(256, rows)
    ins = [(v, (block, v.shape[1]), rows_at) for v in (dgate, dx, dbc, ddt)]
    ins += [(v, v.shape, fixed) for v in (last_x, last_bc, back_rows)]
    ins += [
        block_of(weights["gate"]),
        block_of(weights["x"]),
        (array, (model, ns), lambda i, t: (0, first + t[0])),
        block_of((array, LANES, first + 2)),
    ]
    outs = [((rows, model), BF16, (block, model), rows_at)]
    return call(
        back_low_body, (rows // block,), ins, outs, (), flag, flops=2 * rows * model * (2 * width + 256), name="back_low"
    )[0]


def back_norm_body(up_ref, a_ref, b_ref, h_ref, gain_ref, out_ref, sum_ref):
    @pl.when(pl.program_id(0) == 0)
    def _():
        sum_ref[...] = jnp.zeros_like(sum_ref)

    hidden = h_ref[...].astype(F32)
    grad = a_ref[...].astype(F32) + b_ref[...].astype(F32)
    model = hidden.shape[1]
    norm = lax.rsqrt(jnp.mean(hidden * hidden, axis=1, keepdims=True) + EPSILON)
    normed = hidden * norm
    sum_ref[7:8] += jnp.sum(grad * normed, axis=0, keepdims=True)
    gained = grad * gain_ref[0:1]
    inner = jnp.sum(gained * normed, axis=1, keepdims=True) / model
    out_ref[...] = up_ref[...].astype(F32) + norm * (gained - normed * inner)


def back_norm(up, a, b, hidden, gain):
    rows, model = hidden.shape
    block = min(256, rows)
    wide = (block, model)
    ins = [(v, wide, rows_at) for v in (up, a, b, hidden)] + [(gain, gain.shape, fixed)]
    outs = [((rows, model), F32, wide, rows_at), ((EDGE, model), F32, (EDGE, model), fixed)]
    return call(back_norm_body, (rows // block,), ins, outs, name="back_norm")


def weight_grad_body(places, shards, cuts, owners, ahead, where, *refs):
    count = max(owners) + 1
    lefts, refs = refs[:count], refs[count:]
    factors, refs = refs[: len(cuts)], refs[len(cuts) :]
    if ahead:
        before, priors, refs = refs[0], refs[1 : 1 + len(cuts)], refs[1 + len(cuts) :]
    outs, scratch = refs[:places], refs[places:]
    model = lefts[0].shape[0]
    part = model // places
    rows = part // shards
    step = pl.program_id(0)
    if shards > 1:

        @pl.when(step == 0)
        def _():
            for source, ordered in zip(([lefts[0], before] if ahead else [lefts[0]]), scratch):
                for k in range(places):
                    for z in range(shards):
                        at = pl.ds(pl.multiple_of((z * places + where[k]) * rows, rows), rows)
                        ordered[k * part + z * rows : k * part + (z + 1) * rows] = source[at]

    for i, (factor, owner, (start, end)) in enumerate(zip(factors, owners, cuts)):

        @pl.when((step >= start) & (step < end))
        def _(i=i, factor=factor, owner=owner):
            if ahead:
                prior = priors[i][...]
                empty = jnp.zeros((LANES - EDGE, prior.shape[1]), F32)
                prior = jnp.concatenate([prior, empty], axis=0).astype(BF16)
            for k in range(places):
                if places == 1:
                    at = slice(None)
                elif shards == 1:
                    at = pl.ds(pl.multiple_of(where[k] * part, part), part)
                else:
                    at = slice(k * part, (k + 1) * part)
                made = dot((scratch[0] if shards > 1 else lefts[owner])[at], factor[...])
                if ahead:
                    made = made + dot((scratch[1] if shards > 1 else before)[at], prior)
                outs[k][...] = made.astype(BF16)


def weight_grad(where, places, shards, products, ahead=None):
    model, rows = products[0][0].shape
    tile = 512 if all(b.shape[1] % 512 == 0 for _, factors in products for b in factors) else 256
    cuts, owners, ins, at = [], [], [], 0
    for i, (a, factors) in enumerate(products):
        ins.append((a, a.shape, fixed))
        for b in factors:
            cuts.append((at, at + b.shape[1] // tile))
            owners.append(i)
            at = cuts[-1][1]

    def columns_of(arrays):
        return [
            (b, (b.shape[0], tile), lambda i, *_, s=start, e=end: (0, jnp.clip(i - s, 0, e - s - 1)))
            for b, (start, end) in zip(arrays, cuts)
        ]

    ins += columns_of([b for _, factors in products for b in factors])
    if ahead:
        ins += [(ahead[0], ahead[0].shape, fixed)] + columns_of(ahead[1])
    width = at * tile
    part = model // places
    outs = [((part, width), BF16, (part, tile), columns_at)] * places
    scratch = []
    if shards > 1:
        scratch = [pltpu.VMEM((model, rows), BF16)] + ([pltpu.VMEM((model, LANES), BF16)] if ahead else [])
    return call(
        functools.partial(weight_grad_body, places, shards, cuts, owners, bool(ahead)), (at,), ins, outs, scratch, where,
        name="weight_grad",
    )


def relative(value, axis, by):
    size = lax.axis_size(axis)
    return lax.ppermute(value, axis, [(i, i ^ by) for i in range(size)])


def shifted(value, axis, by):
    size = lax.axis_size(axis)
    return lax.ppermute(value, axis, [(i, i + by) for i in range(size) if 0 <= i + by < size])


def tree_sum(values):
    while len(values) > 1:
        values = [a + b for a, b in zip(values[0::2], values[1::2])]
    return values[0]


def cut_body(joined, where, zx_ref, wbc_ref, wdt_ref, down_ref, *refs):
    width = zx_ref.shape[3]
    both, heads = wbc_ref.shape[2], wdt_ref.shape[2]
    rest, main, turned = refs[0], refs[1], refs[-1]
    other, at = (main, width) if joined else (refs[2], 0)
    rows = main.shape[0]
    main[:, :width] = zx_ref[0, :, 1]
    other[:, at : at + both] = wbc_ref[0]
    other[:, at + both :] = jnp.zeros((other.shape[0], LANES), BF16)
    other[:, at + both : at + both + heads] = wdt_ref[0]
    turned[...] = down_ref[0].astype(F32).T
    rest[:, :width] = zx_ref[0, :, 0]
    rest[:, width:] = turned[pl.ds(pl.multiple_of(where[0] * rows, rows), rows)].astype(BF16)


def cut_rows(layer, joined, place, rows, w_zx, w_bc, w_dt, w_out):
    local, _, width = w_zx.shape[1:]
    extra = w_bc.shape[2] + LANES
    taken = rows if joined else local
    ins = [(w_zx, (1, rows, 2, width), lambda i, c: (layer, c[0], 0, 0))]
    ins += [(v, (1, taken, v.shape[2]), lambda i, c: (layer, c[0] if joined else 0, 0)) for v in (w_bc, w_dt)]
    ins += [(w_out, (1,) + w_out.shape[1:], lambda i, c: (layer, 0, 0))]
    shapes = [(rows, 2 * width)] + ([(rows, width + extra)] if joined else [(rows, width), (local, extra)])
    outs = [(shape, BF16, shape, fixed) for shape in shapes]
    scratch = [pltpu.VMEM((local, width), F32)]
    return call(functools.partial(cut_body, joined), (1,), ins, outs, scratch, place, name="cut")


def gather_rows(piece):
    return lax.all_gather(piece, ("shard", "ctx"), axis=0, tiled=True)


def gather_shard(piece):
    return jnp.concatenate([piece] + [relative(piece, "shard", k) for k in range(1, lax.axis_size("shard"))], axis=0)


def gather_ctx(along):
    return [along] + [relative(along, "ctx", k) for k in range(1, lax.axis_size("ctx"))]


def gather_far(piece):
    return [piece] + [relative(piece, "shard", k) for k in range(1, lax.axis_size("shard"))]


def near_rows(pieces):
    return [pieces[0]] + [relative(p, "ctx", k) for k, p in enumerate(pieces) if k]


def split_sum_body(counts, where, *refs):
    arrays, outs = refs[: sum(counts)], refs[sum(counts) :]
    rows = outs[0].shape[0]
    for k, out in enumerate(outs):
        at = pl.ds(pl.multiple_of(where[k] * rows, rows), rows)
        done, column = 0, 0
        for count in counts:
            total = tree_sum([v[at].astype(F32) for v in arrays[done : done + count]])
            out[:, column : column + total.shape[1]] = total.astype(out.dtype)
            done, column = done + count, column + total.shape[1]


def split_sum(order, parts, groups):
    ins = [(v, v.shape, fixed) for group in groups for v in group]
    shape = (groups[0][0].shape[0] // parts, sum(group[0].shape[1] for group in groups))
    outs = [(shape, BF16 if k else F32, shape, fixed) for k in range(parts)]
    counts = [len(group) for group in groups]
    return call(functools.partial(split_sum_body, counts), (1,), ins, outs, (), order, name="split_sum")


def scattered(pieces, axis):
    return [pieces[0]] + [relative(pieces[k], axis, k) for k in range(1, len(pieces))]


def finish_body(counts, *refs):
    zx_ref, out_ref, small_ref = refs[-3:]
    layers, width = zx_ref.shape[0], zx_ref.shape[3]
    late = tree_sum([v[...].astype(F32) for v in refs[sum(counts) : -3]])
    span = late.shape[1] // layers
    for layer, count in enumerate(counts):
        early = tree_sum([v[...].astype(F32) for v in refs[:count]])
        refs = refs[count:]
        zx_ref[layer, :, 0] = early[:, :width]
        zx_ref[layer, :, 1] = late[:, layer * span : layer * span + width]
        out_ref[layer] = early[:, width:]
        small_ref[layer] = late[:, layer * span + width : (layer + 1) * span]


def finish(early, late, width):
    layers = len(early)
    rows, span = late[0].shape
    ins = [(v, v.shape, fixed) for parts in list(early) + [late] for v in parts]
    shapes = [(layers, rows, 2, width), (layers, rows, width), (layers, rows, span // layers - width)]
    outs = [(v, F32, v, lambda *_, n=len(v): (0,) * n) for v in shapes]
    return call(functools.partial(finish_body, [len(parts) for parts in early]), (1,), ins, outs, name="finish")


def axis_sum(value, axis):
    return tree_sum([value] + [relative(value, axis, k) for k in range(1, lax.axis_size(axis))])


def around(value, by=1):
    size = lax.axis_size("shard")
    return lax.ppermute(value, "shard", [(i, (i + by) % size) for i in range(size)])


def neighbours(ended, sign):
    return [shifted(ended, "ctx", sign * d) for d in range(1, lax.axis_size("ctx"))]


def swap(value):
    return lax.ppermute(value, "tp", [(0, 1), (1, 0)])


def pad_rows(value):
    return jnp.pad(value, ((0, EDGE - value.shape[0]), (0, 0)))


def per_device(
    seq_in, w_zx, w_bc, w_dt, w_out, norm_gain, conv_x, conv_bc, head_params, gate_gain, segments, pad_mask, cotangent
):
    rows, model = seq_in.shape[1:]
    layers = w_zx.shape[0]
    width = w_zx.shape[3]
    heads = head_params.shape[2]
    ns = w_bc.shape[2] // 2
    shards, places = lax.axis_size("shard"), lax.axis_size("ctx")
    inner_total = width * lax.axis_size("tp")
    z, c, t = lax.axis_index("shard"), lax.axis_index("ctx"), lax.axis_index("tp")
    flag = t.astype(jnp.int32).reshape(1)
    chunks = rows // CHUNK

    ids = jnp.concatenate([jnp.full((3,), -1, jnp.int32), segments[0]])
    ext = lax.dynamic_slice_in_dim(ids, c * rows, rows + 3, 0)
    seg = ext[3:]
    mask = lax.dynamic_slice_in_dim(pad_mask[0], c * rows, rows, 0)
    firsts = ext[2 : 2 + rows].reshape(chunks, CHUNK)[:, :1]
    lasts = seg.reshape(chunks, CHUNK)[:, CHUNK - 1 :]
    by_chunk = seg.reshape(chunks, CHUNK)
    columns = [(ext[3 - lag : 3 - lag + rows] == seg) for lag in (1, 2, 3)]
    columns += [mask, (by_chunk == firsts).reshape(rows), (by_chunk == lasts).reshape(rows), mask, seg]
    cols = jnp.stack([v.astype(F32) for v in columns], axis=1)
    segs = jnp.broadcast_to(seg.astype(F32)[None], (EDGE, rows))

    head_of = jnp.arange(width)[None] // (width // heads)
    spread = (jnp.arange(2 * LANES)[:, None] % LANES == head_of).astype(BF16)
    gather = (head_of.T == jnp.arange(LANES)[None]).astype(BF16)
    at = jnp.arange(CHUNK)
    lower = (at[:, None] >= at[None]).astype(F32)
    sums = jnp.concatenate([(at[:, None] <= at[None]).astype(F32), (at[:, None] > at[None]).astype(F32)], axis=1)

    own_count = model // (shards * places)
    tie = lax.optimization_barrier
    place = c.astype(jnp.int32).reshape(1)
    crossed = jnp.concatenate([z ^ jnp.arange(shards), c ^ jnp.arange(places)]).astype(jnp.int32)

    rest_piece, x_piece, other_piece = cut_rows(0, False, place, own_count, w_zx, w_bc, w_dt, w_out)
    before = shifted(seq_in[0, rows - EDGE :], "ctx", 1)
    near, far = gather_ctx(gather_shard(x_piece)), gather_far(other_piece)
    extra = 2 * ns + LANES
    rest = gather_rows(rest_piece)
    weights = [dict(gate=(rest, width, 0), out=(rest, width, 1))]
    mains = [None]
    for layer in range(1, layers):
        rest_piece, main_piece = cut_rows(layer, True, place, own_count, w_zx, w_bc, w_dt, w_out)
        rest = gather_rows(rest_piece)
        weights.append(dict(gate=(rest, width, 0), out=(rest, width, 1)))
        mains.append(main_piece)

    hidden = seq_in[0]
    parts = None
    kept = []
    for layer in range(layers):
        gain_in = pad_rows(norm_gain[layer][None])
        taps = pad_rows(conv_x[layer])
        taps_bc = pad_rows(conv_bc[layer])
        decay = -jnp.exp(head_params[layer, 1])
        head = jnp.pad(
            jnp.stack([head_params[layer, 0], decay]), ((0, EDGE - 2), (0, LANES - heads))
        )
        skip = jnp.repeat(head_params[layer, 2], width // heads)
        rowpack = pad_rows(jnp.stack([gate_gain[layer], skip]))

        if layer > 0:
            p_tail, q_tail = parts[0][rows - EDGE :].astype(F32), parts[1][rows - EDGE :].astype(F32)
            squares = p_tail[:, model : model + 2] + q_tail[:, model : model + 2]
            scale = lax.rsqrt(jnp.sum(squares, axis=1, keepdims=True) / inner_total + EPSILON)
            tail = hidden[rows - EDGE :].astype(F32) + scale * (p_tail[:, :model] + q_tail[:, :model])
            before = shifted(tail, "ctx", 1)
        hidden, low, turned, x_raw, raw_bc, dt_raw, w_x, w_other = enter(
            crossed, shards, near, far, hidden, parts, gain_in, width, 2 * ns, inner_total
        )
        weights[layer].update(x=(w_x, width, 0), other=(w_other, extra, 0), lanes=(w_other, 0))
        more = layer + 1 < layers
        if more:
            main, dt_raw = tie((mains[layer + 1], dt_raw))
            coming = gather_shard(main)
        edge, before_turned, xc, bc, step, cum, entered, phi, ended = states(
            x_raw, raw_bc, dt_raw, before, gain_in, weights[layer], cols, taps, taps_bc, head, spread, lower
        )
        y_in = within(xc, bc, step, cum, cols, segs, spread)
        given = neighbours(ended, 1)
        if more:
            given, coming, y_in = tie((given, coming, y_in))
            near, far = gather_ctx(coming), []
        ssm, gate, p_own, state_in = leave(
            given, y_in, low, xc, bc, cum, cols, entered, phi, rowpack, spread, weights[layer]
        )
        if more:
            p_own, near = tie((p_own, near))
        parts = (p_own, swap(p_own))
        kept.append(
            dict(
                hidden=hidden, turned=turned, x_raw=x_raw, raw_bc=raw_bc, dt_raw=dt_raw, edge=edge, before_turned=before_turned, gate=gate, xc=xc, bc=bc,
                step=step, cum=cum, entered=entered, phi=phi, ended=ended, state_in=state_in, ssm=ssm, parts=parts,
                gain_in=gain_in, taps=taps, taps_bc=taps_bc, head=head, rowpack=rowpack,
            )
        )
    direct = own_count % 16 == 0
    ctx_order = (c ^ jnp.arange(places)).astype(jnp.int32)
    ring_order = ((z - 1 - jnp.arange(shards)) % shards).astype(jnp.int32)
    shard_order = (z ^ jnp.arange(shards)).astype(jnp.int32)

    def owned(full):
        return lax.psum_scatter(full, ("shard", "ctx"), scatter_dimension=0, tiled=True)

    def add(a, b):
        return (a.astype(F32) + b.astype(F32)).astype(BF16)

    up = cotangent[0]
    smalls, early_sums, late_above = [], [], []
    for layer in reversed(range(layers)):
        k = kept[layer]
        last_layer = layer == layers - 1
        made = back_gate(
            up, k["parts"], k["ssm"], k["xc"], k["gate"], k["bc"], k["cum"], cols, k["phi"], k["ended"],
            k["rowpack"], spread, weights[layer], inner_total, k["hidden"] if last_layer else None,
        )
        if last_layer:
            output, made = made[0], made[1:]
        do, dy, dgate, normed, gain_rows, begun = made
        early_pair = [(k["turned"], [dgate]), (do, [normed])]
        later = neighbours(begun, -1)
        quick = direct and layer == 0
        if quick:
            early = weight_grad(ring_order, shards, 1, early_pair)
            dy, early, later = tie((dy, early, later))
            moving = around(early[0])
        else:
            early = weight_grad(ctx_order, 1, 1, early_pair)[0]
            dy, early = tie((dy, early))
        dx_in, left, dbc_in = back_within(
            k["xc"], k["bc"], k["step"], k["cum"], cols, segs, spread, gather, dy, k["ssm"]
        )
        if not quick:
            dx_in, later, early = tie((dx_in, later, early))
            g_early = owned(early)
        if quick and not last_layer:
            dx_in, early_sums[0] = tie((dx_in, early_sums[0]))
            later, rest_above = tie((later, rest_above))
            rest_above = near_rows(rest_above)
        edge = k["edge"]
        dx, last, prior, dbc_mine, dbc_theirs, ddt, conv_rows, head_rows = back_inter(
            flag, later, k["x_raw"], edge, k["xc"], k["bc"], k["step"], k["cum"], cols, k["dt_raw"], dy,
            dx_in, left, dbc_in, k["entered"], k["phi"], k["state_in"], k["taps"], k["head"], k["rowpack"],
            spread, gather, sums,
        )
        if quick:
            dx, moving = tie((dx, moving))
            moving = around(add(moving, early[1]))
            if not last_layer:
                dbc_theirs, late_above[0] = tie((dbc_theirs, rest_above))
        db, last_bc, prior_bc, conv_bc_rows = back_bc(
            flag, k["raw_bc"], edge, cols, k["taps_bc"], dbc_mine, swap(dbc_theirs)
        )
        back_rows = shifted(jnp.concatenate([prior, prior_bc], axis=1), "ctx", -1)
        late_pair = [(k["turned"], [dx, jnp.concatenate([db, ddt], axis=1)])]
        ahead = (k["before_turned"], [prior, jnp.pad(prior_bc, ((0, 0), (0, LANES)))])
        if direct:
            rest = weight_grad(ctx_order, places, shards, late_pair, ahead)
            dgate, rest, back_rows = tie((dgate, rest, back_rows))
            if quick:
                rest = near_rows(rest)
        else:
            g_rest = owned(weight_grad(ctx_order, 1, 1, late_pair, ahead)[0])
        dlow = back_low(flag, dgate, dx, db, ddt, last, last_bc, back_rows, weights[layer])
        if quick:
            dlow, moving = tie((dlow, moving))
            for one in early[2:-1]:
                moving = around(add(moving, one))
            dlow, rest = tie((dlow, rest))
        up, norm_rows = back_norm(up, dlow, swap(dlow), k["hidden"], k["gain_in"])
        packed = jnp.concatenate([conv_rows + gain_rows + norm_rows, conv_bc_rows, head_rows], axis=1)
        smalls.insert(0, packed)
        if not direct:
            early_sums.insert(0, [g_early])
            late_above.insert(0, g_rest)
        elif not quick:
            rest_above = rest
            early_sums.insert(0, [g_early])
            late_above.insert(0, None)
        else:
            late_sum = scattered(split_sum(shard_order, shards, [rest] + late_above), "shard")
            partial = axis_sum(jnp.concatenate(smalls), "ctx")
            partial, moving = tie((partial, moving))
            early_sums.insert(0, scattered(split_sum(ctx_order, places, [[moving, early[-1]]]), "ctx"))
            partial, late_sum, early_sums[0] = tie((partial, late_sum, early_sums[0]))
    if not direct:
        late_sum = [jnp.concatenate(late_above, axis=1)]
        partial = axis_sum(jnp.concatenate(smalls), "ctx")
    packed = axis_sum(partial, "shard").reshape(layers, EDGE, -1)
    grad_zx, grad_out, grad_small = finish(early_sums, late_sum, width)
    small_mine = grad_small[:, :, :ns]
    cb_mine = packed[:, :5, width : width + ns]
    cb_other, small_other = swap(cb_mine), swap(small_mine)

    def ordered(own, other):
        first = jnp.where(t == 0, own, other)
        return jnp.concatenate([first, jnp.where(t == 0, other, own)], axis=-1)

    skip_sum = jnp.sum(packed[:, 5, :width].reshape(layers, heads, width // heads), axis=-1)
    head_sums = packed[:, :2, width + ns : width + ns + heads]
    return (
        output[None],
        up[None],
        grad_zx,
        ordered(small_mine, small_other),
        grad_small[:, :, ns : ns + heads],
        jnp.swapaxes(grad_out, 1, 2),
        packed[:, 7, :width],
        packed[:, :5, :width],
        ordered(cb_mine, cb_other),
        jnp.concatenate([head_sums, skip_sum[:, None]], axis=1),
        packed[:, 6, :width],
    )


def solution(mesh):
    in_specs = (
        P("shard", "ctx", None),
        P(None, "shard", None, "tp"),
        P(None, "shard", None),
        P(None, "shard", "tp"),
        P(None, "tp", "shard"),
        P(),
        P(None, None, "tp"),
        P(),
        P(None, None, "tp"),
        P(None, "tp"),
        P("shard", None),
        P("shard", None),
        P("shard", "ctx", None),
    )
    out_specs = (
        P("shard", "ctx", None),
        P("shard", "ctx", None),
        P(None, ("shard", "ctx"), None, "tp"),
        P(None, ("shard", "ctx"), None),
        P(None, ("shard", "ctx"), "tp"),
        P(None, "tp", ("shard", "ctx")),
        P(),
        P(None, None, "tp"),
        P(),
        P(None, None, "tp"),
        P(None, "tp"),
    )
    return jax.shard_map(per_device, mesh=mesh, in_specs=in_specs, out_specs=out_specs, check_vma=False)
```

```python
import functools

import jax
import jax.numpy as jnp
from jax import lax
from jax.experimental import pallas as pl
from jax.experimental.pallas import tpu as pltpu
from jax.sharding import PartitionSpec as P

EPSILON = 1e-05
EXACT = lax.Precision.HIGHEST
F32 = jnp.float32
BF16 = jnp.bfloat16
CHUNK = 128
LANES = 128
EDGE = 8
CLOSED = -1e30
VMEM = 54 << 20


def dot(a, b, dims=((1,), (0,)), precision=None):
    return lax.dot_general(a, b, (dims, ((), ())), precision=precision, preferred_element_type=F32)


def split(values):
    high = values.astype(BF16)
    return high, (values - high.astype(F32)).astype(BF16)


def expand(values, spread):
    return dot(jnp.concatenate(split(values), axis=1), spread)


def folded(payloads):
    ns = payloads[0].shape[0] - EDGE
    total = payloads[-1][:ns].astype(F32)
    for one in reversed(payloads[:-1]):
        total = one[:ns].astype(F32) + one[ns : ns + 1].astype(F32) * total
    return total


def conv_shifts(ext, same):
    return [ext[EDGE:]] + [pltpu.roll(ext, lag, 0)[EDGE:] * same[lag] for lag in (1, 2, 3)]


def conv_sum(shifts, taps):
    total = taps[4:5] + taps[0:1] * shifts[0]
    for lag in (1, 2, 3):
        total = total + taps[lag : lag + 1] * shifts[lag]
    return total


def same_columns(cols, width):
    return [None] + [jnp.broadcast_to(cols[:, lag - 1 : lag], (cols.shape[0], width)) for lag in (1, 2, 3)]


def pair_masked(values):
    lane = lax.broadcasted_iota(jnp.int32, values.shape, 1)
    zero = jnp.zeros_like(values)
    first = lane < LANES // 2
    return jnp.concatenate([jnp.where(first, values, zero), jnp.where(first, zero, values)], axis=0)


def pairs_bias(seg_col, seg_row, later_rows):
    size = seg_col.shape[0]
    row = lax.broadcasted_iota(jnp.int32, (size, size), 0)
    col = lax.broadcasted_iota(jnp.int32, (size, size), 1)
    ordered = (row >= col) if later_rows else (row <= col)
    return jnp.where(ordered & (seg_col == seg_row), 0.0, CLOSED)


def chunks_of(ref):
    return [slice(at, at + CHUNK) for at in range(0, ref.shape[0], CHUNK)]


def silu_parts(values):
    sig = jax.nn.sigmoid(values)
    return sig, values * sig


def call(body, grid, ins, outs, scratch=(), scalars=None, flops=0, name=None):
    count = 0 if scalars is None else 1

    def adapt(block, fn):
        if block is None:
            return pl.BlockSpec(memory_space=pl.ANY)
        return pl.BlockSpec(block, fn)

    in_specs = [adapt(block, fn) for _, block, fn in ins]
    out_specs = [adapt(block, fn) for _, _, block, fn in outs]
    shapes = [jax.ShapeDtypeStruct(shape, dtype) for shape, dtype, _, _ in outs]
    moved = sum(a.size * a.dtype.itemsize for a, _, _ in ins) + sum(
        s.size * s.dtype.itemsize for s in shapes
    )
    made = pl.pallas_call(
        body,
        out_shape=shapes,
        grid_spec=pltpu.PrefetchScalarGridSpec(
            num_scalar_prefetch=count,
            grid=grid,
            in_specs=in_specs,
            out_specs=out_specs,
            scratch_shapes=list(scratch),
        ),
        compiler_params=pltpu.CompilerParams(
            vmem_limit_bytes=VMEM, dimension_semantics=("arbitrary",) * len(grid)
        ),
        cost_estimate=pl.CostEstimate(flops=1, bytes_accessed=1, transcendentals=0),
        name=name,
    )
    arrays = [a for a, _, _ in ins]
    return made(*(([scalars] if count else []) + arrays))


def rows_at(i, *_):
    return (i, 0)


def columns_at(i, *_):
    return (0, i)


def fixed(*_):
    return (0, 0)


def piece_copies(pieces, sems):
    copies = []
    for source, target, start in pieces:
        rows = source.shape[0]
        at = target.at[pl.ds(pl.multiple_of(start, rows), rows)]
        copies.append(pltpu.make_async_copy(source, at, sems.at[len(copies)]))
    for one in copies:
        one.start()
    for one in copies:
        one.wait()


def enter_body(first, inner_total, cuts, where, *refs):
    shards, places, rows = cuts
    near, refs = refs[:places], refs[places:]
    far, refs = (refs[:shards], refs[shards:]) if first else ((), refs)
    if first:
        h_ref, gain, u_ref, turned_ref, x_ref, bc_ref, dt_ref, w_x, w_other, sems = refs
        hidden = h_ref[...].astype(F32)
    else:
        h_ref, p_ref, q_ref, gain, h_out, u_ref, turned_ref, x_ref, bc_ref, dt_ref, w_x, w_other, sems = refs
        model = h_ref.shape[1]
        summed = p_ref[:, :model].astype(F32) + q_ref[:, :model].astype(F32)
        hidden = h_ref[...].astype(F32) + gated_scale(p_ref, q_ref, model, inner_total) * summed
        h_out[...] = hidden
    both = bc_ref.shape[1]
    width = x_ref.shape[1]

    @pl.when(pl.program_id(0) == 0)
    def _():
        pieces = [(v, w_other, where[z] * v.shape[0]) for z, v in enumerate(far)]
        for z in range(shards):
            for k in range(places):
                start = (where[z] * places + where[shards + k]) * rows
                source = near[k].at[pl.ds(z * rows, rows)]
                pieces.append((source.at[:, :width], w_x, start))
                if not far:
                    pieces.append((source.at[:, width:], w_other, start))
        piece_copies(pieces, sems)

    norm = lax.rsqrt(jnp.mean(hidden * hidden, axis=1, keepdims=True) + EPSILON)
    lowered = (hidden * norm * gain[0:1]).astype(BF16)
    u_ref[...] = lowered
    turned_ref[...] = lowered.T
    x_ref[...] = dot(lowered, w_x[...]).astype(BF16)
    made = dot(lowered, w_other[...])
    bc_ref[...] = made[:, :both].astype(BF16)
    dt_ref[...] = made[:, both:]


def gated_scale(p_ref, q_ref, model, inner_total):
    squares = p_ref[:, model:].astype(F32) + q_ref[:, model:].astype(F32)
    return lax.rsqrt((squares[:, 0:1] + squares[:, 1:2]) / inner_total + EPSILON)


def block_of(part):
    array, width, index = part
    return (array, (array.shape[0], width), lambda *_: (0, index))


def enter(where, shards, near, far, hidden, parts, gain, width, both, inner_total):
    rows, model = hidden.shape
    first = parts is None
    block = min(256, rows)
    wide = (block, model)
    ins = [(v, None, None) for v in near + far] + [(hidden, wide, rows_at)]
    outs = []
    if not first:
        ins += [(part, (block, model + LANES), rows_at) for part in parts]
        outs.append(((rows, model), F32, wide, rows_at))
    ins += [(gain, gain.shape, fixed)]
    outs += [
        ((rows, model), BF16, wide, rows_at),
        ((model, rows), BF16, (model, block), columns_at),
        ((rows, width), BF16, (block, width), rows_at),
        ((rows, both), BF16, (block, both), rows_at),
        ((rows, LANES), F32, (block, LANES), rows_at),
    ]
    outs += [((model, v), BF16, (model, v), fixed) for v in (width, both + LANES)]
    scratch = [pltpu.SemaphoreType.DMA((shards * (2 * len(near)),))]
    cuts = (shards, len(near), near[0].shape[0] // shards)
    made = call(
        functools.partial(enter_body, first, inner_total, cuts), (rows // block,), ins, outs, scratch, where, name="enter"
    )
    return [hidden] + list(made) if first else list(made)


def states_body(
    x_ref, raw_bc_ref, dt_ref, before_ref, gain_ref, w_x, w_other, cols_ref, taps_ref, taps_bc_ref, head_ref,
    spread_ref, lower_ref, edge_ref, before_turned, xc_ref, bc_ref, step_ref, cum_ref, enter_ref, phi_ref, last_ref,
    tail_x, tail_bc, state, phi,
):
    chunk = pl.program_id(0)
    width = x_ref.shape[1]
    ns = raw_bc_ref.shape[1] // 2

    @pl.when(chunk == 0)
    def _():
        before = before_ref[...].astype(F32)
        norm = lax.rsqrt(jnp.mean(before * before, axis=1, keepdims=True) + EPSILON)
        lowered = (before * norm * gain_ref[0:1]).astype(BF16)
        padding = jnp.zeros((LANES - EDGE, lowered.shape[1]), F32)
        before_turned[...] = jnp.concatenate([lowered.astype(F32), padding], axis=0).T.astype(BF16)
        edge = dot(lowered, w_x[...]).astype(BF16)
        edge_bc = dot(lowered, w_other[:, : 2 * ns]).astype(BF16)
        edge_ref[:, :width] = edge
        edge_ref[:, width:] = edge_bc
        tail_x[...] = edge.astype(F32)
        tail_bc[...] = edge_bc.astype(F32)
        state[...] = jnp.zeros_like(state)
        phi[...] = jnp.ones_like(phi)

    for sub, here in enumerate(chunks_of(x_ref)):
        cols = cols_ref[here]
        same = same_columns(cols, LANES)
        dt = jax.nn.softplus(dt_ref[here] + head_ref[0:1]) * cols[:, 3:4]
        rates = head_ref[1:2] * dt
        cum = dot(lower_ref[...], rates, precision=EXACT)
        step_ref[here] = dt
        cum_ref[here] = cum
        size = cum.shape[0]
        tail_dt = cols[:, 5:6] * jnp.exp(cum[size - 1 : size] - cum) * dt
        fold = cols[size - 1 : size, 4:5] * jnp.exp(cum[size - EDGE : size])[EDGE - 1 : EDGE]
        fold_rows = jnp.broadcast_to(fold, phi.shape)
        wide = expand(jnp.concatenate([tail_dt, fold_rows], axis=0), spread_ref[...])

        halves = []
        for i in range(2):
            part = slice(i * ns, (i + 1) * ns)
            now = raw_bc_ref[here, part].astype(F32)
            shifts = conv_shifts(jnp.concatenate([tail_bc[:, part], now], axis=0), same)
            tail_bc[:, part] = now[size - EDGE :]
            halves.append(silu_parts(conv_sum(shifts, taps_bc_ref[:, part]))[1].astype(BF16))
            bc_ref[here, part] = halves[i]
        b_turned = halves[0].astype(F32).T.astype(BF16)

        enter_ref[sub] = state[...].astype(BF16)
        phi_ref[sub] = phi[...]
        for i in range(width // LANES):
            part = slice(i * LANES, (i + 1) * LANES)
            now = x_ref[here, part].astype(F32)
            shifts = conv_shifts(jnp.concatenate([tail_x[:, part], now], axis=0), same)
            tail_x[:, part] = now[size - EDGE :]
            x_conv = silu_parts(conv_sum(shifts, taps_ref[:, part]))[1].astype(BF16)
            xc_ref[here, part] = x_conv
            held = (x_conv.astype(F32) * wide[:size, part]).astype(BF16)
            state[:, part] = wide[size : size + 1, part] * state[:, part] + dot(b_turned, held)
        phi[...] = phi[...] * fold_rows

    @pl.when(chunk == pl.num_programs(0) - 1)
    def _():
        last_ref[:ns] = state[...].astype(BF16)
        last_ref[ns:] = expand(phi[...], spread_ref[...]).astype(BF16)


def states(x_raw, raw_bc, dt_raw, before, gain, weights, cols, taps, taps_bc, head, spread, lower):
    rows, width = x_raw.shape
    ns = raw_bc.shape[1] // 2
    count = rows // CHUNK
    block = min(256, rows)
    subs = block // CHUNK
    ins = [
        (x_raw, (block, width), rows_at),
        (raw_bc, (block, 2 * ns), rows_at),
        (dt_raw, (block, LANES), rows_at),
        (before, before.shape, fixed),
        (gain, gain.shape, fixed),
        block_of(weights["x"]),
        block_of(weights["other"]),
        (cols, (block, cols.shape[1]), rows_at),
        (taps, taps.shape, fixed),
        (taps_bc, taps_bc.shape, fixed),
        (head, head.shape, fixed),
        (spread, spread.shape, fixed),
        (lower, lower.shape, fixed),
    ]
    outs = [
        ((EDGE, width + 2 * ns), BF16, (EDGE, width + 2 * ns), fixed),
        ((before.shape[1], LANES), BF16, (before.shape[1], LANES), fixed),
        ((rows, width), BF16, (block, width), rows_at),
        ((rows, 2 * ns), BF16, (block, 2 * ns), rows_at),
        ((rows, LANES), F32, (block, LANES), rows_at),
        ((rows, LANES), F32, (block, LANES), rows_at),
        ((count, ns, width), BF16, (subs, ns, width), lambda i, *_: (i, 0, 0)),
        ((count, EDGE, LANES), F32, (subs, EDGE, LANES), lambda i, *_: (i, 0, 0)),
        ((ns + EDGE, width), BF16, (ns + EDGE, width), fixed),
    ]
    scratch = [
        pltpu.VMEM((EDGE, width), F32),
        pltpu.VMEM((EDGE, 2 * ns), F32),
        pltpu.VMEM((ns, width), F32),
        pltpu.VMEM((EDGE, LANES), F32),
    ]
    return call(states_body, (rows // block,), ins, outs, scratch, flops=2 * rows * width * ns * 4, name="states")


def within_body(xc_ref, bc_ref, step_ref, cum_ref, cols_ref, segs_ref, spread_ref, y_ref):
    ns = bc_ref.shape[1] // 2
    width = xc_ref.shape[1]
    for here in chunks_of(y_ref):
        cum = cum_ref[here]
        cum_rows = cum.T
        bias = pairs_bias(cols_ref[here, 7:8], segs_ref[0:1, here], True)
        both = dot(bc_ref[here, ns:], bc_ref[here, :ns], ((1,), (1,)))
        step_wide = expand(step_ref[here], spread_ref[...])
        for pair in range(width // LANES):
            part = slice(pair * LANES, (pair + 1) * LANES)
            weighted = (xc_ref[here, part].astype(F32) * step_wide[:, part]).astype(BF16)
            maps = []
            for head in (2 * pair, 2 * pair + 1):
                gap = (cum[:, head : head + 1] - cum_rows[head : head + 1]) + bias
                maps.append((jnp.exp(gap) * both).astype(BF16))
            y_ref[here, part] = dot(jnp.concatenate(maps, axis=1), pair_masked(weighted))


def within(xc, bc, step, cum, cols, segs, spread):
    rows, width = xc.shape
    block = min(512, rows)
    ins = [
        (xc, (block, width), rows_at),
        (bc, (block, bc.shape[1]), rows_at),
        (step, (block, LANES), rows_at),
        (cum, (block, LANES), rows_at),
        (cols, (block, cols.shape[1]), rows_at),
        (segs, (EDGE, block), columns_at),
        (spread, spread.shape, fixed),
    ]
    outs = [((rows, width), F32, (block, width), rows_at)]
    return call(within_body, (rows // block,), ins, outs, name="within")[0]


def leave_body(count, *refs):
    payloads, refs = refs[:count], refs[count:]
    (w_gate, w_out, y_ref, low_ref, xc_ref, bc_ref, cum_ref, cols_ref, enter_ref, phi_ref, rows_ref, spread_ref) = refs[:12]
    ssm_ref, gate_ref, p_ref, in_ref, normed = refs[12:]
    ns = in_ref.shape[0]
    width = xc_ref.shape[1]
    spread = spread_ref[...]

    @pl.when(pl.program_id(0) == 0)
    def _():
        in_ref[...] = folded([p[...] for p in payloads])

    gate_ref[...] = dot(low_ref[...], w_gate[...])
    for sub in range(y_ref.shape[0] // CHUNK):
        here = slice(sub * CHUNK, (sub + 1) * CHUNK)
        phi_wide = expand(phi_ref[sub], spread)[0:1]
        begun = (enter_ref[sub].astype(F32) + phi_wide * in_ref[...]).astype(BF16)
        carried = cols_ref[here, 4:5] * jnp.exp(cum_ref[here])
        carried_wide = expand(carried, spread)
        far = dot(bc_ref[here, ns:], begun)
        ssm_ref[here] = y_ref[here] + carried_wide * far
    total = jnp.zeros((y_ref.shape[0], LANES), F32)
    for i in range(width // LANES):
        part = slice(i * LANES, (i + 1) * LANES)
        mixed = ssm_ref[:, part] + rows_ref[1:2, part] * xc_ref[:, part].astype(F32)
        gated = mixed * silu_parts(gate_ref[:, part])[1]
        total = total + gated * gated
        normed[:, part] = (gated * rows_ref[0:1, part]).astype(BF16)
    high, rest = split(jnp.broadcast_to(jnp.sum(total, axis=1, keepdims=True), total.shape))
    lane = lax.broadcasted_iota(jnp.int32, total.shape, 1)
    model = w_out.shape[0]
    p_ref[:, :model] = dot(normed[...], w_out[...], ((1,), (1,))).astype(BF16)
    p_ref[:, model:] = jnp.where(lane == 0, high.astype(F32), rest.astype(F32)).astype(BF16)


def leave(payloads, y_in, low, xc, bc, cum, cols, entered, phi, rowpack, spread, weights):
    rows, width = xc.shape
    model = low.shape[1]
    ns = bc.shape[1] // 2
    block = min(256, rows)
    subs = block // CHUNK
    ins = [(p, p.shape, fixed) for p in payloads]
    ins += [
        block_of(weights["gate"]),
        block_of(weights["out"]),
        (y_in, (block, width), rows_at),
        (low, (block, model), rows_at),
        (xc, (block, width), rows_at),
        (bc, (block, bc.shape[1]), rows_at),
        (cum, (block, LANES), rows_at),
        (cols, (block, cols.shape[1]), rows_at),
        (entered, (subs, ns, width), lambda i, *_: (i, 0, 0)),
        (phi, (subs, EDGE, LANES), lambda i, *_: (i, 0, 0)),
        (rowpack, rowpack.shape, fixed),
        (spread, spread.shape, fixed),
    ]
    outs = [
        ((rows, width), F32, (block, width), rows_at),
        ((rows, width), F32, (block, width), rows_at),
        ((rows, model + LANES), BF16, (block, model + LANES), rows_at),
        ((ns, width), F32, (ns, width), fixed),
    ]
    scratch = [pltpu.VMEM((block, width), BF16)]
    return call(functools.partial(leave_body, len(payloads)), (rows // block,), ins, outs, scratch, name="leave")


def back_gate_body(
    inner_total, ends, *refs
):
    if ends:
        hidden_ref, refs = refs[0], refs[1:]
        output_ref, refs = refs[14], refs[:14] + refs[15:]
    (
        up_ref, p_ref, q_ref, ssm_ref, xc_ref, gate_ref, bc_ref, cum_ref, cols_ref, phi_ref,
        factor_ref, rows_ref, spread_ref, w_ref,
        do_ref, dy_ref, dgate_ref, n_ref, gain_ref, out_ref, state,
    ) = refs
    step = pl.program_id(0)
    ns = state.shape[0]
    width = xc_ref.shape[1]
    spread = spread_ref[...]

    @pl.when(step == 0)
    def _():
        gain_ref[...] = jnp.zeros_like(gain_ref)
        state[...] = jnp.zeros_like(state)

    model = up_ref.shape[1]
    scale = gated_scale(p_ref, q_ref, model, inner_total)
    up = up_ref[...].astype(BF16)
    do_ref[...] = up.T
    summed = p_ref[:, :model].astype(F32) + q_ref[:, :model].astype(F32)
    if ends:
        output_ref[...] = hidden_ref[...].astype(F32) + scale * summed
    spread_sum = jnp.sum(up.astype(F32) * summed, axis=1, keepdims=True)
    pull = scale * scale * scale * spread_sum / inner_total
    scale_wide = jnp.broadcast_to(scale, (scale.shape[0], LANES))
    pull_wide = jnp.broadcast_to(pull, scale_wide.shape)
    back = dot(up, w_ref[...])
    for i in range(width // LANES):
        part = slice(i * LANES, (i + 1) * LANES)
        gain = rows_ref[0:1, part]
        gate = gate_ref[:, part]
        sig, soft = silu_parts(gate)
        mixed = ssm_ref[:, part] + rows_ref[1:2, part] * xc_ref[:, part].astype(F32)
        gated = mixed * soft
        scaled = gated * scale_wide
        grad = back[:, part]
        gain_ref[6:7, part] += jnp.sum(grad * scaled, axis=0, keepdims=True)
        grad_gated = grad * gain * scale_wide - gated * pull_wide
        dy_ref[:, part] = (grad_gated * soft).astype(BF16)
        dgate_ref[:, part] = (grad_gated * mixed * (sig * (1.0 + gate * (1.0 - sig)))).astype(BF16)
        n_ref[:, part] = (scaled * gain).astype(BF16)
    for sub in range(up_ref.shape[0] // CHUNK):
        here = slice(sub * CHUNK, (sub + 1) * CHUNK)
        phi_wide = expand(phi_ref[sub], spread)[0:1]
        carried_wide = expand(cols_ref[here, 4:5] * jnp.exp(cum_ref[here]), spread)
        c_turned = bc_ref[here, ns:].astype(F32).T.astype(BF16)
        carried_dy = (dy_ref[here].astype(F32) * carried_wide).astype(BF16)
        state[...] += phi_wide * dot(c_turned, carried_dy)

    @pl.when(step == pl.num_programs(0) - 1)
    def _():
        out_ref[:ns] = state[...].astype(BF16)
        out_ref[ns:] = factor_ref[...]


def back_gate(up, parts, ssm, xc, gate, bc, cum, cols, phi, ended, rowpack, spread, weights, inner_total, hidden=None):
    rows, width = xc.shape
    model = up.shape[1]
    ns = bc.shape[1] // 2
    block = min(256, rows)
    subs = block // CHUNK
    wide = (block, model)
    ins = [
        (up, wide, rows_at),
        (parts[0], (block, model + LANES), rows_at),
        (parts[1], (block, model + LANES), rows_at),
        (ssm, (block, width), rows_at),
        (xc, (block, width), rows_at),
        (gate, (block, width), rows_at),
        (bc, (block, 2 * ns), rows_at),
        (cum, (block, LANES), rows_at),
        (cols, (block, cols.shape[1]), rows_at),
        (phi, (subs, EDGE, LANES), lambda i, *_: (i, 0, 0)),
        (ended, (EDGE, width), lambda i, *_: (ns // EDGE, 0)),
        (rowpack, rowpack.shape, fixed),
        (spread, spread.shape, fixed),
        block_of(weights["out"]),
    ]
    outs = [
        ((model, rows), BF16, (model, block), columns_at),
        ((rows, width), BF16, (block, width), rows_at),
        ((rows, width), BF16, (block, width), rows_at),
        ((rows, width), BF16, (block, width), rows_at),
        ((EDGE, width), F32, (EDGE, width), fixed),
        ((ns + EDGE, width), BF16, (ns + EDGE, width), fixed),
    ]
    if hidden is not None:
        ins = [(hidden, wide, rows_at)] + ins
        outs = [((rows, model), F32, wide, rows_at)] + outs
    scratch = [pltpu.VMEM((ns, width), F32)]
    return call(
        functools.partial(back_gate_body, inner_total, hidden is not None), (rows // block,), ins, outs, scratch,
        flops=2 * rows * width * model * 1.3, name="back_gate",
    )


def back_within_body(
    xc_ref, bc_ref, step_ref, cum_ref, cols_ref, segs_ref, spread_ref, gather_ref, dy_ref, ssm_ref,
    dx_ref, left_ref, dbc_ref, products,
):
    ns = bc_ref.shape[1] // 2
    size, width = CHUNK, xc_ref.shape[1]
    for here in chunks_of(xc_ref):
        cum = cum_ref[here]
        cum_rows = cum.T
        bias = pairs_bias(cols_ref[here, 7:8], segs_ref[0:1, here], False)
        b_part = bc_ref[here, :ns]
        c_part = bc_ref[here, ns:]
        both = dot(b_part, c_part, ((1,), (1,)))
        step_wide = expand(step_ref[here], spread_ref[...])
        grad_both = jnp.zeros((size, size), F32)
        for pair in range(width // LANES):
            part = slice(pair * LANES, (pair + 1) * LANES)
            weighted = (xc_ref[here, part].astype(F32) * step_wide[:, part]).astype(BF16)
            dy = dy_ref[here, part]
            dy_pair = pair_masked(dy)
            grad_maps = dot(weighted, dy_pair, ((1,), (1,)))
            maps = []
            for k in (0, 1):
                head = 2 * pair + k
                decay = jnp.exp((cum_rows[head : head + 1] - cum[:, head : head + 1]) + bias)
                maps.append((decay * both).astype(BF16))
                grad_both = grad_both + decay * grad_maps[:, k * size : (k + 1) * size]
            grad_x = dot(jnp.concatenate(maps, axis=1), dy_pair)
            dx_ref[here, part] = grad_x.astype(BF16)
            high, rest = split(dy.astype(F32) * ssm_ref[here, part] - weighted.astype(F32) * grad_x)
            products[:size, part] = high
            products[size:, part] = rest
        left = dot(products[...], gather_ref[...])
        left_ref[here] = left[:size] + left[size:]
        dbc_ref[here, :ns] = dot(grad_both.astype(BF16), c_part)
        dbc_ref[here, ns:] = dot(grad_both.T.astype(BF16), b_part)


def back_within(xc, bc, step, cum, cols, segs, spread, gather, dy, ssm):
    rows, width = xc.shape
    block = min(256, rows)
    ins = [
        (xc, (block, width), rows_at),
        (bc, (block, bc.shape[1]), rows_at),
        (step, (block, LANES), rows_at),
        (cum, (block, LANES), rows_at),
        (cols, (block, cols.shape[1]), rows_at),
        (segs, (EDGE, block), columns_at),
        (spread, spread.shape, fixed),
        (gather, gather.shape, fixed),
        (dy, (block, width), rows_at),
        (ssm, (block, width), rows_at),
    ]
    outs = [
        ((rows, width), BF16, (block, width), rows_at),
        ((rows, LANES), F32, (block, LANES), rows_at),
        ((rows, bc.shape[1]), F32, (block, bc.shape[1]), rows_at),
    ]
    scratch = [pltpu.VMEM((2 * CHUNK, width), BF16)]
    return call(back_within_body, (rows // block,), ins, outs, scratch, name="back_within")


def conv_back(ext, same, taps, grad_conv, next_rows):
    size = ext.shape[0] - EDGE
    shifts = conv_shifts(ext, same)
    pre = conv_sum(shifts, taps)
    sig = jax.nn.sigmoid(pre)
    grad_pre = grad_conv * (sig * (1.0 + pre * (1.0 - sig)))
    sums = [jnp.sum(grad_pre * shifts[lag], axis=0, keepdims=True) for lag in range(4)]
    sums.append(jnp.sum(grad_pre, axis=0, keepdims=True))
    zero = jnp.zeros((EDGE, ext.shape[1]), F32)
    length = size + 2 * EDGE
    raw = taps[0:1] * jnp.concatenate([zero, grad_pre], axis=0)
    firsts = []
    for lag in (1, 2, 3):
        term = grad_pre * same[lag] * taps[lag : lag + 1]
        firsts.append(term[:EDGE])
        padded = jnp.concatenate([zero, term, next_rows[lag - 1]], axis=0)
        raw = raw + pltpu.roll(padded, length - lag, 0)[: size + EDGE]
    return raw, firsts, sums


def back_inter_body(count_in, flag, *refs):
    payloads, refs = refs[:count_in], refs[count_in:]
    (
        x_ref, before_ref, edge_ref, xc_ref, bc_ref, step_ref, cum_ref, cols_ref, dt_ref, dy_ref, dxi_ref,
        left_ref, dbci_ref, enter_ref, phi_ref, in_ref, taps_ref, head_ref, rows_ref, spread_ref, gather_ref, sums_ref,
        dx_ref, last_ref, prior_ref, mine_ref, theirs_ref, ddt_ref, conv_ref, heads_ref,
        grad_state, next_rows, wide, far, carried, held, begun, ending, products,
    ) = refs
    step = pl.program_id(0)
    first_block = step == pl.num_programs(0) - 1
    ns = in_ref.shape[0]
    size, width = CHUNK, xc_ref.shape[1]

    @pl.when(step == 0)
    def _():
        grad_state[...] = folded([p[...] for p in payloads])
        next_rows[...] = jnp.zeros_like(next_rows)
        conv_ref[...] = jnp.zeros_like(conv_ref)
        heads_ref[...] = jnp.zeros_like(heads_ref)

    subs = len(chunks_of(xc_ref))
    for sub, here in reversed(list(enumerate(chunks_of(xc_ref)))):
        cols = cols_ref[here]
        same = same_columns(cols, LANES)
        cum = cum_ref[here]
        dt = step_ref[here]
        decay_in = cols[:, 4:5] * jnp.exp(cum)
        decay_out = cols[:, 5:6] * jnp.exp(cum[size - 1 : size] - cum)
        fold_rows = jnp.broadcast_to(decay_in[size - EDGE : size][EDGE - 1 : EDGE], (EDGE, LANES))
        b_part = bc_ref[here, :ns]
        c_part = bc_ref[here, ns:]
        c_turned = c_part.astype(F32).T.astype(BF16)
        stacked = jnp.concatenate([decay_in, decay_out, dt, fold_rows, phi_ref[sub]], axis=0)
        wide[...] = expand(stacked, spread_ref[...])
        fold_at = 3 * size
        for i in range(width // LANES):
            part = slice(i * LANES, (i + 1) * LANES)
            dy = dy_ref[here, part].astype(F32)
            weighted = xc_ref[here, part].astype(F32) * wide[2 * size : 3 * size, part]
            fold_wide = wide[fold_at : fold_at + 1, part]
            grad_end = grad_state[:, part]
            start = enter_ref[sub, :, part].astype(F32) + wide[fold_at + EDGE : fold_at + EDGE + 1, part] * in_ref[:, part]
            carried[:, part] = (dy * wide[:size, part]).astype(BF16)
            held[:, part] = (weighted * wide[size : 2 * size, part]).astype(BF16)
            begun[:, part] = start.astype(BF16)
            ending[:, part] = grad_end.astype(BF16)
            pass_sum = jnp.sum(start * grad_end, axis=0, keepdims=True) * fold_wide
            products[2 * size :, part] = jnp.broadcast_to(pass_sum, (2 * EDGE, LANES)).astype(BF16)
            grad_state[:, part] = fold_wide * grad_end
        far[...] = dot(b_part, ending[...])
        dbc_c = dbci_ref[here, ns:] + dot(carried[...], begun[...], ((1,), (1,)))
        dbc_b = dbci_ref[here, :ns] + dot(held[...], ending[...], ((1,), (1,)))
        grad_state[...] += dot(c_turned, carried[...])
        own_b = flag[0] == 0
        mine_ref[here] = jnp.where(own_b, dbc_b, dbc_c).astype(BF16)
        theirs_ref[here] = jnp.where(own_b, dbc_c, dbc_b).astype(BF16)

        for i in range(width // LANES):
            part = slice(i * LANES, (i + 1) * LANES)
            dy = dy_ref[here, part].astype(F32)
            x_conv = xc_ref[here, part].astype(F32)
            dt_wide = wide[2 * size : 3 * size, part]
            grad_far = wide[size : 2 * size, part] * far[:, part]
            grad_weighted = dxi_ref[here, part].astype(F32) + grad_far
            products[:size, part] = (x_conv * dt_wide * grad_far).astype(BF16)
            products[size : 2 * size, part] = (x_conv * grad_weighted).astype(BF16)
            conv_ref[5:6, part] += jnp.sum(dy * x_conv, axis=0, keepdims=True)
            grad_conv = dt_wide * grad_weighted + rows_ref[1:2, part] * dy
            if sub:
                ahead = x_ref[here.start - EDGE : here.start, part].astype(F32)
            else:
                ahead = jnp.where(first_block, edge_ref[:, part].astype(F32), before_ref[:, part].astype(F32))
            ext = jnp.concatenate([ahead, x_ref[here, part].astype(F32)], axis=0)
            raw, firsts, tap_sums = conv_back(
                ext, same, taps_ref[:, part], grad_conv, [next_rows[k, :, part] for k in range(3)]
            )
            for k in range(3):
                next_rows[k, :, part] = firsts[k]
            for k in range(5):
                conv_ref[k : k + 1, part] += tap_sums[k]
            dx_ref[here, part] = raw[EDGE:].astype(BF16)
            prior_ref[:, part] = raw[:EDGE]

            if sub == subs - 1:

                @pl.when(step == 0)
                def _(raw=raw, part=part):
                    last_ref[:, part] = raw[size:]

        per_head = dot(products[...], gather_ref[...])
        outward, direct, through = per_head[:size], per_head[size : 2 * size], per_head[2 * size : 2 * size + 1]
        grad_rate = dot(sums_ref[...], jnp.concatenate([left_ref[here], outward], axis=0), precision=EXACT) + through
        grad_dt = direct + head_ref[1:2] * grad_rate
        grad_raw = grad_dt * cols[:, 3:4] * jax.nn.sigmoid(dt_ref[here] + head_ref[0:1])
        ddt_ref[here] = grad_raw.astype(BF16)
        heads_ref[0:1] += jnp.sum(grad_raw, axis=0, keepdims=True)
        heads_ref[1:2] += jnp.sum(grad_rate * head_ref[1:2] * dt, axis=0, keepdims=True)


def back_inter(
    flag, payloads, x_raw, edge, xc, bc, step, cum, cols, dt_raw, dy, dx_in, left, dbc_in, entered, phi, state_in,
    taps, head, rowpack, spread, gather, sums,
):
    rows, width = xc.shape
    ns = bc.shape[1] // 2
    block = min(256, rows)
    subs = block // CHUNK
    count = rows // block

    def back(i, *_):
        return (count - 1 - i, 0)

    def back3(i, *_):
        return (count - 1 - i, 0, 0)

    def before(i, *_):
        return (jnp.maximum((count - 1 - i) * (block // EDGE) - 1, 0), 0)

    def at(width_now):
        return (block, width_now)

    ins = [(p, p.shape, fixed) for p in payloads] + [
        (x_raw, at(width), back),
        (x_raw, (EDGE, width), before),
        (edge, (EDGE, width), fixed),
        (xc, at(width), back),
        (bc, at(2 * ns), back),
        (step, at(LANES), back),
        (cum, at(LANES), back),
        (cols, at(cols.shape[1]), back),
        (dt_raw, at(LANES), back),
        (dy, at(width), back),
        (dx_in, at(width), back),
        (left, at(LANES), back),
        (dbc_in, at(2 * ns), back),
        (entered, (subs, ns, width), back3),
        (phi, (subs, EDGE, LANES), back3),
        (state_in, state_in.shape, fixed),
        (taps, taps.shape, fixed),
        (head, head.shape, fixed),
        (rowpack, rowpack.shape, fixed),
        (spread, spread.shape, fixed),
        (gather, gather.shape, fixed),
        (sums, sums.shape, fixed),
    ]
    outs = [
        ((rows, width), BF16, at(width), back),
        ((EDGE, width), F32, (EDGE, width), fixed),
        ((EDGE, width), F32, (EDGE, width), fixed),
        ((rows, ns), BF16, at(ns), back),
        ((rows, ns), BF16, at(ns), back),
        ((rows, LANES), BF16, at(LANES), back),
        ((EDGE, width), F32, (EDGE, width), fixed),
        ((EDGE, LANES), F32, (EDGE, LANES), fixed),
    ]
    scratch = [
        pltpu.VMEM((ns, width), F32),
        pltpu.VMEM((3, EDGE, width), F32),
        pltpu.VMEM((3 * CHUNK + 2 * EDGE, width), F32),
        pltpu.VMEM((CHUNK, width), F32),
        pltpu.VMEM((CHUNK, width), BF16),
        pltpu.VMEM((CHUNK, width), BF16),
        pltpu.VMEM((ns, width), BF16),
        pltpu.VMEM((ns, width), BF16),
        pltpu.VMEM((2 * CHUNK + 2 * EDGE, width), BF16),
    ]
    return call(
        functools.partial(back_inter_body, len(payloads)), (count,), ins, outs, scratch, flag, name="back_inter"
    )


def back_bc_body(
    flag, raw_ref, edge_ref, cols_ref, taps_ref, mine_ref, theirs_ref, ddt_ref, out_ref, last_ref, prior_ref, sums_ref
):
    size, width = raw_ref.shape
    same = same_columns(cols_ref[...], width)
    ext = jnp.concatenate([edge_ref[...].astype(F32), raw_ref[...].astype(F32)], axis=0)
    grad = mine_ref[...].astype(F32) + theirs_ref[...].astype(F32)
    zero = jnp.zeros((EDGE, width), F32)
    raw, _, sums = conv_back(ext, same, taps_ref[...], grad, [zero] * 3)
    out_ref[:, :width] = raw[EDGE:].astype(BF16)
    out_ref[:, width:] = ddt_ref[...]
    last_ref[...] = raw[size:]
    prior_ref[:, :width] = raw[:EDGE]
    prior_ref[:, width:] = jnp.zeros((EDGE, ddt_ref.shape[1]), F32)
    sums_ref[...] = jnp.concatenate(sums + [zero[:3]], axis=0)


def back_bc(flag, raw, edge, cols, taps, mine, theirs, ddt):
    rows, ns = mine.shape
    joined = ns + ddt.shape[1]
    before = edge.shape[1] // ns - 2
    ins = [
        (raw, (rows, ns), lambda i, t: (0, t[0])),
        (edge, (EDGE, ns), lambda i, t: (0, before + t[0])),
        (cols, cols.shape, fixed),
        (taps, (EDGE, ns), lambda i, t: (0, t[0])),
        (mine, mine.shape, fixed),
        (theirs, theirs.shape, fixed),
        (ddt, ddt.shape, fixed),
    ]
    outs = [((rows, joined), BF16, (rows, joined), fixed)]
    outs += [((EDGE, v), F32, (EDGE, v), fixed) for v in (ns, joined, ns)]
    return call(back_bc_body, (1,), ins, outs, (), flag, name="back_bc")


def back_low_body(
    flag, gate_ref, x_ref, small_ref, last_x, last_bc, back_ref, wg_ref, wx_ref, wb_ref, wt_ref, out_ref
):
    ns = last_bc.shape[1]

    def product(gate, x, bc, dt):
        over = ((1,), (1,))
        total = dot(gate, wg_ref[...], over) + dot(x, wx_ref[...], over)
        return (total + dot(bc, wb_ref[...], over) + dot(dt, wt_ref[...], over)).astype(BF16)

    out_ref[...] = product(gate_ref[...], x_ref[...], small_ref[:, :ns], small_ref[:, ns:])

    @pl.when(pl.program_id(0) == pl.num_programs(0) - 1)
    def _():
        size, width = x_ref.shape
        end = slice(size - 2 * EDGE, size)

        def righted(value, last, back):
            kept = value.astype(F32)[:EDGE]
            return jnp.concatenate([kept, last[...] + back], axis=0).astype(BF16)

        x = righted(x_ref[end], last_x, back_ref[:, :width])
        bc = righted(small_ref[end, :ns], last_bc, back_ref[:, width : width + ns])
        out_ref[end] = product(gate_ref[end], x, bc, small_ref[end, ns:])


def back_low(flag, dgate, dx, small, last_x, last_bc, back_rows, weights):
    rows, width = dx.shape
    ns = last_bc.shape[1]
    array, first = weights["lanes"]
    model = array.shape[0]
    block = min(256, rows)
    ins = [(v, (block, v.shape[1]), rows_at) for v in (dgate, dx, small)]
    ins += [(v, v.shape, fixed) for v in (last_x, last_bc, back_rows)]
    ins += [
        block_of(weights["gate"]),
        block_of(weights["x"]),
        (array, (model, ns), lambda i, t: (0, first + t[0])),
        block_of((array, LANES, first + 2)),
    ]
    outs = [((rows, model), BF16, (block, model), rows_at)]
    return call(
        back_low_body, (rows // block,), ins, outs, (), flag, flops=2 * rows * model * (2 * width + 256), name="back_low"
    )[0]


def back_norm_body(up_ref, a_ref, b_ref, h_ref, gain_ref, out_ref, sum_ref):
    @pl.when(pl.program_id(0) == 0)
    def _():
        sum_ref[...] = jnp.zeros_like(sum_ref)

    hidden = h_ref[...].astype(F32)
    grad = a_ref[...].astype(F32) + b_ref[...].astype(F32)
    model = hidden.shape[1]
    norm = lax.rsqrt(jnp.mean(hidden * hidden, axis=1, keepdims=True) + EPSILON)
    normed = hidden * norm
    sum_ref[7:8] += jnp.sum(grad * normed, axis=0, keepdims=True)
    gained = grad * gain_ref[0:1]
    inner = jnp.sum(gained * normed, axis=1, keepdims=True) / model
    out_ref[...] = up_ref[...].astype(F32) + norm * (gained - normed * inner)


def back_norm(up, a, b, hidden, gain):
    rows, model = hidden.shape
    block = min(256, rows)
    wide = (block, model)
    ins = [(v, wide, rows_at) for v in (up, a, b, hidden)] + [(gain, gain.shape, fixed)]
    outs = [((rows, model), F32, wide, rows_at), ((EDGE, model), F32, (EDGE, model), fixed)]
    return call(back_norm_body, (rows // block,), ins, outs, name="back_norm")


def weight_grad_body(places, shards, cuts, owners, ahead, where, *refs):
    count = max(owners) + 1
    lefts, refs = refs[:count], refs[count:]
    factors, refs = refs[: len(cuts)], refs[len(cuts) :]
    if ahead:
        before, priors, refs = refs[0], refs[1 : 1 + len(cuts)], refs[1 + len(cuts) :]
    outs, scratch = refs[:places], refs[places:]
    model = lefts[0].shape[0]
    part = model // places
    rows = part // shards
    step = pl.program_id(0)
    if shards > 1:

        @pl.when(step == 0)
        def _():
            for source, ordered in zip(([lefts[0], before] if ahead else [lefts[0]]), scratch):
                for k in range(places):
                    for z in range(shards):
                        at = pl.ds(pl.multiple_of((z * places + where[k]) * rows, rows), rows)
                        ordered[k * part + z * rows : k * part + (z + 1) * rows] = source[at]

    for i, (factor, owner, (start, end)) in enumerate(zip(factors, owners, cuts)):

        @pl.when((step >= start) & (step < end))
        def _(i=i, factor=factor, owner=owner):
            if ahead:
                prior = priors[i][...]
                empty = jnp.zeros((LANES - EDGE, prior.shape[1]), F32)
                prior = jnp.concatenate([prior, empty], axis=0).astype(BF16)
            for k in range(places):
                if places == 1:
                    at = slice(None)
                elif shards == 1:
                    at = pl.ds(pl.multiple_of(where[k] * part, part), part)
                else:
                    at = slice(k * part, (k + 1) * part)
                made = dot((scratch[0] if shards > 1 else lefts[owner])[at], factor[...])
                if ahead:
                    made = made + dot((scratch[1] if shards > 1 else before)[at], prior)
                outs[k][...] = made.astype(BF16)


def weight_grad(where, places, shards, products, ahead=None):
    model, rows = products[0][0].shape
    tile = 512 if all(b.shape[1] % 512 == 0 for _, factors in products for b in factors) else 256
    cuts, owners, ins, at = [], [], [], 0
    for i, (a, factors) in enumerate(products):
        ins.append((a, a.shape, fixed))
        for b in factors:
            cuts.append((at, at + b.shape[1] // tile))
            owners.append(i)
            at = cuts[-1][1]

    def columns_of(arrays):
        return [
            (b, (b.shape[0], tile), lambda i, *_, s=start, e=end: (0, jnp.clip(i - s, 0, e - s - 1)))
            for b, (start, end) in zip(arrays, cuts)
        ]

    ins += columns_of([b for _, factors in products for b in factors])
    if ahead:
        ins += [(ahead[0], ahead[0].shape, fixed)] + columns_of(ahead[1])
    width = at * tile
    part = model // places
    outs = [((part, width), BF16, (part, tile), columns_at)] * places
    scratch = []
    if shards > 1:
        scratch = [pltpu.VMEM((model, rows), BF16)] + ([pltpu.VMEM((model, LANES), BF16)] if ahead else [])
    return call(
        functools.partial(weight_grad_body, places, shards, cuts, owners, bool(ahead)), (at,), ins, outs, scratch, where,
        name="weight_grad",
    )


def relative(value, axis, by):
    size = lax.axis_size(axis)
    return lax.ppermute(value, axis, [(i, i ^ by) for i in range(size)])


def shifted(value, axis, by):
    size = lax.axis_size(axis)
    return lax.ppermute(value, axis, [(i, i + by) for i in range(size) if 0 <= i + by < size])


def tree_sum(values):
    while len(values) > 1:
        values = [a + b for a, b in zip(values[0::2], values[1::2])]
    return values[0]


def cut_body(joined, where, zx_ref, wbc_ref, wdt_ref, down_ref, *refs):
    width = zx_ref.shape[3]
    both, heads = wbc_ref.shape[2], wdt_ref.shape[2]
    rest, main, turned = refs[0], refs[1], refs[-1]
    other, at = (main, width) if joined else (refs[2], 0)
    rows = main.shape[0]
    main[:, :width] = zx_ref[0, :, 1]
    other[:, at : at + both] = wbc_ref[0]
    other[:, at + both :] = jnp.zeros((other.shape[0], LANES), BF16)
    other[:, at + both : at + both + heads] = wdt_ref[0]
    turned[...] = down_ref[0].astype(F32).T
    rest[:, :width] = zx_ref[0, :, 0]
    rest[:, width:] = turned[pl.ds(pl.multiple_of(where[0] * rows, rows), rows)].astype(BF16)


def cut_rows(layer, joined, place, rows, w_zx, w_bc, w_dt, w_out):
    local, _, width = w_zx.shape[1:]
    extra = w_bc.shape[2] + LANES
    taken = rows if joined else local
    ins = [(w_zx, (1, rows, 2, width), lambda i, c: (layer, c[0], 0, 0))]
    ins += [(v, (1, taken, v.shape[2]), lambda i, c: (layer, c[0] if joined else 0, 0)) for v in (w_bc, w_dt)]
    ins += [(w_out, (1,) + w_out.shape[1:], lambda i, c: (layer, 0, 0))]
    shapes = [(rows, 2 * width)] + ([(rows, width + extra)] if joined else [(rows, width), (local, extra)])
    outs = [(shape, BF16, shape, fixed) for shape in shapes]
    scratch = [pltpu.VMEM((local, width), F32)]
    return call(functools.partial(cut_body, joined), (1,), ins, outs, scratch, place, name="cut")


def gather_rows(piece):
    return lax.all_gather(piece, ("shard", "ctx"), axis=0, tiled=True)


def gather_shard(piece):
    return jnp.concatenate([piece] + [relative(piece, "shard", k) for k in range(1, lax.axis_size("shard"))], axis=0)


def gather_ctx(along):
    return [along] + [relative(along, "ctx", k) for k in range(1, lax.axis_size("ctx"))]


def gather_far(piece):
    return [piece] + [relative(piece, "shard", k) for k in range(1, lax.axis_size("shard"))]


def near_rows(pieces):
    return [pieces[0]] + [relative(p, "ctx", k) for k, p in enumerate(pieces) if k]


def split_sum_body(counts, where, *refs):
    arrays, outs = refs[: sum(counts)], refs[sum(counts) :]
    rows = outs[0].shape[0]
    for k, out in enumerate(outs):
        at = pl.ds(pl.multiple_of(where[k] * rows, rows), rows)
        done, column = 0, 0
        for count in counts:
            total = tree_sum([v[at].astype(F32) for v in arrays[done : done + count]])
            out[:, column : column + total.shape[1]] = total.astype(out.dtype)
            done, column = done + count, column + total.shape[1]


def split_sum(order, parts, groups):
    ins = [(v, v.shape, fixed) for group in groups for v in group]
    shape = (groups[0][0].shape[0] // parts, sum(group[0].shape[1] for group in groups))
    outs = [(shape, BF16 if k else F32, shape, fixed) for k in range(parts)]
    counts = [len(group) for group in groups]
    return call(functools.partial(split_sum_body, counts), (1,), ins, outs, (), order, name="split_sum")


def scattered(pieces, axis):
    return [pieces[0]] + [relative(pieces[k], axis, k) for k in range(1, len(pieces))]


def finish_body(counts, *refs):
    zx_ref, out_ref, small_ref = refs[-3:]
    layers, width = zx_ref.shape[0], zx_ref.shape[3]
    late = tree_sum([v[...].astype(F32) for v in refs[sum(counts) : -3]])
    span = late.shape[1] // layers
    for layer, count in enumerate(counts):
        early = tree_sum([v[...].astype(F32) for v in refs[:count]])
        refs = refs[count:]
        zx_ref[layer, :, 0] = early[:, :width]
        zx_ref[layer, :, 1] = late[:, layer * span : layer * span + width]
        out_ref[layer] = early[:, width:]
        small_ref[layer] = late[:, layer * span + width : (layer + 1) * span]


def finish(early, late, width):
    layers = len(early)
    rows, span = late[0].shape
    ins = [(v, v.shape, fixed) for parts in list(early) + [late] for v in parts]
    shapes = [(layers, rows, 2, width), (layers, rows, width), (layers, rows, span // layers - width)]
    outs = [(v, F32, v, lambda *_, n=len(v): (0,) * n) for v in shapes]
    return call(functools.partial(finish_body, [len(parts) for parts in early]), (1,), ins, outs, name="finish")


def axis_sum(value, axis):
    return tree_sum([value] + [relative(value, axis, k) for k in range(1, lax.axis_size(axis))])


def around(value, by=1):
    size = lax.axis_size("shard")
    return lax.ppermute(value, "shard", [(i, (i + by) % size) for i in range(size)])


def neighbours(ended, sign):
    return [shifted(ended, "ctx", sign * d) for d in range(1, lax.axis_size("ctx"))]


def swap(value):
    return lax.ppermute(value, "tp", [(0, 1), (1, 0)])


def pad_rows(value):
    return jnp.pad(value, ((0, EDGE - value.shape[0]), (0, 0)))


def per_device(
    seq_in, w_zx, w_bc, w_dt, w_out, norm_gain, conv_x, conv_bc, head_params, gate_gain, segments, pad_mask, cotangent
):
    rows, model = seq_in.shape[1:]
    layers = w_zx.shape[0]
    width = w_zx.shape[3]
    heads = head_params.shape[2]
    ns = w_bc.shape[2] // 2
    shards, places = lax.axis_size("shard"), lax.axis_size("ctx")
    inner_total = width * lax.axis_size("tp")
    z, c, t = lax.axis_index("shard"), lax.axis_index("ctx"), lax.axis_index("tp")
    flag = t.astype(jnp.int32).reshape(1)
    chunks = rows // CHUNK

    ids = jnp.concatenate([jnp.full((3,), -1, jnp.int32), segments[0]])
    ext = lax.dynamic_slice_in_dim(ids, c * rows, rows + 3, 0)
    seg = ext[3:]
    mask = lax.dynamic_slice_in_dim(pad_mask[0], c * rows, rows, 0)
    firsts = ext[2 : 2 + rows].reshape(chunks, CHUNK)[:, :1]
    lasts = seg.reshape(chunks, CHUNK)[:, CHUNK - 1 :]
    by_chunk = seg.reshape(chunks, CHUNK)
    columns = [(ext[3 - lag : 3 - lag + rows] == seg) for lag in (1, 2, 3)]
    columns += [mask, (by_chunk == firsts).reshape(rows), (by_chunk == lasts).reshape(rows), mask, seg]
    cols = jnp.stack([v.astype(F32) for v in columns], axis=1)
    segs = jnp.broadcast_to(seg.astype(F32)[None], (EDGE, rows))

    head_of = jnp.arange(width)[None] // (width // heads)
    spread = (jnp.arange(2 * LANES)[:, None] % LANES == head_of).astype(BF16)
    gather = (head_of.T == jnp.arange(LANES)[None]).astype(BF16)
    at = jnp.arange(CHUNK)
    lower = (at[:, None] >= at[None]).astype(F32)
    sums = jnp.concatenate([(at[:, None] <= at[None]).astype(F32), (at[:, None] > at[None]).astype(F32)], axis=1)

    own_count = model // (shards * places)
    tie = lax.optimization_barrier
    place = c.astype(jnp.int32).reshape(1)
    crossed = jnp.concatenate([z ^ jnp.arange(shards), c ^ jnp.arange(places)]).astype(jnp.int32)

    rest_piece, x_piece, other_piece = cut_rows(0, False, place, own_count, w_zx, w_bc, w_dt, w_out)
    before = shifted(seq_in[0, rows - EDGE :], "ctx", 1)
    near, far = gather_ctx(gather_shard(x_piece)), gather_far(other_piece)
    extra = 2 * ns + LANES
    rest = gather_rows(rest_piece)
    weights = [dict(gate=(rest, width, 0), out=(rest, width, 1))]
    mains = [None]
    for layer in range(1, layers):
        rest_piece, main_piece = cut_rows(layer, True, place, own_count, w_zx, w_bc, w_dt, w_out)
        rest = gather_rows(rest_piece)
        weights.append(dict(gate=(rest, width, 0), out=(rest, width, 1)))
        mains.append(main_piece)

    params = []
    for layer in range(layers):
        gain_in = pad_rows(norm_gain[layer][None])
        taps = pad_rows(conv_x[layer])
        taps_bc = pad_rows(conv_bc[layer])
        decay = -jnp.exp(head_params[layer, 1])
        head = jnp.pad(
            jnp.stack([head_params[layer, 0], decay]), ((0, EDGE - 2), (0, LANES - heads))
        )
        skip = jnp.repeat(head_params[layer, 2], width // heads)
        rowpack = pad_rows(jnp.stack([gate_gain[layer], skip]))
        params.append((gain_in, taps, taps_bc, head, rowpack))
    ctx_order = (c ^ jnp.arange(places)).astype(jnp.int32)
    ring_order = ((z - 1 - jnp.arange(shards)) % shards).astype(jnp.int32)
    shard_order = (z ^ jnp.arange(shards)).astype(jnp.int32)
    constants = (cols, segs, spread, gather, lower, sums, flag, ctx_order, ring_order, shard_order)
    near, far, params, constants = tie((near, far, params, constants))
    cols, segs, spread, gather, lower, sums, flag, ctx_order, ring_order, shard_order = constants

    hidden = seq_in[0]
    parts = None
    kept = []
    for layer in range(layers):
        gain_in, taps, taps_bc, head, rowpack = params[layer]

        if layer > 0:
            p_tail, q_tail = parts[0][rows - EDGE :].astype(F32), parts[1][rows - EDGE :].astype(F32)
            squares = p_tail[:, model : model + 2] + q_tail[:, model : model + 2]
            scale = lax.rsqrt(jnp.sum(squares, axis=1, keepdims=True) / inner_total + EPSILON)
            tail = hidden[rows - EDGE :].astype(F32) + scale * (p_tail[:, :model] + q_tail[:, :model])
            before = shifted(tail, "ctx", 1)
        hidden, low, turned, x_raw, raw_bc, dt_raw, w_x, w_other = enter(
            crossed, shards, near, far, hidden, parts, gain_in, width, 2 * ns, inner_total
        )
        weights[layer].update(x=(w_x, width, 0), other=(w_other, extra, 0), lanes=(w_other, 0))
        more = layer + 1 < layers
        if more:
            main, dt_raw = tie((mains[layer + 1], dt_raw))
            coming = gather_shard(main)
        edge, before_turned, xc, bc, step, cum, entered, phi, ended = states(
            x_raw, raw_bc, dt_raw, before, gain_in, weights[layer], cols, taps, taps_bc, head, spread, lower
        )
        y_in = within(xc, bc, step, cum, cols, segs, spread)
        given = neighbours(ended, 1)
        if more:
            given, coming, y_in = tie((given, coming, y_in))
            near, far = gather_ctx(coming), []
        ssm, gate, p_own, state_in = leave(
            given, y_in, low, xc, bc, cum, cols, entered, phi, rowpack, spread, weights[layer]
        )
        if more:
            p_own, near = tie((p_own, near))
        parts = (p_own, swap(p_own))
        kept.append(
            dict(
                hidden=hidden, turned=turned, x_raw=x_raw, raw_bc=raw_bc, dt_raw=dt_raw, edge=edge, before_turned=before_turned, gate=gate, xc=xc, bc=bc,
                step=step, cum=cum, entered=entered, phi=phi, ended=ended, state_in=state_in, ssm=ssm, parts=parts,
                gain_in=gain_in, taps=taps, taps_bc=taps_bc, head=head, rowpack=rowpack,
            )
        )
    direct = own_count % 16 == 0

    def owned(full):
        return lax.psum_scatter(full, ("shard", "ctx"), scatter_dimension=0, tiled=True)

    def add(a, b):
        return (a.astype(F32) + b.astype(F32)).astype(BF16)

    up = cotangent[0]
    smalls, early_sums, late_above = [], [], []
    for layer in reversed(range(layers)):
        k = kept[layer]
        last_layer = layer == layers - 1
        made = back_gate(
            up, k["parts"], k["ssm"], k["xc"], k["gate"], k["bc"], k["cum"], cols, k["phi"], k["ended"],
            k["rowpack"], spread, weights[layer], inner_total, k["hidden"] if last_layer else None,
        )
        if last_layer:
            output, made = made[0], made[1:]
        do, dy, dgate, normed, gain_rows, begun = made
        early_pair = [(k["turned"], [dgate]), (do, [normed])]
        later = neighbours(begun, -1)
        quick = direct and layer == 0
        if quick:
            early = weight_grad(ring_order, shards, 1, early_pair)
            dy, early, later = tie((dy, early, later))
            moving = around(early[0])
        else:
            early = weight_grad(ctx_order, 1, 1, early_pair)[0]
            dy, early = tie((dy, early))
        dx_in, left, dbc_in = back_within(
            k["xc"], k["bc"], k["step"], k["cum"], cols, segs, spread, gather, dy, k["ssm"]
        )
        if not quick:
            dx_in, later, early = tie((dx_in, later, early))
            g_early = owned(early)
        if quick and not last_layer:
            dx_in, early_sums[0] = tie((dx_in, early_sums[0]))
            later, rest_above = tie((later, rest_above))
            rest_above = near_rows(rest_above)
        edge = k["edge"]
        dx, last, prior, dbc_mine, dbc_theirs, ddt, conv_rows, head_rows = back_inter(
            flag, later, k["x_raw"], edge, k["xc"], k["bc"], k["step"], k["cum"], cols, k["dt_raw"], dy,
            dx_in, left, dbc_in, k["entered"], k["phi"], k["state_in"], k["taps"], k["head"], k["rowpack"],
            spread, gather, sums,
        )
        if quick:
            dx, moving = tie((dx, moving))
            moving = around(add(moving, early[1]))
            if not last_layer:
                dbc_theirs, late_above[0] = tie((dbc_theirs, rest_above))
        small, last_bc, prior_bc, conv_bc_rows = back_bc(
            flag, k["raw_bc"], edge, cols, k["taps_bc"], dbc_mine, swap(dbc_theirs), ddt
        )
        back_rows = shifted(jnp.concatenate([prior, prior_bc], axis=1), "ctx", -1)
        late_pair = [(k["turned"], [dx, small])]
        ahead = (k["before_turned"], [prior, prior_bc])
        if direct:
            rest = weight_grad(ctx_order, places, shards, late_pair, ahead)
            dgate, rest, back_rows = tie((dgate, rest, back_rows))
            if quick:
                rest = near_rows(rest)
        else:
            g_rest = owned(weight_grad(ctx_order, 1, 1, late_pair, ahead)[0])
        dlow = back_low(flag, dgate, dx, small, last, last_bc, back_rows, weights[layer])
        if quick:
            dlow, moving = tie((dlow, moving))
            for one in early[2:-1]:
                moving = around(add(moving, one))
            dlow, rest = tie((dlow, rest))
        up, norm_rows = back_norm(up, dlow, swap(dlow), k["hidden"], k["gain_in"])
        packed = jnp.concatenate([conv_rows + gain_rows + norm_rows, conv_bc_rows, head_rows], axis=1)
        smalls.insert(0, packed)
        if not direct:
            early_sums.insert(0, [g_early])
            late_above.insert(0, g_rest)
        elif not quick:
            rest_above = rest
            early_sums.insert(0, [g_early])
            late_above.insert(0, None)
        else:
            late_sum = scattered(split_sum(shard_order, shards, [rest] + late_above), "shard")
            partial = axis_sum(jnp.concatenate(smalls), "ctx")
            partial, moving = tie((partial, moving))
            early_sums.insert(0, scattered(split_sum(ctx_order, places, [[moving, early[-1]]]), "ctx"))
            partial, late_sum, early_sums[0] = tie((partial, late_sum, early_sums[0]))
    if not direct:
        late_sum = [jnp.concatenate(late_above, axis=1)]
        partial = axis_sum(jnp.concatenate(smalls), "ctx")
    packed = axis_sum(partial, "shard").reshape(layers, EDGE, -1)
    grad_zx, grad_out, grad_small = finish(early_sums, late_sum, width)
    packed, grad_small = tie((packed, grad_small))
    small_mine = grad_small[:, :, :ns]
    cb_mine = packed[:, :5, width : width + ns]
    cb_other, small_other = swap(cb_mine), swap(small_mine)

    def ordered(own, other):
        first = jnp.where(t == 0, own, other)
        return jnp.concatenate([first, jnp.where(t == 0, other, own)], axis=-1)

    skip_sum = jnp.sum(packed[:, 5, :width].reshape(layers, heads, width // heads), axis=-1)
    head_sums = packed[:, :2, width + ns : width + ns + heads]
    return (
        output[None],
        up[None],
        grad_zx,
        ordered(small_mine, small_other),
        grad_small[:, :, ns : ns + heads],
        jnp.swapaxes(grad_out, 1, 2),
        packed[:, 7, :width],
        packed[:, :5, :width],
        ordered(cb_mine, cb_other),
        jnp.concatenate([head_sums, skip_sum[:, None]], axis=1),
        packed[:, 6, :width],
    )


def solution(mesh):
    in_specs = (
        P("shard", "ctx", None),
        P(None, "shard", None, "tp"),
        P(None, "shard", None),
        P(None, "shard", "tp"),
        P(None, "tp", "shard"),
        P(),
        P(None, None, "tp"),
        P(),
        P(None, None, "tp"),
        P(None, "tp"),
        P("shard", None),
        P("shard", None),
        P("shard", "ctx", None),
    )
    out_specs = (
        P("shard", "ctx", None),
        P("shard", "ctx", None),
        P(None, ("shard", "ctx"), None, "tp"),
        P(None, ("shard", "ctx"), None),
        P(None, ("shard", "ctx"), "tp"),
        P(None, "tp", ("shard", "ctx")),
        P(),
        P(None, None, "tp"),
        P(),
        P(None, None, "tp"),
        P(None, "tp"),
    )
    return jax.shard_map(per_device, mesh=mesh, in_specs=in_specs, out_specs=out_specs, check_vma=False)
```

```python
import functools

import jax
import jax.numpy as jnp
from jax import lax
from jax.experimental import pallas as pl
from jax.experimental.pallas import tpu as pltpu
from jax.sharding import PartitionSpec as P

EPSILON = 1e-05
EXACT = lax.Precision.HIGHEST
F32 = jnp.float32
BF16 = jnp.bfloat16
CHUNK = 128
LANES = 128
EDGE = 8
CLOSED = -1e30
VMEM = 54 << 20


def dot(a, b, dims=((1,), (0,)), precision=None):
    return lax.dot_general(a, b, (dims, ((), ())), precision=precision, preferred_element_type=F32)


def split(values):
    high = values.astype(BF16)
    return high, (values - high.astype(F32)).astype(BF16)


def expand(values, spread):
    return dot(jnp.concatenate(split(values), axis=1), spread)


def folded(payloads):
    ns = payloads[0].shape[0] - EDGE
    total = payloads[-1][:ns].astype(F32)
    for one in reversed(payloads[:-1]):
        total = one[:ns].astype(F32) + one[ns : ns + 1].astype(F32) * total
    return total


def conv_shifts(ext, same):
    return [ext[EDGE:]] + [pltpu.roll(ext, lag, 0)[EDGE:] * same[lag] for lag in (1, 2, 3)]


def conv_sum(shifts, taps):
    total = taps[4:5] + taps[0:1] * shifts[0]
    for lag in (1, 2, 3):
        total = total + taps[lag : lag + 1] * shifts[lag]
    return total


def same_columns(cols, width):
    return [None] + [jnp.broadcast_to(cols[:, lag - 1 : lag], (cols.shape[0], width)) for lag in (1, 2, 3)]


def pair_masked(values):
    lane = lax.broadcasted_iota(jnp.int32, values.shape, 1)
    zero = jnp.zeros_like(values)
    first = lane < LANES // 2
    return jnp.concatenate([jnp.where(first, values, zero), jnp.where(first, zero, values)], axis=0)


def pairs_bias(seg_col, seg_row, later_rows):
    size = seg_col.shape[0]
    row = lax.broadcasted_iota(jnp.int32, (size, size), 0)
    col = lax.broadcasted_iota(jnp.int32, (size, size), 1)
    ordered = (row >= col) if later_rows else (row <= col)
    return jnp.where(ordered & (seg_col == seg_row), 0.0, CLOSED)


def chunks_of(ref):
    return [slice(at, at + CHUNK) for at in range(0, ref.shape[0], CHUNK)]


def silu_parts(values):
    sig = jax.nn.sigmoid(values)
    return sig, values * sig


def call(body, grid, ins, outs, scratch=(), scalars=None, flops=0, name=None):
    count = 0 if scalars is None else 1

    def adapt(block, fn):
        if block is None:
            return pl.BlockSpec(memory_space=pl.ANY)
        return pl.BlockSpec(block, fn)

    in_specs = [adapt(block, fn) for _, block, fn in ins]
    out_specs = [adapt(block, fn) for _, _, block, fn in outs]
    shapes = [jax.ShapeDtypeStruct(shape, dtype) for shape, dtype, _, _ in outs]
    moved = sum(a.size * a.dtype.itemsize for a, _, _ in ins) + sum(
        s.size * s.dtype.itemsize for s in shapes
    )
    made = pl.pallas_call(
        body,
        out_shape=shapes,
        grid_spec=pltpu.PrefetchScalarGridSpec(
            num_scalar_prefetch=count,
            grid=grid,
            in_specs=in_specs,
            out_specs=out_specs,
            scratch_shapes=list(scratch),
        ),
        compiler_params=pltpu.CompilerParams(
            vmem_limit_bytes=VMEM, dimension_semantics=("arbitrary",) * len(grid)
        ),
        cost_estimate=pl.CostEstimate(flops=1, bytes_accessed=1, transcendentals=0),
        name=name,
    )
    arrays = [a for a, _, _ in ins]
    return made(*(([scalars] if count else []) + arrays))


def rows_at(i, *_):
    return (i, 0)


def columns_at(i, *_):
    return (0, i)


def fixed(*_):
    return (0, 0)


def piece_copies(pieces, sems):
    copies = []
    for source, target, start in pieces:
        rows = source.shape[0]
        at = target.at[pl.ds(pl.multiple_of(start, rows), rows)]
        copies.append(pltpu.make_async_copy(source, at, sems.at[len(copies)]))
    for one in copies:
        one.start()
    for one in copies:
        one.wait()


def enter_body(first, inner_total, cuts, where, *refs):
    shards, places, rows = cuts
    near, refs = refs[:places], refs[places:]
    far, refs = (refs[:shards], refs[shards:]) if first else ((), refs)
    if first:
        h_ref, gain, u_ref, turned_ref, x_ref, bc_ref, dt_ref, w_x, w_other, sems = refs
        hidden = h_ref[...].astype(F32)
    else:
        h_ref, p_ref, q_ref, gain, h_out, u_ref, turned_ref, x_ref, bc_ref, dt_ref, w_x, w_other, sems = refs
        model = h_ref.shape[1]
        summed = p_ref[:, :model].astype(F32) + q_ref[:, :model].astype(F32)
        hidden = h_ref[...].astype(F32) + gated_scale(p_ref, q_ref, model, inner_total) * summed
        h_out[...] = hidden
    both = bc_ref.shape[1]
    width = x_ref.shape[1]

    @pl.when(pl.program_id(0) == 0)
    def _():
        pieces = [(v, w_other, where[z] * v.shape[0]) for z, v in enumerate(far)]
        for z in range(shards):
            for k in range(places):
                start = (where[z] * places + where[shards + k]) * rows
                source = near[k].at[pl.ds(z * rows, rows)]
                pieces.append((source.at[:, :width], w_x, start))
                if not far:
                    pieces.append((source.at[:, width:], w_other, start))
        piece_copies(pieces, sems)

    norm = lax.rsqrt(jnp.mean(hidden * hidden, axis=1, keepdims=True) + EPSILON)
    lowered = (hidden * norm * gain[0:1]).astype(BF16)
    u_ref[...] = lowered
    turned_ref[...] = lowered.T
    x_ref[...] = dot(lowered, w_x[...]).astype(BF16)
    made = dot(lowered, w_other[...])
    bc_ref[...] = made[:, :both].astype(BF16)
    dt_ref[...] = made[:, both:]


def gated_scale(p_ref, q_ref, model, inner_total):
    squares = p_ref[:, model:].astype(F32) + q_ref[:, model:].astype(F32)
    return lax.rsqrt((squares[:, 0:1] + squares[:, 1:2]) / inner_total + EPSILON)


def block_of(part):
    array, width, index = part
    return (array, (array.shape[0], width), lambda *_: (0, index))


def enter(where, shards, near, far, hidden, parts, gain, width, both, inner_total):
    rows, model = hidden.shape
    first = parts is None
    block = min(256, rows)
    wide = (block, model)
    ins = [(v, None, None) for v in near + far] + [(hidden, wide, rows_at)]
    outs = []
    if not first:
        ins += [(part, (block, model + LANES), rows_at) for part in parts]
        outs.append(((rows, model), F32, wide, rows_at))
    ins += [(gain, gain.shape, fixed)]
    outs += [
        ((rows, model), BF16, wide, rows_at),
        ((model, rows), BF16, (model, block), columns_at),
        ((rows, width), BF16, (block, width), rows_at),
        ((rows, both), BF16, (block, both), rows_at),
        ((rows, LANES), F32, (block, LANES), rows_at),
    ]
    outs += [((model, v), BF16, (model, v), fixed) for v in (width, both + LANES)]
    scratch = [pltpu.SemaphoreType.DMA((shards * (2 * len(near)),))]
    cuts = (shards, len(near), near[0].shape[0] // shards)
    made = call(
        functools.partial(enter_body, first, inner_total, cuts), (rows // block,), ins, outs, scratch, where, name="enter"
    )
    return [hidden] + list(made) if first else list(made)


def states_body(
    x_ref, raw_bc_ref, dt_ref, before_ref, gain_ref, w_x, w_other, cols_ref, taps_ref, taps_bc_ref, head_ref,
    spread_ref, lower_ref, edge_ref, before_turned, xc_ref, bc_ref, step_ref, cum_ref, enter_ref, phi_ref, last_ref,
    tail_x, tail_bc, state, phi,
):
    chunk = pl.program_id(0)
    width = x_ref.shape[1]
    ns = raw_bc_ref.shape[1] // 2

    @pl.when(chunk == 0)
    def _():
        before = before_ref[...].astype(F32)
        norm = lax.rsqrt(jnp.mean(before * before, axis=1, keepdims=True) + EPSILON)
        lowered = (before * norm * gain_ref[0:1]).astype(BF16)
        padding = jnp.zeros((LANES - EDGE, lowered.shape[1]), F32)
        before_turned[...] = jnp.concatenate([lowered.astype(F32), padding], axis=0).T.astype(BF16)
        edge = dot(lowered, w_x[...]).astype(BF16)
        edge_bc = dot(lowered, w_other[:, : 2 * ns]).astype(BF16)
        edge_ref[:, :width] = edge
        edge_ref[:, width:] = edge_bc
        tail_x[...] = edge.astype(F32)
        tail_bc[...] = edge_bc.astype(F32)
        state[...] = jnp.zeros_like(state)
        phi[...] = jnp.ones_like(phi)

    for sub, here in enumerate(chunks_of(x_ref)):
        cols = cols_ref[here]
        same = same_columns(cols, LANES)
        dt = jax.nn.softplus(dt_ref[here] + head_ref[0:1]) * cols[:, 3:4]
        rates = head_ref[1:2] * dt
        cum = dot(lower_ref[...], rates, precision=EXACT)
        step_ref[here] = dt
        cum_ref[here] = cum
        size = cum.shape[0]
        tail_dt = cols[:, 5:6] * jnp.exp(cum[size - 1 : size] - cum) * dt
        fold = cols[size - 1 : size, 4:5] * jnp.exp(cum[size - EDGE : size])[EDGE - 1 : EDGE]
        fold_rows = jnp.broadcast_to(fold, phi.shape)
        wide = expand(jnp.concatenate([tail_dt, fold_rows], axis=0), spread_ref[...])

        halves = []
        for i in range(2):
            part = slice(i * ns, (i + 1) * ns)
            now = raw_bc_ref[here, part].astype(F32)
            shifts = conv_shifts(jnp.concatenate([tail_bc[:, part], now], axis=0), same)
            tail_bc[:, part] = now[size - EDGE :]
            halves.append(silu_parts(conv_sum(shifts, taps_bc_ref[:, part]))[1].astype(BF16))
            bc_ref[here, part] = halves[i]
        b_turned = halves[0].astype(F32).T.astype(BF16)

        enter_ref[sub] = state[...].astype(BF16)
        phi_ref[sub] = phi[...]
        for i in range(width // LANES):
            part = slice(i * LANES, (i + 1) * LANES)
            now = x_ref[here, part].astype(F32)
            shifts = conv_shifts(jnp.concatenate([tail_x[:, part], now], axis=0), same)
            tail_x[:, part] = now[size - EDGE :]
            x_conv = silu_parts(conv_sum(shifts, taps_ref[:, part]))[1].astype(BF16)
            xc_ref[here, part] = x_conv
            held = (x_conv.astype(F32) * wide[:size, part]).astype(BF16)
            state[:, part] = wide[size : size + 1, part] * state[:, part] + dot(b_turned, held)
        phi[...] = phi[...] * fold_rows

    @pl.when(chunk == pl.num_programs(0) - 1)
    def _():
        last_ref[:ns] = state[...].astype(BF16)
        last_ref[ns:] = expand(phi[...], spread_ref[...]).astype(BF16)


def states(x_raw, raw_bc, dt_raw, before, gain, weights, cols, taps, taps_bc, head, spread, lower):
    rows, width = x_raw.shape
    ns = raw_bc.shape[1] // 2
    count = rows // CHUNK
    block = min(256, rows)
    subs = block // CHUNK
    ins = [
        (x_raw, (block, width), rows_at),
        (raw_bc, (block, 2 * ns), rows_at),
        (dt_raw, (block, LANES), rows_at),
        (before, before.shape, fixed),
        (gain, gain.shape, fixed),
        block_of(weights["x"]),
        block_of(weights["other"]),
        (cols, (block, cols.shape[1]), rows_at),
        (taps, taps.shape, fixed),
        (taps_bc, taps_bc.shape, fixed),
        (head, head.shape, fixed),
        (spread, spread.shape, fixed),
        (lower, lower.shape, fixed),
    ]
    outs = [
        ((EDGE, width + 2 * ns), BF16, (EDGE, width + 2 * ns), fixed),
        ((before.shape[1], LANES), BF16, (before.shape[1], LANES), fixed),
        ((rows, width), BF16, (block, width), rows_at),
        ((rows, 2 * ns), BF16, (block, 2 * ns), rows_at),
        ((rows, LANES), F32, (block, LANES), rows_at),
        ((rows, LANES), F32, (block, LANES), rows_at),
        ((count, ns, width), BF16, (subs, ns, width), lambda i, *_: (i, 0, 0)),
        ((count, EDGE, LANES), F32, (subs, EDGE, LANES), lambda i, *_: (i, 0, 0)),
        ((ns + EDGE, width), BF16, (ns + EDGE, width), fixed),
    ]
    scratch = [
        pltpu.VMEM((EDGE, width), F32),
        pltpu.VMEM((EDGE, 2 * ns), F32),
        pltpu.VMEM((ns, width), F32),
        pltpu.VMEM((EDGE, LANES), F32),
    ]
    return call(states_body, (rows // block,), ins, outs, scratch, flops=2 * rows * width * ns * 4, name="states")


def within_body(xc_ref, bc_ref, step_ref, cum_ref, cols_ref, segs_ref, spread_ref, y_ref):
    ns = bc_ref.shape[1] // 2
    width = xc_ref.shape[1]
    for here in chunks_of(y_ref):
        cum = cum_ref[here]
        cum_rows = cum.T
        bias = pairs_bias(cols_ref[here, 7:8], segs_ref[0:1, here], True)
        both = dot(bc_ref[here, ns:], bc_ref[here, :ns], ((1,), (1,)))
        step_wide = expand(step_ref[here], spread_ref[...])
        for pair in range(width // LANES):
            part = slice(pair * LANES, (pair + 1) * LANES)
            weighted = (xc_ref[here, part].astype(F32) * step_wide[:, part]).astype(BF16)
            maps = []
            for head in (2 * pair, 2 * pair + 1):
                gap = (cum[:, head : head + 1] - cum_rows[head : head + 1]) + bias
                maps.append((jnp.exp(gap) * both).astype(BF16))
            y_ref[here, part] = dot(jnp.concatenate(maps, axis=1), pair_masked(weighted))


def within(xc, bc, step, cum, cols, segs, spread):
    rows, width = xc.shape
    block = min(512, rows)
    ins = [
        (xc, (block, width), rows_at),
        (bc, (block, bc.shape[1]), rows_at),
        (step, (block, LANES), rows_at),
        (cum, (block, LANES), rows_at),
        (cols, (block, cols.shape[1]), rows_at),
        (segs, (EDGE, block), columns_at),
        (spread, spread.shape, fixed),
    ]
    outs = [((rows, width), F32, (block, width), rows_at)]
    return call(within_body, (rows // block,), ins, outs, name="within")[0]


def leave_body(count, *refs):
    payloads, refs = refs[:count], refs[count:]
    (w_gate, w_out, y_ref, low_ref, xc_ref, bc_ref, cum_ref, cols_ref, enter_ref, phi_ref, rows_ref, spread_ref) = refs[:12]
    ssm_ref, gate_ref, p_ref, in_ref, normed = refs[12:]
    ns = in_ref.shape[0]
    width = xc_ref.shape[1]
    spread = spread_ref[...]

    @pl.when(pl.program_id(0) == 0)
    def _():
        in_ref[...] = folded([p[...] for p in payloads])

    gate_ref[...] = dot(low_ref[...], w_gate[...])
    for sub in range(y_ref.shape[0] // CHUNK):
        here = slice(sub * CHUNK, (sub + 1) * CHUNK)
        phi_wide = expand(phi_ref[sub], spread)[0:1]
        begun = (enter_ref[sub].astype(F32) + phi_wide * in_ref[...]).astype(BF16)
        carried = cols_ref[here, 4:5] * jnp.exp(cum_ref[here])
        carried_wide = expand(carried, spread)
        far = dot(bc_ref[here, ns:], begun)
        ssm_ref[here] = y_ref[here] + carried_wide * far
    total = jnp.zeros((y_ref.shape[0], LANES), F32)
    for i in range(width // LANES):
        part = slice(i * LANES, (i + 1) * LANES)
        mixed = ssm_ref[:, part] + rows_ref[1:2, part] * xc_ref[:, part].astype(F32)
        gated = mixed * silu_parts(gate_ref[:, part])[1]
        total = total + gated * gated
        normed[:, part] = (gated * rows_ref[0:1, part]).astype(BF16)
    high, rest = split(jnp.broadcast_to(jnp.sum(total, axis=1, keepdims=True), total.shape))
    lane = lax.broadcasted_iota(jnp.int32, total.shape, 1)
    model = w_out.shape[0]
    p_ref[:, :model] = dot(normed[...], w_out[...], ((1,), (1,))).astype(BF16)
    p_ref[:, model:] = jnp.where(lane == 0, high.astype(F32), rest.astype(F32)).astype(BF16)


def leave(payloads, y_in, low, xc, bc, cum, cols, entered, phi, rowpack, spread, weights):
    rows, width = xc.shape
    model = low.shape[1]
    ns = bc.shape[1] // 2
    block = min(256, rows)
    subs = block // CHUNK
    ins = [(p, p.shape, fixed) for p in payloads]
    ins += [
        block_of(weights["gate"]),
        block_of(weights["out"]),
        (y_in, (block, width), rows_at),
        (low, (block, model), rows_at),
        (xc, (block, width), rows_at),
        (bc, (block, bc.shape[1]), rows_at),
        (cum, (block, LANES), rows_at),
        (cols, (block, cols.shape[1]), rows_at),
        (entered, (subs, ns, width), lambda i, *_: (i, 0, 0)),
        (phi, (subs, EDGE, LANES), lambda i, *_: (i, 0, 0)),
        (rowpack, rowpack.shape, fixed),
        (spread, spread.shape, fixed),
    ]
    outs = [
        ((rows, width), F32, (block, width), rows_at),
        ((rows, width), F32, (block, width), rows_at),
        ((rows, model + LANES), BF16, (block, model + LANES), rows_at),
        ((ns, width), F32, (ns, width), fixed),
    ]
    scratch = [pltpu.VMEM((block, width), BF16)]
    return call(functools.partial(leave_body, len(payloads)), (rows // block,), ins, outs, scratch, name="leave")


def back_gate_body(
    inner_total, ends, *refs
):
    if ends:
        hidden_ref, refs = refs[0], refs[1:]
        output_ref, refs = refs[14], refs[:14] + refs[15:]
    (
        up_ref, p_ref, q_ref, ssm_ref, xc_ref, gate_ref, bc_ref, cum_ref, cols_ref, phi_ref,
        factor_ref, rows_ref, spread_ref, w_ref,
        do_ref, dy_ref, dgate_ref, n_ref, gain_ref, out_ref, state,
    ) = refs
    step = pl.program_id(0)
    ns = state.shape[0]
    width = xc_ref.shape[1]
    spread = spread_ref[...]

    @pl.when(step == 0)
    def _():
        gain_ref[...] = jnp.zeros_like(gain_ref)
        state[...] = jnp.zeros_like(state)

    model = up_ref.shape[1]
    scale = gated_scale(p_ref, q_ref, model, inner_total)
    up = up_ref[...].astype(BF16)
    do_ref[...] = up.T
    summed = p_ref[:, :model].astype(F32) + q_ref[:, :model].astype(F32)
    if ends:
        output_ref[...] = hidden_ref[...].astype(F32) + scale * summed
    spread_sum = jnp.sum(up.astype(F32) * summed, axis=1, keepdims=True)
    pull = scale * scale * scale * spread_sum / inner_total
    scale_wide = jnp.broadcast_to(scale, (scale.shape[0], LANES))
    pull_wide = jnp.broadcast_to(pull, scale_wide.shape)
    back = dot(up, w_ref[...])
    for i in range(width // LANES):
        part = slice(i * LANES, (i + 1) * LANES)
        gain = rows_ref[0:1, part]
        gate = gate_ref[:, part]
        sig, soft = silu_parts(gate)
        mixed = ssm_ref[:, part] + rows_ref[1:2, part] * xc_ref[:, part].astype(F32)
        gated = mixed * soft
        scaled = gated * scale_wide
        grad = back[:, part]
        gain_ref[6:7, part] += jnp.sum(grad * scaled, axis=0, keepdims=True)
        grad_gated = grad * gain * scale_wide - gated * pull_wide
        dy_ref[:, part] = (grad_gated * soft).astype(BF16)
        dgate_ref[:, part] = (grad_gated * mixed * (sig * (1.0 + gate * (1.0 - sig)))).astype(BF16)
        n_ref[:, part] = (scaled * gain).astype(BF16)
    for sub in range(up_ref.shape[0] // CHUNK):
        here = slice(sub * CHUNK, (sub + 1) * CHUNK)
        phi_wide = expand(phi_ref[sub], spread)[0:1]
        carried_wide = expand(cols_ref[here, 4:5] * jnp.exp(cum_ref[here]), spread)
        c_turned = bc_ref[here, ns:].astype(F32).T.astype(BF16)
        carried_dy = (dy_ref[here].astype(F32) * carried_wide).astype(BF16)
        state[...] += phi_wide * dot(c_turned, carried_dy)

    @pl.when(step == pl.num_programs(0) - 1)
    def _():
        out_ref[:ns] = state[...].astype(BF16)
        out_ref[ns:] = factor_ref[...]


def back_gate(up, parts, ssm, xc, gate, bc, cum, cols, phi, ended, rowpack, spread, weights, inner_total, hidden=None):
    rows, width = xc.shape
    model = up.shape[1]
    ns = bc.shape[1] // 2
    block = min(256, rows)
    subs = block // CHUNK
    wide = (block, model)
    ins = [
        (up, wide, rows_at),
        (parts[0], (block, model + LANES), rows_at),
        (parts[1], (block, model + LANES), rows_at),
        (ssm, (block, width), rows_at),
        (xc, (block, width), rows_at),
        (gate, (block, width), rows_at),
        (bc, (block, 2 * ns), rows_at),
        (cum, (block, LANES), rows_at),
        (cols, (block, cols.shape[1]), rows_at),
        (phi, (subs, EDGE, LANES), lambda i, *_: (i, 0, 0)),
        (ended, (EDGE, width), lambda i, *_: (ns // EDGE, 0)),
        (rowpack, rowpack.shape, fixed),
        (spread, spread.shape, fixed),
        block_of(weights["out"]),
    ]
    outs = [
        ((model, rows), BF16, (model, block), columns_at),
        ((rows, width), BF16, (block, width), rows_at),
        ((rows, width), BF16, (block, width), rows_at),
        ((rows, width), BF16, (block, width), rows_at),
        ((EDGE, width), F32, (EDGE, width), fixed),
        ((ns + EDGE, width), BF16, (ns + EDGE, width), fixed),
    ]
    if hidden is not None:
        ins = [(hidden, wide, rows_at)] + ins
        outs = [((rows, model), F32, wide, rows_at)] + outs
    scratch = [pltpu.VMEM((ns, width), F32)]
    return call(
        functools.partial(back_gate_body, inner_total, hidden is not None), (rows // block,), ins, outs, scratch,
        flops=2 * rows * width * model * 1.3, name="back_gate",
    )


def back_within_body(
    xc_ref, bc_ref, step_ref, cum_ref, cols_ref, segs_ref, spread_ref, gather_ref, dy_ref, ssm_ref,
    dx_ref, left_ref, dbc_ref, products,
):
    ns = bc_ref.shape[1] // 2
    size, width = CHUNK, xc_ref.shape[1]
    for here in chunks_of(xc_ref):
        cum = cum_ref[here]
        cum_rows = cum.T
        bias = pairs_bias(cols_ref[here, 7:8], segs_ref[0:1, here], False)
        b_part = bc_ref[here, :ns]
        c_part = bc_ref[here, ns:]
        both = dot(b_part, c_part, ((1,), (1,)))
        step_wide = expand(step_ref[here], spread_ref[...])
        grad_both = jnp.zeros((size, size), F32)
        for pair in range(width // LANES):
            part = slice(pair * LANES, (pair + 1) * LANES)
            weighted = (xc_ref[here, part].astype(F32) * step_wide[:, part]).astype(BF16)
            dy = dy_ref[here, part]
            dy_pair = pair_masked(dy)
            grad_maps = dot(weighted, dy_pair, ((1,), (1,)))
            maps = []
            for k in (0, 1):
                head = 2 * pair + k
                decay = jnp.exp((cum_rows[head : head + 1] - cum[:, head : head + 1]) + bias)
                maps.append((decay * both).astype(BF16))
                grad_both = grad_both + decay * grad_maps[:, k * size : (k + 1) * size]
            grad_x = dot(jnp.concatenate(maps, axis=1), dy_pair)
            dx_ref[here, part] = grad_x.astype(BF16)
            high, rest = split(dy.astype(F32) * ssm_ref[here, part] - weighted.astype(F32) * grad_x)
            products[:size, part] = high
            products[size:, part] = rest
        left = dot(products[...], gather_ref[...])
        left_ref[here] = left[:size] + left[size:]
        dbc_ref[here, :ns] = dot(grad_both.astype(BF16), c_part)
        dbc_ref[here, ns:] = dot(grad_both.T.astype(BF16), b_part)


def back_within(xc, bc, step, cum, cols, segs, spread, gather, dy, ssm):
    rows, width = xc.shape
    block = min(256, rows)
    ins = [
        (xc, (block, width), rows_at),
        (bc, (block, bc.shape[1]), rows_at),
        (step, (block, LANES), rows_at),
        (cum, (block, LANES), rows_at),
        (cols, (block, cols.shape[1]), rows_at),
        (segs, (EDGE, block), columns_at),
        (spread, spread.shape, fixed),
        (gather, gather.shape, fixed),
        (dy, (block, width), rows_at),
        (ssm, (block, width), rows_at),
    ]
    outs = [
        ((rows, width), BF16, (block, width), rows_at),
        ((rows, LANES), F32, (block, LANES), rows_at),
        ((rows, bc.shape[1]), F32, (block, bc.shape[1]), rows_at),
    ]
    scratch = [pltpu.VMEM((2 * CHUNK, width), BF16)]
    return call(back_within_body, (rows // block,), ins, outs, scratch, name="back_within")


def conv_back(ext, same, taps, grad_conv, next_rows):
    size = ext.shape[0] - EDGE
    shifts = conv_shifts(ext, same)
    pre = conv_sum(shifts, taps)
    sig = jax.nn.sigmoid(pre)
    grad_pre = grad_conv * (sig * (1.0 + pre * (1.0 - sig)))
    sums = [jnp.sum(grad_pre * shifts[lag], axis=0, keepdims=True) for lag in range(4)]
    sums.append(jnp.sum(grad_pre, axis=0, keepdims=True))
    zero = jnp.zeros((EDGE, ext.shape[1]), F32)
    length = size + 2 * EDGE
    raw = taps[0:1] * jnp.concatenate([zero, grad_pre], axis=0)
    firsts = []
    for lag in (1, 2, 3):
        term = grad_pre * same[lag] * taps[lag : lag + 1]
        firsts.append(term[:EDGE])
        padded = jnp.concatenate([zero, term, next_rows[lag - 1]], axis=0)
        raw = raw + pltpu.roll(padded, length - lag, 0)[: size + EDGE]
    return raw, firsts, sums


def back_inter_body(count_in, flag, *refs):
    payloads, refs = refs[:count_in], refs[count_in:]
    (
        x_ref, before_ref, edge_ref, xc_ref, bc_ref, step_ref, cum_ref, cols_ref, dt_ref, dy_ref, dxi_ref,
        left_ref, dbci_ref, enter_ref, phi_ref, in_ref, taps_ref, head_ref, rows_ref, spread_ref, gather_ref, sums_ref,
        dx_ref, last_ref, prior_ref, mine_ref, theirs_ref, ddt_ref, conv_ref, heads_ref,
        grad_state, next_rows, wide, far, carried, held, begun, ending, products,
    ) = refs
    step = pl.program_id(0)
    first_block = step == pl.num_programs(0) - 1
    ns = in_ref.shape[0]
    size, width = CHUNK, xc_ref.shape[1]

    @pl.when(step == 0)
    def _():
        grad_state[...] = folded([p[...] for p in payloads])
        next_rows[...] = jnp.zeros_like(next_rows)
        conv_ref[...] = jnp.zeros_like(conv_ref)
        heads_ref[...] = jnp.zeros_like(heads_ref)

    subs = len(chunks_of(xc_ref))
    for sub, here in reversed(list(enumerate(chunks_of(xc_ref)))):
        cols = cols_ref[here]
        same = same_columns(cols, LANES)
        cum = cum_ref[here]
        dt = step_ref[here]
        decay_in = cols[:, 4:5] * jnp.exp(cum)
        decay_out = cols[:, 5:6] * jnp.exp(cum[size - 1 : size] - cum)
        fold_rows = jnp.broadcast_to(decay_in[size - EDGE : size][EDGE - 1 : EDGE], (EDGE, LANES))
        b_part = bc_ref[here, :ns]
        c_part = bc_ref[here, ns:]
        c_turned = c_part.astype(F32).T.astype(BF16)
        stacked = jnp.concatenate([decay_in, decay_out, dt, fold_rows, phi_ref[sub]], axis=0)
        wide[...] = expand(stacked, spread_ref[...])
        fold_at = 3 * size
        for i in range(width // LANES):
            part = slice(i * LANES, (i + 1) * LANES)
            dy = dy_ref[here, part].astype(F32)
            weighted = xc_ref[here, part].astype(F32) * wide[2 * size : 3 * size, part]
            fold_wide = wide[fold_at : fold_at + 1, part]
            grad_end = grad_state[:, part]
            start = enter_ref[sub, :, part].astype(F32) + wide[fold_at + EDGE : fold_at + EDGE + 1, part] * in_ref[:, part]
            carried[:, part] = (dy * wide[:size, part]).astype(BF16)
            held[:, part] = (weighted * wide[size : 2 * size, part]).astype(BF16)
            begun[:, part] = start.astype(BF16)
            ending[:, part] = grad_end.astype(BF16)
            pass_sum = jnp.sum(start * grad_end, axis=0, keepdims=True) * fold_wide
            products[2 * size :, part] = jnp.broadcast_to(pass_sum, (2 * EDGE, LANES)).astype(BF16)
            grad_state[:, part] = fold_wide * grad_end
        far[...] = dot(b_part, ending[...])
        dbc_c = dbci_ref[here, ns:] + dot(carried[...], begun[...], ((1,), (1,)))
        dbc_b = dbci_ref[here, :ns] + dot(held[...], ending[...], ((1,), (1,)))
        grad_state[...] += dot(c_turned, carried[...])
        own_b = flag[0] == 0
        mine_ref[here] = jnp.where(own_b, dbc_b, dbc_c).astype(BF16)
        theirs_ref[here] = jnp.where(own_b, dbc_c, dbc_b).astype(BF16)

        for i in range(width // LANES):
            part = slice(i * LANES, (i + 1) * LANES)
            dy = dy_ref[here, part].astype(F32)
            x_conv = xc_ref[here, part].astype(F32)
            dt_wide = wide[2 * size : 3 * size, part]
            grad_far = wide[size : 2 * size, part] * far[:, part]
            grad_weighted = dxi_ref[here, part].astype(F32) + grad_far
            products[:size, part] = (x_conv * dt_wide * grad_far).astype(BF16)
            products[size : 2 * size, part] = (x_conv * grad_weighted).astype(BF16)
            conv_ref[5:6, part] += jnp.sum(dy * x_conv, axis=0, keepdims=True)
            grad_conv = dt_wide * grad_weighted + rows_ref[1:2, part] * dy
            if sub:
                ahead = x_ref[here.start - EDGE : here.start, part].astype(F32)
            else:
                ahead = jnp.where(first_block, edge_ref[:, part].astype(F32), before_ref[:, part].astype(F32))
            ext = jnp.concatenate([ahead, x_ref[here, part].astype(F32)], axis=0)
            raw, firsts, tap_sums = conv_back(
                ext, same, taps_ref[:, part], grad_conv, [next_rows[k, :, part] for k in range(3)]
            )
            for k in range(3):
                next_rows[k, :, part] = firsts[k]
            for k in range(5):
                conv_ref[k : k + 1, part] += tap_sums[k]
            dx_ref[here, part] = raw[EDGE:].astype(BF16)
            prior_ref[:, part] = raw[:EDGE]

            if sub == subs - 1:

                @pl.when(step == 0)
                def _(raw=raw, part=part):
                    last_ref[:, part] = raw[size:]

        per_head = dot(products[...], gather_ref[...])
        outward, direct, through = per_head[:size], per_head[size : 2 * size], per_head[2 * size : 2 * size + 1]
        grad_rate = dot(sums_ref[...], jnp.concatenate([left_ref[here], outward], axis=0), precision=EXACT) + through
        grad_dt = direct + head_ref[1:2] * grad_rate
        grad_raw = grad_dt * cols[:, 3:4] * jax.nn.sigmoid(dt_ref[here] + head_ref[0:1])
        ddt_ref[here] = grad_raw.astype(BF16)
        heads_ref[0:1] += jnp.sum(grad_raw, axis=0, keepdims=True)
        heads_ref[1:2] += jnp.sum(grad_rate * head_ref[1:2] * dt, axis=0, keepdims=True)


def back_inter(
    flag, payloads, x_raw, edge, xc, bc, step, cum, cols, dt_raw, dy, dx_in, left, dbc_in, entered, phi, state_in,
    taps, head, rowpack, spread, gather, sums,
):
    rows, width = xc.shape
    ns = bc.shape[1] // 2
    block = min(256, rows)
    subs = block // CHUNK
    count = rows // block

    def back(i, *_):
        return (count - 1 - i, 0)

    def back3(i, *_):
        return (count - 1 - i, 0, 0)

    def before(i, *_):
        return (jnp.maximum((count - 1 - i) * (block // EDGE) - 1, 0), 0)

    def at(width_now):
        return (block, width_now)

    ins = [(p, p.shape, fixed) for p in payloads] + [
        (x_raw, at(width), back),
        (x_raw, (EDGE, width), before),
        (edge, (EDGE, width), fixed),
        (xc, at(width), back),
        (bc, at(2 * ns), back),
        (step, at(LANES), back),
        (cum, at(LANES), back),
        (cols, at(cols.shape[1]), back),
        (dt_raw, at(LANES), back),
        (dy, at(width), back),
        (dx_in, at(width), back),
        (left, at(LANES), back),
        (dbc_in, at(2 * ns), back),
        (entered, (subs, ns, width), back3),
        (phi, (subs, EDGE, LANES), back3),
        (state_in, state_in.shape, fixed),
        (taps, taps.shape, fixed),
        (head, head.shape, fixed),
        (rowpack, rowpack.shape, fixed),
        (spread, spread.shape, fixed),
        (gather, gather.shape, fixed),
        (sums, sums.shape, fixed),
    ]
    outs = [
        ((rows, width), BF16, at(width), back),
        ((EDGE, width), F32, (EDGE, width), fixed),
        ((EDGE, width), F32, (EDGE, width), fixed),
        ((rows, ns), BF16, at(ns), back),
        ((rows, ns), BF16, at(ns), back),
        ((rows, LANES), BF16, at(LANES), back),
        ((EDGE, width), F32, (EDGE, width), fixed),
        ((EDGE, LANES), F32, (EDGE, LANES), fixed),
    ]
    scratch = [
        pltpu.VMEM((ns, width), F32),
        pltpu.VMEM((3, EDGE, width), F32),
        pltpu.VMEM((3 * CHUNK + 2 * EDGE, width), F32),
        pltpu.VMEM((CHUNK, width), F32),
        pltpu.VMEM((CHUNK, width), BF16),
        pltpu.VMEM((CHUNK, width), BF16),
        pltpu.VMEM((ns, width), BF16),
        pltpu.VMEM((ns, width), BF16),
        pltpu.VMEM((2 * CHUNK + 2 * EDGE, width), BF16),
    ]
    return call(
        functools.partial(back_inter_body, len(payloads)), (count,), ins, outs, scratch, flag, name="back_inter"
    )


def back_bc_body(
    flag, raw_ref, edge_ref, cols_ref, taps_ref, mine_ref, theirs_ref, ddt_ref, out_ref, last_ref, prior_ref, sums_ref
):
    size, width = raw_ref.shape
    same = same_columns(cols_ref[...], width)
    ext = jnp.concatenate([edge_ref[...].astype(F32), raw_ref[...].astype(F32)], axis=0)
    grad = mine_ref[...].astype(F32) + theirs_ref[...].astype(F32)
    zero = jnp.zeros((EDGE, width), F32)
    raw, _, sums = conv_back(ext, same, taps_ref[...], grad, [zero] * 3)
    out_ref[:, :width] = raw[EDGE:].astype(BF16)
    out_ref[:, width:] = ddt_ref[...]
    last_ref[...] = raw[size:]
    prior_ref[:, :width] = raw[:EDGE]
    prior_ref[:, width:] = jnp.zeros((EDGE, ddt_ref.shape[1]), F32)
    sums_ref[...] = jnp.concatenate(sums + [zero[:3]], axis=0)


def back_bc(flag, raw, edge, cols, taps, mine, theirs, ddt):
    rows, ns = mine.shape
    joined = ns + ddt.shape[1]
    before = edge.shape[1] // ns - 2
    ins = [
        (raw, (rows, ns), lambda i, t: (0, t[0])),
        (edge, (EDGE, ns), lambda i, t: (0, before + t[0])),
        (cols, cols.shape, fixed),
        (taps, (EDGE, ns), lambda i, t: (0, t[0])),
        (mine, mine.shape, fixed),
        (theirs, theirs.shape, fixed),
        (ddt, ddt.shape, fixed),
    ]
    outs = [((rows, joined), BF16, (rows, joined), fixed)]
    outs += [((EDGE, v), F32, (EDGE, v), fixed) for v in (ns, joined, ns)]
    return call(back_bc_body, (1,), ins, outs, (), flag, name="back_bc")


def back_low_body(
    flag, gate_ref, x_ref, small_ref, last_x, last_bc, back_ref, wg_ref, wx_ref, wb_ref, wt_ref, out_ref
):
    ns = last_bc.shape[1]

    def product(gate, x, bc, dt):
        over = ((1,), (1,))
        total = dot(gate, wg_ref[...], over) + dot(x, wx_ref[...], over)
        return (total + dot(bc, wb_ref[...], over) + dot(dt, wt_ref[...], over)).astype(BF16)

    out_ref[...] = product(gate_ref[...], x_ref[...], small_ref[:, :ns], small_ref[:, ns:])

    @pl.when(pl.program_id(0) == pl.num_programs(0) - 1)
    def _():
        size, width = x_ref.shape
        end = slice(size - 2 * EDGE, size)

        def righted(value, last, back):
            kept = value.astype(F32)[:EDGE]
            return jnp.concatenate([kept, last[...] + back], axis=0).astype(BF16)

        x = righted(x_ref[end], last_x, back_ref[:, :width])
        bc = righted(small_ref[end, :ns], last_bc, back_ref[:, width : width + ns])
        out_ref[end] = product(gate_ref[end], x, bc, small_ref[end, ns:])


def back_low(flag, dgate, dx, small, last_x, last_bc, back_rows, weights):
    rows, width = dx.shape
    ns = last_bc.shape[1]
    array, first = weights["lanes"]
    model = array.shape[0]
    block = min(256, rows)
    ins = [(v, (block, v.shape[1]), rows_at) for v in (dgate, dx, small)]
    ins += [(v, v.shape, fixed) for v in (last_x, last_bc, back_rows)]
    ins += [
        block_of(weights["gate"]),
        block_of(weights["x"]),
        (array, (model, ns), lambda i, t: (0, first + t[0])),
        block_of((array, LANES, first + 2)),
    ]
    outs = [((rows, model), BF16, (block, model), rows_at)]
    return call(
        back_low_body, (rows // block,), ins, outs, (), flag, flops=2 * rows * model * (2 * width + 256), name="back_low"
    )[0]


def back_norm_body(up_ref, a_ref, b_ref, h_ref, gain_ref, out_ref, sum_ref):
    @pl.when(pl.program_id(0) == 0)
    def _():
        sum_ref[...] = jnp.zeros_like(sum_ref)

    hidden = h_ref[...].astype(F32)
    grad = a_ref[...].astype(F32) + b_ref[...].astype(F32)
    model = hidden.shape[1]
    norm = lax.rsqrt(jnp.mean(hidden * hidden, axis=1, keepdims=True) + EPSILON)
    normed = hidden * norm
    sum_ref[7:8] += jnp.sum(grad * normed, axis=0, keepdims=True)
    gained = grad * gain_ref[0:1]
    inner = jnp.sum(gained * normed, axis=1, keepdims=True) / model
    out_ref[...] = up_ref[...].astype(F32) + norm * (gained - normed * inner)


def back_norm(up, a, b, hidden, gain):
    rows, model = hidden.shape
    block = min(256, rows)
    wide = (block, model)
    ins = [(v, wide, rows_at) for v in (up, a, b, hidden)] + [(gain, gain.shape, fixed)]
    outs = [((rows, model), F32, wide, rows_at), ((EDGE, model), F32, (EDGE, model), fixed)]
    return call(back_norm_body, (rows // block,), ins, outs, name="back_norm")


def weight_grad_body(places, shards, cuts, owners, ahead, where, *refs):
    count = max(owners) + 1
    lefts, refs = refs[:count], refs[count:]
    factors, refs = refs[: len(cuts)], refs[len(cuts) :]
    if ahead:
        before, priors, refs = refs[0], refs[1 : 1 + len(cuts)], refs[1 + len(cuts) :]
    outs, scratch = refs[:places], refs[places:]
    model = lefts[0].shape[0]
    part = model // places
    rows = part // shards
    step = pl.program_id(0)
    if shards > 1:

        @pl.when(step == 0)
        def _():
            for source, ordered in zip(([lefts[0], before] if ahead else [lefts[0]]), scratch):
                for k in range(places):
                    for z in range(shards):
                        at = pl.ds(pl.multiple_of((z * places + where[k]) * rows, rows), rows)
                        ordered[k * part + z * rows : k * part + (z + 1) * rows] = source[at]

    for i, (factor, owner, (start, end)) in enumerate(zip(factors, owners, cuts)):

        @pl.when((step >= start) & (step < end))
        def _(i=i, factor=factor, owner=owner):
            if ahead:
                prior = priors[i][...]
                empty = jnp.zeros((LANES - EDGE, prior.shape[1]), F32)
                prior = jnp.concatenate([prior, empty], axis=0).astype(BF16)
            for k in range(places):
                if places == 1:
                    at = slice(None)
                elif shards == 1:
                    at = pl.ds(pl.multiple_of(where[k] * part, part), part)
                else:
                    at = slice(k * part, (k + 1) * part)
                made = dot((scratch[0] if shards > 1 else lefts[owner])[at], factor[...])
                if ahead:
                    made = made + dot((scratch[1] if shards > 1 else before)[at], prior)
                outs[k][...] = made.astype(BF16)


def weight_grad(where, places, shards, products, ahead=None):
    model, rows = products[0][0].shape
    tile = 512 if all(b.shape[1] % 512 == 0 for _, factors in products for b in factors) else 256
    cuts, owners, ins, at = [], [], [], 0
    for i, (a, factors) in enumerate(products):
        ins.append((a, a.shape, fixed))
        for b in factors:
            cuts.append((at, at + b.shape[1] // tile))
            owners.append(i)
            at = cuts[-1][1]

    def columns_of(arrays):
        return [
            (b, (b.shape[0], tile), lambda i, *_, s=start, e=end: (0, jnp.clip(i - s, 0, e - s - 1)))
            for b, (start, end) in zip(arrays, cuts)
        ]

    ins += columns_of([b for _, factors in products for b in factors])
    if ahead:
        ins += [(ahead[0], ahead[0].shape, fixed)] + columns_of(ahead[1])
    width = at * tile
    part = model // places
    outs = [((part, width), BF16, (part, tile), columns_at)] * places
    scratch = []
    if shards > 1:
        scratch = [pltpu.VMEM((model, rows), BF16)] + ([pltpu.VMEM((model, LANES), BF16)] if ahead else [])
    return call(
        functools.partial(weight_grad_body, places, shards, cuts, owners, bool(ahead)), (at,), ins, outs, scratch, where,
        name="weight_grad",
    )


def relative(value, axis, by):
    size = lax.axis_size(axis)
    return lax.ppermute(value, axis, [(i, i ^ by) for i in range(size)])


def shifted(value, axis, by):
    size = lax.axis_size(axis)
    return lax.ppermute(value, axis, [(i, i + by) for i in range(size) if 0 <= i + by < size])


def tree_sum(values):
    while len(values) > 1:
        values = [a + b for a, b in zip(values[0::2], values[1::2])]
    return values[0]


def cut_body(joined, where, zx_ref, wbc_ref, wdt_ref, down_ref, *refs):
    width = zx_ref.shape[3]
    both, heads = wbc_ref.shape[2], wdt_ref.shape[2]
    rest, main, turned = refs[0], refs[1], refs[-1]
    other, at = (main, width) if joined else (refs[2], 0)
    rows = main.shape[0]
    main[:, :width] = zx_ref[0, :, 1]
    other[:, at : at + both] = wbc_ref[0]
    other[:, at + both :] = jnp.zeros((other.shape[0], LANES), BF16)
    other[:, at + both : at + both + heads] = wdt_ref[0]
    turned[...] = down_ref[0].astype(F32).T
    rest[:, :width] = zx_ref[0, :, 0]
    rest[:, width:] = turned[pl.ds(pl.multiple_of(where[0] * rows, rows), rows)].astype(BF16)


def cut_rows(layer, joined, place, rows, w_zx, w_bc, w_dt, w_out):
    local, _, width = w_zx.shape[1:]
    extra = w_bc.shape[2] + LANES
    taken = rows if joined else local
    ins = [(w_zx, (1, rows, 2, width), lambda i, c: (layer, c[0], 0, 0))]
    ins += [(v, (1, taken, v.shape[2]), lambda i, c: (layer, c[0] if joined else 0, 0)) for v in (w_bc, w_dt)]
    ins += [(w_out, (1,) + w_out.shape[1:], lambda i, c: (layer, 0, 0))]
    shapes = [(rows, 2 * width)] + ([(rows, width + extra)] if joined else [(rows, width), (local, extra)])
    outs = [(shape, BF16, shape, fixed) for shape in shapes]
    scratch = [pltpu.VMEM((local, width), F32)]
    return call(functools.partial(cut_body, joined), (1,), ins, outs, scratch, place, name="cut")


def gather_rows(piece):
    return lax.all_gather(piece, ("shard", "ctx"), axis=0, tiled=True)


def gather_shard(piece):
    return jnp.concatenate([piece] + [relative(piece, "shard", k) for k in range(1, lax.axis_size("shard"))], axis=0)


def gather_ctx(along):
    return [along] + [relative(along, "ctx", k) for k in range(1, lax.axis_size("ctx"))]


def gather_far(piece):
    return [piece] + [relative(piece, "shard", k) for k in range(1, lax.axis_size("shard"))]


def near_rows(pieces):
    return [pieces[0]] + [relative(p, "ctx", k) for k, p in enumerate(pieces) if k]


def split_sum_body(counts, where, *refs):
    arrays, outs = refs[: sum(counts)], refs[sum(counts) :]
    rows = outs[0].shape[0]
    for k, out in enumerate(outs):
        at = pl.ds(pl.multiple_of(where[k] * rows, rows), rows)
        done, column = 0, 0
        for count in counts:
            total = tree_sum([v[at].astype(F32) for v in arrays[done : done + count]])
            out[:, column : column + total.shape[1]] = total.astype(out.dtype)
            done, column = done + count, column + total.shape[1]


def split_sum(order, parts, groups):
    ins = [(v, v.shape, fixed) for group in groups for v in group]
    shape = (groups[0][0].shape[0] // parts, sum(group[0].shape[1] for group in groups))
    outs = [(shape, BF16 if k else F32, shape, fixed) for k in range(parts)]
    counts = [len(group) for group in groups]
    return call(functools.partial(split_sum_body, counts), (1,), ins, outs, (), order, name="split_sum")


def scattered(pieces, axis):
    return [pieces[0]] + [relative(pieces[k], axis, k) for k in range(1, len(pieces))]


def finish_body(counts, *refs):
    zx_ref, out_ref, small_ref = refs[-3:]
    layers, width = zx_ref.shape[0], zx_ref.shape[3]
    late = tree_sum([v[...].astype(F32) for v in refs[sum(counts) : -3]])
    span = late.shape[1] // layers
    for layer, count in enumerate(counts):
        early = tree_sum([v[...].astype(F32) for v in refs[:count]])
        refs = refs[count:]
        zx_ref[layer, :, 0] = early[:, :width]
        zx_ref[layer, :, 1] = late[:, layer * span : layer * span + width]
        out_ref[layer] = early[:, width:]
        small_ref[layer] = late[:, layer * span + width : (layer + 1) * span]


def finish(early, late, width):
    layers = len(early)
    rows, span = late[0].shape
    ins = [(v, v.shape, fixed) for parts in list(early) + [late] for v in parts]
    shapes = [(layers, rows, 2, width), (layers, rows, width), (layers, rows, span // layers - width)]
    outs = [(v, F32, v, lambda *_, n=len(v): (0,) * n) for v in shapes]
    return call(functools.partial(finish_body, [len(parts) for parts in early]), (1,), ins, outs, name="finish")


def axis_sum(value, axis):
    return tree_sum([value] + [relative(value, axis, k) for k in range(1, lax.axis_size(axis))])


def around(value, by=1):
    size = lax.axis_size("shard")
    return lax.ppermute(value, "shard", [(i, (i + by) % size) for i in range(size)])


def neighbours(ended, sign):
    return [shifted(ended, "ctx", sign * d) for d in range(1, lax.axis_size("ctx"))]


def swap(value):
    return lax.ppermute(value, "tp", [(0, 1), (1, 0)])


def pad_rows(value):
    return jnp.pad(value, ((0, EDGE - value.shape[0]), (0, 0)))


def per_device(
    seq_in, w_zx, w_bc, w_dt, w_out, norm_gain, conv_x, conv_bc, head_params, gate_gain, segments, pad_mask, cotangent
):
    rows, model = seq_in.shape[1:]
    layers = w_zx.shape[0]
    width = w_zx.shape[3]
    heads = head_params.shape[2]
    ns = w_bc.shape[2] // 2
    shards, places = lax.axis_size("shard"), lax.axis_size("ctx")
    inner_total = width * lax.axis_size("tp")
    z, c, t = lax.axis_index("shard"), lax.axis_index("ctx"), lax.axis_index("tp")
    flag = t.astype(jnp.int32).reshape(1)
    chunks = rows // CHUNK

    ids = jnp.concatenate([jnp.full((3,), -1, jnp.int32), segments[0]])
    ext = lax.dynamic_slice_in_dim(ids, c * rows, rows + 3, 0)
    seg = ext[3:]
    mask = lax.dynamic_slice_in_dim(pad_mask[0], c * rows, rows, 0)
    firsts = ext[2 : 2 + rows].reshape(chunks, CHUNK)[:, :1]
    lasts = seg.reshape(chunks, CHUNK)[:, CHUNK - 1 :]
    by_chunk = seg.reshape(chunks, CHUNK)
    columns = [(ext[3 - lag : 3 - lag + rows] == seg) for lag in (1, 2, 3)]
    columns += [mask, (by_chunk == firsts).reshape(rows), (by_chunk == lasts).reshape(rows), mask, seg]
    cols = jnp.stack([v.astype(F32) for v in columns], axis=1)
    segs = jnp.broadcast_to(seg.astype(F32)[None], (EDGE, rows))

    head_of = jnp.arange(width)[None] // (width // heads)
    spread = (jnp.arange(2 * LANES)[:, None] % LANES == head_of).astype(BF16)
    gather = (head_of.T == jnp.arange(LANES)[None]).astype(BF16)
    at = jnp.arange(CHUNK)
    lower = (at[:, None] >= at[None]).astype(F32)
    sums = jnp.concatenate([(at[:, None] <= at[None]).astype(F32), (at[:, None] > at[None]).astype(F32)], axis=1)

    own_count = model // (shards * places)
    tie = lax.optimization_barrier
    place = c.astype(jnp.int32).reshape(1)
    crossed = jnp.concatenate([z ^ jnp.arange(shards), c ^ jnp.arange(places)]).astype(jnp.int32)

    rest_piece, x_piece, other_piece = cut_rows(0, False, place, own_count, w_zx, w_bc, w_dt, w_out)
    before = shifted(seq_in[0, rows - EDGE :], "ctx", 1)
    near, far = gather_ctx(gather_shard(x_piece)), gather_far(other_piece)
    extra = 2 * ns + LANES
    rest = gather_rows(rest_piece)
    weights = [dict(gate=(rest, width, 0), out=(rest, width, 1))]
    mains = [None]
    for layer in range(1, layers):
        rest_piece, main_piece = cut_rows(layer, True, place, own_count, w_zx, w_bc, w_dt, w_out)
        rest = gather_rows(rest_piece)
        weights.append(dict(gate=(rest, width, 0), out=(rest, width, 1)))
        mains.append(main_piece)

    params = []
    for layer in range(layers):
        gain_in = pad_rows(norm_gain[layer][None])
        taps = pad_rows(conv_x[layer])
        taps_bc = pad_rows(conv_bc[layer])
        decay = -jnp.exp(head_params[layer, 1])
        head = jnp.pad(
            jnp.stack([head_params[layer, 0], decay]), ((0, EDGE - 2), (0, LANES - heads))
        )
        skip = jnp.repeat(head_params[layer, 2], width // heads)
        rowpack = pad_rows(jnp.stack([gate_gain[layer], skip]))
        params.append((gain_in, taps, taps_bc, head, rowpack))
    ctx_order = (c ^ jnp.arange(places)).astype(jnp.int32)
    ring_order = ((z - 1 - jnp.arange(shards)) % shards).astype(jnp.int32)
    shard_order = (z ^ jnp.arange(shards)).astype(jnp.int32)
    constants = (cols, segs, spread, gather, lower, sums, flag, ctx_order, ring_order, shard_order)
    near, far, before, params, constants = tie((near, far, before, params, constants))
    cols, segs, spread, gather, lower, sums, flag, ctx_order, ring_order, shard_order = constants

    hidden = seq_in[0]
    parts = None
    kept = []
    for layer in range(layers):
        gain_in, taps, taps_bc, head, rowpack = params[layer]

        if layer > 0:
            p_tail, q_tail = parts[0][rows - EDGE :].astype(F32), parts[1][rows - EDGE :].astype(F32)
            squares = p_tail[:, model : model + 2] + q_tail[:, model : model + 2]
            scale = lax.rsqrt(jnp.sum(squares, axis=1, keepdims=True) / inner_total + EPSILON)
            tail = hidden[rows - EDGE :].astype(F32) + scale * (p_tail[:, :model] + q_tail[:, :model])
            before = shifted(tail, "ctx", 1)
        hidden, low, turned, x_raw, raw_bc, dt_raw, w_x, w_other = enter(
            crossed, shards, near, far, hidden, parts, gain_in, width, 2 * ns, inner_total
        )
        weights[layer].update(x=(w_x, width, 0), other=(w_other, extra, 0), lanes=(w_other, 0))
        more = layer + 1 < layers
        if more:
            main, dt_raw = tie((mains[layer + 1], dt_raw))
            coming = gather_shard(main)
        edge, before_turned, xc, bc, step, cum, entered, phi, ended = states(
            x_raw, raw_bc, dt_raw, before, gain_in, weights[layer], cols, taps, taps_bc, head, spread, lower
        )
        y_in = within(xc, bc, step, cum, cols, segs, spread)
        given = neighbours(ended, 1)
        if more:
            given, coming, y_in = tie((given, coming, y_in))
            near, far = gather_ctx(coming), []
        ssm, gate, p_own, state_in = leave(
            given, y_in, low, xc, bc, cum, cols, entered, phi, rowpack, spread, weights[layer]
        )
        if more:
            p_own, near = tie((p_own, near))
        parts = (p_own, swap(p_own))
        kept.append(
            dict(
                hidden=hidden, turned=turned, x_raw=x_raw, raw_bc=raw_bc, dt_raw=dt_raw, edge=edge, before_turned=before_turned, gate=gate, xc=xc, bc=bc,
                step=step, cum=cum, entered=entered, phi=phi, ended=ended, state_in=state_in, ssm=ssm, parts=parts,
                gain_in=gain_in, taps=taps, taps_bc=taps_bc, head=head, rowpack=rowpack,
            )
        )
    direct = own_count % 16 == 0

    def owned(full):
        return lax.psum_scatter(full, ("shard", "ctx"), scatter_dimension=0, tiled=True)

    def add(a, b):
        return (a.astype(F32) + b.astype(F32)).astype(BF16)

    up = cotangent[0]
    smalls, early_sums, late_above = [], [], []
    for layer in reversed(range(layers)):
        k = kept[layer]
        last_layer = layer == layers - 1
        made = back_gate(
            up, k["parts"], k["ssm"], k["xc"], k["gate"], k["bc"], k["cum"], cols, k["phi"], k["ended"],
            k["rowpack"], spread, weights[layer], inner_total, k["hidden"] if last_layer else None,
        )
        if last_layer:
            output, made = made[0], made[1:]
        do, dy, dgate, normed, gain_rows, begun = made
        early_pair = [(k["turned"], [dgate]), (do, [normed])]
        later = neighbours(begun, -1)
        quick = direct and layer == 0
        if quick:
            early = weight_grad(ring_order, shards, 1, early_pair)
            dy, early, later = tie((dy, early, later))
            moving = around(early[0])
        else:
            early = weight_grad(ctx_order, 1, 1, early_pair)[0]
            dy, early = tie((dy, early))
        dx_in, left, dbc_in = back_within(
            k["xc"], k["bc"], k["step"], k["cum"], cols, segs, spread, gather, dy, k["ssm"]
        )
        if not quick:
            dx_in, later, early = tie((dx_in, later, early))
            g_early = owned(early)
        if quick and not last_layer:
            dx_in, early_sums[0] = tie((dx_in, early_sums[0]))
            later, rest_above = tie((later, rest_above))
            rest_above = near_rows(rest_above)
        edge = k["edge"]
        dx, last, prior, dbc_mine, dbc_theirs, ddt, conv_rows, head_rows = back_inter(
            flag, later, k["x_raw"], edge, k["xc"], k["bc"], k["step"], k["cum"], cols, k["dt_raw"], dy,
            dx_in, left, dbc_in, k["entered"], k["phi"], k["state_in"], k["taps"], k["head"], k["rowpack"],
            spread, gather, sums,
        )
        if quick:
            dx, moving = tie((dx, moving))
            moving = around(add(moving, early[1]))
            if not last_layer:
                dbc_theirs, late_above[0] = tie((dbc_theirs, rest_above))
        small, last_bc, prior_bc, conv_bc_rows = back_bc(
            flag, k["raw_bc"], edge, cols, k["taps_bc"], dbc_mine, swap(dbc_theirs), ddt
        )
        back_rows = shifted(jnp.concatenate([prior, prior_bc], axis=1), "ctx", -1)
        late_pair = [(k["turned"], [dx, small])]
        ahead = (k["before_turned"], [prior, prior_bc])
        if direct:
            rest = weight_grad(ctx_order, places, shards, late_pair, ahead)
            dgate, rest, back_rows = tie((dgate, rest, back_rows))
            if quick:
                rest = near_rows(rest)
        else:
            g_rest = owned(weight_grad(ctx_order, 1, 1, late_pair, ahead)[0])
        dlow = back_low(flag, dgate, dx, small, last, last_bc, back_rows, weights[layer])
        if quick:
            dlow, moving = tie((dlow, moving))
            for one in early[2:-1]:
                moving = around(add(moving, one))
            dlow, rest = tie((dlow, rest))
        up, norm_rows = back_norm(up, dlow, swap(dlow), k["hidden"], k["gain_in"])
        packed = jnp.concatenate([conv_rows + gain_rows + norm_rows, conv_bc_rows, head_rows], axis=1)
        smalls.insert(0, packed)
        if not direct:
            early_sums.insert(0, [g_early])
            late_above.insert(0, g_rest)
        elif not quick:
            rest_above = rest
            early_sums.insert(0, [g_early])
            late_above.insert(0, None)
        else:
            late_sum = scattered(split_sum(shard_order, shards, [rest] + late_above), "shard")
            partial = axis_sum(jnp.concatenate(smalls), "ctx")
            partial, moving = tie((partial, moving))
            early_sums.insert(0, scattered(split_sum(ctx_order, places, [[moving, early[-1]]]), "ctx"))
            partial, late_sum, early_sums[0] = tie((partial, late_sum, early_sums[0]))
    if not direct:
        late_sum = [jnp.concatenate(late_above, axis=1)]
        partial = axis_sum(jnp.concatenate(smalls), "ctx")
    packed = axis_sum(partial, "shard").reshape(layers, EDGE, -1)
    grad_zx, grad_out, grad_small = finish(early_sums, late_sum, width)
    packed, grad_small = tie((packed, grad_small))
    small_mine = grad_small[:, :, :ns]
    cb_mine = packed[:, :5, width : width + ns]
    cb_other, small_other = swap(cb_mine), swap(small_mine)

    def ordered(own, other):
        first = jnp.where(t == 0, own, other)
        return jnp.concatenate([first, jnp.where(t == 0, other, own)], axis=-1)

    skip_sum = jnp.sum(packed[:, 5, :width].reshape(layers, heads, width // heads), axis=-1)
    head_sums = packed[:, :2, width + ns : width + ns + heads]
    return (
        output[None],
        up[None],
        grad_zx,
        ordered(small_mine, small_other),
        grad_small[:, :, ns : ns + heads],
        jnp.swapaxes(grad_out, 1, 2),
        packed[:, 7, :width],
        packed[:, :5, :width],
        ordered(cb_mine, cb_other),
        jnp.concatenate([head_sums, skip_sum[:, None]], axis=1),
        packed[:, 6, :width],
    )


def solution(mesh):
    in_specs = (
        P("shard", "ctx", None),
        P(None, "shard", None, "tp"),
        P(None, "shard", None),
        P(None, "shard", "tp"),
        P(None, "tp", "shard"),
        P(),
        P(None, None, "tp"),
        P(),
        P(None, None, "tp"),
        P(None, "tp"),
        P("shard", None),
        P("shard", None),
        P("shard", "ctx", None),
    )
    out_specs = (
        P("shard", "ctx", None),
        P("shard", "ctx", None),
        P(None, ("shard", "ctx"), None, "tp"),
        P(None, ("shard", "ctx"), None),
        P(None, ("shard", "ctx"), "tp"),
        P(None, "tp", ("shard", "ctx")),
        P(),
        P(None, None, "tp"),
        P(),
        P(None, None, "tp"),
        P(None, "tp"),
    )
    return jax.shard_map(per_device, mesh=mesh, in_specs=in_specs, out_specs=out_specs, check_vma=False)
```
